128 devices in a mesh: ma: 32 (over y, z, core), sa: 4 (over x).
Axes of the slice: x: 4, y: 4, z: 4, core: 2. Of those that a mesh axis runs over, the one named last changes fastest.
Arguments:
- initial_heat_matrix: float32 [128, 128, 8192], P('ma', 'sa'), may hold values from -6 to 6
- conductivity: float32 [128, 8192], P('sa'), may hold values from 0.5 to 2
- laser_x: int32 [128, 2], P('ma'), may hold values from 0 to 127
- laser_y: int32 [128, 2], P('ma'), may hold values from 0 to 127
- pixel_cell: int32 [128, 512], P('sa', 'ma'), may hold values from 0 to 127, as said below
- observed: float32 [128, 512], P('sa', 'ma'), may hold values from -6 to 6
- obs_var: float32 [128, 512], P('sa', 'ma'), may hold values from 20 to 400
Outputs:
- analysis: float32 [128, 128, 8192], P('ma', 'sa')
The draws below stay inside these ranges and needn't reach their ends.
Inputs may be any that keep to these rules, and one draw needn't show every extreme that they name: `pixel_cell`: pixel column j views a surface cell y of its own plane; y lies within 2 of j // 4 and in the same aligned group of 4 cells as that value.
All inputs are finite; a program needn't handle non-finite values.
Results may differ from the reference program's by a relative error of at most 0.000096.
Values sent between devices are 32-bit elements; how exact they have to be, the bound alone decides.
No kernel may reach another device: no remote copies, remote signals or barrier semaphores. Data moves between devices by JAX's collectives and lax.ppermute only.
A program may use at most 192 MiB of HBM per device.

```python
import math
import jax
import jax.numpy as jnp
from jax import lax

ENSEMBLE_SIZE = 128
CELLS_FIRST_AXIS = 128
CELLS_SECOND_AXIS = 128
CELLS_DEPTHWISE = 64
PIX_ROW = 512
STEPS = 2
YB = 4


def draw_pixel_cell(key, part):
    per_cell = PIX_ROW // CELLS_SECOND_AXIS
    columns = jnp.arange(PIX_ROW, dtype=jnp.int32)
    centre = columns // per_cell
    base = centre // YB * YB
    jitter = jax.random.randint(key, (CELLS_FIRST_AXIS, PIX_ROW), -2, 3, dtype=jnp.int32)
    return base[None, :] + jnp.clip(centre[None, :] - base[None, :] + jitter, 0, YB - 1)


def touch_ends(drawn, rng, low, largest):
    spot = [jax.random.randint(jax.random.fold_in(rng, axis), (), 0, length) for axis, length in enumerate(drawn.shape)]
    longest = drawn.shape.index(max(drawn.shape))
    next_to = spot[:longest] + [(spot[longest] + 1) % drawn.shape[longest]] + spot[longest + 1:]
    return drawn.at[tuple(spot)].set(low).at[tuple(next_to)].set(largest)


def block_scale(rng, extent, cuts, low, high):
    def one(axis_at, blocks):
        steps = jax.random.uniform(jax.random.fold_in(jax.random.fold_in(rng, 6), axis_at), (blocks,), jnp.float32, low / len(cuts), high / len(cuts))
        return jnp.repeat(jnp.exp(steps), extent[axis_at] // blocks).reshape((-1,) + (1,) * (len(extent) - axis_at - 1))

    factor_of = one(*cuts[0])
    for cut in cuts[1:]:
        factor_of = factor_of * one(*cut)
    return factor_of


def bell_draw(stream_key, dims, spread, most, split=(), kind=jnp.bfloat16):
    result = spread * jax.random.normal(stream_key, dims, jnp.float32)
    if split:
        result = result * block_scale(stream_key, dims, split, -0.22, 0.18)
    return jnp.clip(result, -most, most).astype(kind)


def setup_inputs(seed: int = 0) -> dict:
    keys = jax.random.split(jax.random.key(seed), 8)
    return {
        "initial_heat_matrix": bell_draw(keys[0], (ENSEMBLE_SIZE, CELLS_FIRST_AXIS, CELLS_SECOND_AXIS * CELLS_DEPTHWISE), 1.0, 6.0, ((0, 32), (1, 4)), jnp.float32),
        "conductivity": jnp.clip(jnp.exp(math.log(2.0) - 1.3862944 * jax.random.uniform(keys[1], (CELLS_FIRST_AXIS, CELLS_SECOND_AXIS * CELLS_DEPTHWISE), jnp.float32) ** block_scale(keys[1], (CELLS_FIRST_AXIS, CELLS_SECOND_AXIS * CELLS_DEPTHWISE), ((0, 4),), -0.2, 0.2)), 0.5, 2.0),
        "laser_x": touch_ends(jax.random.randint(keys[2], (ENSEMBLE_SIZE, STEPS), 0, CELLS_FIRST_AXIS), jax.random.fold_in(keys[2], 1), 0, CELLS_FIRST_AXIS - 1).astype(jnp.int32),
        "laser_y": touch_ends(jax.random.randint(keys[3], (ENSEMBLE_SIZE, STEPS), 0, CELLS_SECOND_AXIS), jax.random.fold_in(keys[3], 1), 0, CELLS_SECOND_AXIS - 1).astype(jnp.int32),
        "pixel_cell": draw_pixel_cell(jax.random.fold_in(keys[7], 71), 0),
        "observed": bell_draw(keys[5], (CELLS_FIRST_AXIS, PIX_ROW), 1.0, 6.0, ((0, 4), (1, 32)), jnp.float32),
        "obs_var": jnp.clip(jnp.exp(math.log(400.0) - 2.9957323 * jax.random.uniform(keys[6], (CELLS_FIRST_AXIS, PIX_ROW), jnp.float32) ** block_scale(keys[6], (CELLS_FIRST_AXIS, PIX_ROW), ((0, 4), (1, 32)), -0.2, 0.2)), 20.0, 400.0),
    }


step_dt = 0.025
alpha_cond = 0.05
laser_power = 12.0
beam_spot_width = 18.0

def conduct(field_ext, cond_ext, first_plane, spot_x, spot_y):
    kext = cond_ext[None] * (1.0 + alpha_cond * field_ext * field_ext)
    fpad = jnp.pad(field_ext, ((0, 0), (0, 0), (1, 1), (1, 1)))
    kpad = jnp.pad(kext, ((0, 0), (0, 0), (1, 1), (1, 1)))
    centre = fpad[:, 1:-1, 1:-1, 1:-1]
    kcentre = kpad[:, 1:-1, 1:-1, 1:-1]
    shifted = [(slice(2, None), slice(1, -1), slice(1, -1)), (slice(None, -2), slice(1, -1), slice(1, -1)), (slice(1, -1), slice(2, None), slice(1, -1)), (slice(1, -1), slice(None, -2), slice(1, -1)), (slice(1, -1), slice(1, -1), slice(2, None)), (slice(1, -1), slice(1, -1), slice(None, -2))]
    flux = jnp.zeros_like(centre)
    for pick in shifted:
        neighbour = fpad[(slice(None),) + pick]
        kneigh = kpad[(slice(None),) + pick]
        flux = flux + 0.5 * (kcentre + kneigh) * (neighbour - centre)
    width = centre.shape[1]
    rows_y = centre.shape[2]
    depth = centre.shape[3]
    xglob = first_plane + jnp.arange(width, dtype=jnp.int32)
    yglob = jnp.arange(rows_y, dtype=jnp.int32)
    delta_x = (xglob[None, :] - spot_x[:, None]).astype(centre.dtype)
    delta_y = (yglob[None, :] - spot_y[:, None]).astype(centre.dtype)
    spot = laser_power * jnp.exp(-(delta_x[:, :, None] ** 2 + delta_y[:, None, :] ** 2) / beam_spot_width)
    surface_top = (jnp.arange(depth, dtype=jnp.int32) == depth - 1).astype(centre.dtype)
    heat = spot[:, :, :, None] * surface_top[None, None, None, :]
    return centre + step_dt * (flux + heat)

def reference(initial_heat_matrix, conductivity, laser_x, laser_y, pixel_cell, observed, obs_var):
    realization_batch = math.gcd(ENSEMBLE_SIZE, 8)
    thermal_profiles = initial_heat_matrix.reshape(ENSEMBLE_SIZE // realization_batch, realization_batch, CELLS_FIRST_AXIS, CELLS_SECOND_AXIS, CELLS_DEPTHWISE)
    cond_grid = conductivity.reshape(CELLS_FIRST_AXIS, CELLS_SECOND_AXIS, CELLS_DEPTHWISE)
    cond_ext = jnp.pad(cond_grid, ((1, 1), (0, 0), (0, 0)))
    heating_centres_first = laser_x.reshape(ENSEMBLE_SIZE // realization_batch, realization_batch, STEPS)
    heating_centres_second = laser_y.reshape(ENSEMBLE_SIZE // realization_batch, realization_batch, STEPS)

    def predicted_ensemble(flattened_ensemble):
        field, sx, sy = flattened_ensemble
        for tstep in range(STEPS):
            ext = jnp.pad(field, ((0, 0), (1, 1), (0, 0), (0, 0)))
            field = conduct(ext, cond_ext, jnp.int32(0), sx[:, tstep], sy[:, tstep])
        return field
    assimilated_outcome = lax.map(predicted_ensemble, (thermal_profiles, heating_centres_first, heating_centres_second))
    assimilated_outcome = assimilated_outcome.reshape(ENSEMBLE_SIZE, CELLS_FIRST_AXIS, CELLS_SECOND_AXIS, CELLS_DEPTHWISE)
    surface = assimilated_outcome[:, :, :, CELLS_DEPTHWISE - 1]
    index = jnp.broadcast_to(pixel_cell[None], (ENSEMBLE_SIZE, CELLS_FIRST_AXIS, PIX_ROW)).astype(jnp.int32)
    seen = jnp.take_along_axis(surface, index, axis=2)
    seen_mean = jnp.mean(seen, axis=0)
    seen_anom = seen - seen_mean[None]
    innovation = observed - seen_mean
    weight = 1.0 / obs_var
    gram = jnp.einsum('kxj,lxj->kl', seen_anom * weight[None], seen_anom, precision=lax.Precision.HIGHEST)
    proj = jnp.einsum('kxj,xj->k', seen_anom, weight * innovation, precision=lax.Precision.HIGHEST)
    eye = jnp.eye(ENSEMBLE_SIZE, dtype=gram.dtype)
    amat = eye + gram / (ENSEMBLE_SIZE - 1)
    chol = jnp.linalg.cholesky(amat)
    wroot = jax.scipy.linalg.solve_triangular(chol.T, eye, lower=False)
    middle = jax.scipy.linalg.solve_triangular(chol, proj[:, None], lower=True)
    wmean = jax.scipy.linalg.solve_triangular(chol.T, middle, lower=False)[:, 0] / (ENSEMBLE_SIZE - 1)
    mix = wroot + wmean[:, None]
    flat = assimilated_outcome.reshape(ENSEMBLE_SIZE, CELLS_FIRST_AXIS, CELLS_SECOND_AXIS * CELLS_DEPTHWISE)

    def transform(plane):
        fmean = jnp.mean(plane, axis=0)
        anom = plane - fmean[None]
        return fmean[None] + jnp.dot(mix.T, anom, precision=lax.Precision.HIGHEST)
    planes = lax.map(transform, jnp.transpose(flat, (1, 0, 2)))
    return jnp.transpose(planes, (1, 0, 2))
```

```python
import functools

import jax
import jax.numpy as jnp
from jax import lax
from jax.experimental import pallas as pl
from jax.experimental.pallas import tpu as pltpu
from jax.sharding import Mesh
from jax.sharding import PartitionSpec as P

DEPTH = 64
STEPS = 2
LANES = 128
MA = ("ma_0", "ma_1", "ma_2")
MA_SA = ("ma_0", "ma_1", "ma_2", "sa")

step_dt = 0.025
alpha_cond = 0.05
laser_power = 12.0
beam_spot_width = 18.0

HALO_TILE = 8


def _roll(x, shift, axis):
    return pltpu.roll(x, shift, axis)


def _stencil_step(src, cond, row_first, tiles, edges, exs, ey_at, emit, extra):
    lane = lax.broadcasted_iota(jnp.int32, (8, LANES), 1)
    sub = lax.broadcasted_iota(jnp.int32, (8, LANES), 0)
    low_half = lane < DEPTH
    zpos = lane & (DEPTH - 1)
    z_last = zpos == DEPTH - 1
    z_first = zpos == 0
    sub_last = sub == 7
    sub_first = sub == 0
    pairs = (src.shape[1] - LANES) // (2 * LANES)

    def load(row, v):
        cols = pl.ds(pl.multiple_of(v * LANES, LANES), LANES)
        u = src[pl.ds(row, 8), cols]
        k = cond[pl.ds(row, 8), cols]
        return u, k * (1.0 + alpha_cond * (u * u))

    rows = [row_first + 8 * i for i in range(tiles)]
    first = [load(r, 0) for r in rows]
    us = [a for a, _ in first]
    ks = [b for _, b in first]
    rus = [_roll(a, DEPTH, 1) for a in us]
    rks = [_roll(b, DEPTH, 1) for b in ks]
    rfs = [a * b for a, b in first]

    def one(v, half, d, carry):
        us, ks, rus, rks, rfs, ext = carry
        nxt = [load(r, v + 1) for r in rows]
        run = [_roll(a, DEPTH, 1) for a, _ in nxt]
        rkn = [_roll(b, DEPTH, 1) for _, b in nxt]
        if edges:
            ul, kl = load(row_first - 8, v)
            uh, kh = load(row_first + 8 * tiles, v)
            ux, kx = [ul] + us + [uh], [kl] + ks + [kh]
        else:
            ux, kx = us, ks
        rot_u = [_roll(a, 7, 0) for a in ux]
        rot_k = [_roll(a, 7, 0) for a in kx]
        fx, rfx = [], []
        count = len(ux)
        for i in range(count - 1 if edges else count):
            j = min(i + 1, count - 1)
            xp = jnp.where(sub_last, rot_u[j], rot_u[i])
            kp = jnp.where(sub_last, rot_k[j], rot_k[i])
            face = (kx[i] + kp) * (xp - ux[i])
            fx.append(face)
            rfx.append(_roll(face, 1, 0))
        shift = 1 if edges else 0
        new_rfs = []
        ey = ey_at(v)
        for i in range(tiles):
            u, k = us[i], ks[i]
            yp = jnp.where(low_half, rus[i], run[i])
            kyp = jnp.where(low_half, rks[i], rkn[i])
            fy = (k + kyp) * (yp - u)
            rfy = _roll(fy, DEPTH, 1)
            new_rfs.append(rfy)
            acc = fy - jnp.where(low_half, rfs[i], rfy)
            zp = jnp.where(z_last, 0.0, _roll(u, LANES - 1, 1))
            kzp = jnp.where(z_last, 0.0, _roll(k, LANES - 1, 1))
            fz = (k + kzp) * (zp - u)
            acc = acc + (fz - jnp.where(z_first, k * u, _roll(fz, 1, 1)))
            below = rfx[max(i + shift - 1, 0)]
            acc = acc + (fx[i + shift] - jnp.where(sub_first, below, rfx[i + shift]))
            new = u + (0.5 * step_dt) * acc + exs[i] * ey
            ext = emit(d, v, half, i, new, ext)
        return [a for a, _ in nxt], [b for _, b in nxt], run, rkn, new_rfs, ext

    def pair(d, carry):
        carry = one(2 * d, 0, d, carry)
        return one(2 * d + 1, 1, d, carry)

    carry = lax.fori_loop(0, pairs, pair, (us, ks, rus, rks, rfs, extra))
    return carry[-1]


def _forecast_body(
    planes, u_ref, c_ref, lo_ref, hi_ref, clo_ref, chi_ref, ex_ref, ey_ref, pc_ref, obs_ref, var_ref,
    out_ref, surf_ref, e_ref, ce_ref, u1_ref,
):
    m = pl.program_id(0)
    columns = u_ref.shape[2]
    main = pl.ds(HALO_TILE, planes)
    low = pl.ds(HALO_TILE - 2, 2)
    high = pl.ds(HALO_TILE + planes, 2)
    body = pl.ds(0, columns)
    lane = lax.broadcasted_iota(jnp.int32, (8, LANES), 1)
    insert = (lane & (DEPTH - 1)) == DEPTH - 1
    tiles = planes // 8

    @pl.when(m == 0)
    def _():
        for ref in (e_ref, ce_ref, u1_ref):
            ref[pl.ds(0, HALO_TILE), :] = jnp.zeros((HALO_TILE, ref.shape[1]), jnp.float32)
            ref[pl.ds(HALO_TILE + planes, HALO_TILE), :] = jnp.zeros((HALO_TILE, ref.shape[1]), jnp.float32)
            ref[main, pl.ds(columns, LANES)] = jnp.zeros((planes, LANES), jnp.float32)
        ce_ref[main, body] = c_ref[...]
        ce_ref[low, body] = clo_ref[0]
        ce_ref[high, body] = chi_ref[0]
        wide = lax.broadcasted_iota(jnp.int32, (planes, LANES), 1)
        cell = jnp.where(wide < DEPTH, 2 * wide, 2 * wide - (LANES - 1))
        weight = 1.0 / var_ref[...]
        value = weight * obs_ref[...]
        pc = pc_ref[...]
        wsum = jnp.zeros((planes, LANES), jnp.float32)
        rsum = jnp.zeros((planes, LANES), jnp.float32)
        for j in range(pc.shape[1]):
            hit = pc[:, j : j + 1] == cell
            wsum = wsum + jnp.where(hit, weight[:, j : j + 1], 0.0)
            rsum = rsum + jnp.where(hit, value[:, j : j + 1], 0.0)
        surf_ref[:, 4, :] = wsum
        surf_ref[:, 5, :] = rsum
        surf_ref[:, 6, :] = jnp.zeros((planes, LANES), jnp.float32)
        surf_ref[:, 7, :] = jnp.zeros((planes, LANES), jnp.float32)

    e_ref[main, body] = u_ref[0]
    e_ref[low, body] = lo_ref[0]
    e_ref[high, body] = hi_ref[0]

    def ey_row(t):
        def at(v):
            cols = pl.ds(pl.multiple_of(v * LANES, LANES), LANES)
            return ey_ref[0, pl.ds(t, 1), cols]

        return at

    def emit1(d, v, half, i, new, ext):
        cols = pl.ds(pl.multiple_of(v * LANES, LANES), LANES)
        rows = pl.ds(8 * i, 8)
        if i == 0 or i == tiles + 1:
            new = jnp.where(ce_ref[rows, cols] > 0.0, new, 0.0)
        u1_ref[rows, cols] = new
        return ext

    ex1 = [ex_ref[0, 0, pl.ds(8 * i, 8), :] for i in range(tiles + 2)]
    _stencil_step(e_ref, ce_ref, 0, tiles + 2, False, ex1, ey_row(0), emit1, ())

    def emit2(d, v, half, i, new, ext):
        out_ref[d, 0, pl.ds(8 * i, 8), pl.ds(half * LANES, LANES)] = new
        ext = list(ext)
        ext[i] = jnp.where(insert, new, _roll(ext[i], LANES - 1, 1))
        return tuple(ext)

    ex2 = [ex_ref[0, 1, pl.ds(8 * (i + 1), 8), :] for i in range(tiles)]
    start = tuple(jnp.zeros((8, LANES), jnp.float32) for _ in range(tiles))
    surface = _stencil_step(u1_ref, ce_ref, HALO_TILE, tiles, True, ex2, ey_row(1), emit2, start)
    for k in range(4):

        @pl.when(m == k)
        def _():
            for i in range(tiles):
                surf_ref[pl.ds(8 * i, 8), k, :] = surface[i]


def forecast(u, cond, low, high, ex, ey, pixel_cell, observed, obs_var, blocks):
    members, planes, columns = u.shape
    per = columns // blocks
    ext = planes + 2 * HALO_TILE
    whole = lambda shape: pl.BlockSpec(shape, lambda m: (0,) * len(shape))
    scratch = pltpu.VMEM((ext, columns + LANES), jnp.float32)
    pix = pixel_cell.shape
    return pl.pallas_call(
        functools.partial(_forecast_body, planes),
        grid=(members,),
        in_specs=[
            pl.BlockSpec((1, planes, columns), lambda m: (m, 0, 0)),
            whole((planes, columns)),
            pl.BlockSpec((1, 2, columns), lambda m: (m, 0, 0)),
            pl.BlockSpec((1, 2, columns), lambda m: (m, 0, 0)),
            pl.BlockSpec((1, 2, columns), lambda m: (members, 0, 0)),
            pl.BlockSpec((1, 2, columns), lambda m: (members, 0, 0)),
            pl.BlockSpec((1, STEPS, ext, LANES), lambda m: (m, 0, 0, 0)),
            pl.BlockSpec((1, STEPS, columns), lambda m: (m, 0, 0)),
            whole(pix),
            whole(pix),
            whole(pix),
        ],
        out_specs=[
            pl.BlockSpec((blocks, 1, planes, per), lambda m: (0, m, 0, 0)),
            whole((planes, 8, LANES)),
        ],
        out_shape=[
            jax.ShapeDtypeStruct((blocks, members, planes, per), jnp.float32),
            jax.ShapeDtypeStruct((planes, 8, LANES), jnp.float32),
        ],
        scratch_shapes=[scratch, scratch, scratch],
        compiler_params=pltpu.CompilerParams(
            dimension_semantics=("arbitrary",), vmem_limit_bytes=32 << 20
        ),
        cost_estimate=pl.CostEstimate(flops=200_000_000, bytes_accessed=10_000_000, transcendentals=0),
        name="forecast",
    )(u, cond, low, high, low, high, ex, ey, pixel_cell, observed, obs_var)


def _nt(a, b):
    return lax.dot_general(
        a, b, (((1,), (1,)), ((), ())), precision=lax.Precision.HIGHEST, preferred_element_type=jnp.float32
    )


def _member_rows(ref, full_ref, groups):
    for k in range(4):
        full_ref[pl.ds(k, groups, stride=4), :] = ref[pl.ds(k, groups, stride=8), :]


def _gram_body(recv_ref, out_ref, s_ref):
    groups = recv_ref.shape[0] // 8
    count = groups * 4
    _member_rows(recv_ref, s_ref, groups)
    wsum = jnp.sum(recv_ref[pl.ds(4, groups, stride=8), :], axis=0, keepdims=True)
    rsum = jnp.sum(recv_ref[pl.ds(5, groups, stride=8), :], axis=0, keepdims=True)
    s = s_ref[...]
    mean = jnp.sum(s, axis=0, keepdims=True) * (1.0 / count)
    anom = s - mean
    gram = _nt(anom * wsum, anom)
    q = rsum - wsum * mean
    proj = _nt(jnp.broadcast_to(q, (8, LANES)), anom)
    s_ref[...] = gram
    for k in range(4):
        out_ref[pl.ds(k, groups, stride=8), :] = s_ref[pl.ds(k, groups, stride=4), :]
    for k in range(4, 8):
        out_ref[pl.ds(k, groups, stride=8), :] = jnp.broadcast_to(proj[0:1], (groups, LANES))


def gram_message(recv):
    rows = recv.shape[0]
    return pl.pallas_call(
        _gram_body,
        out_shape=jax.ShapeDtypeStruct((rows, LANES), jnp.float32),
        scratch_shapes=[pltpu.VMEM((rows // 2, LANES), jnp.float32)],
        cost_estimate=pl.CostEstimate(flops=40_000_000, bytes_accessed=300_000, transcendentals=0),
        name="gram",
    )(recv)


def _total_body(recv_ref, out_ref):
    total = recv_ref[0]
    for i in range(1, recv_ref.shape[0]):
        total = total + recv_ref[i]
    for i in range(out_ref.shape[0]):
        out_ref[i] = total


def total_message(recv, copies):
    return pl.pallas_call(
        _total_body,
        out_shape=jax.ShapeDtypeStruct((copies,) + recv.shape[1:], jnp.float32),
        cost_estimate=pl.CostEstimate(flops=100_000, bytes_accessed=700_000, transcendentals=0),
        name="total",
    )(recv)


GROUP = 4


def _mix_body(recv_ref, hi_ref, lo_ref, a_ref, rows_ref):
    groups, slabs = recv_ref.shape[0], recv_ref.shape[1]
    count = 4 * groups
    for g in range(groups):
        total = recv_ref[g, 0]
        for s in range(1, slabs):
            total = total + recv_ref[g, s]
        rows_ref[pl.ds(8 * g, 8), :] = total
    _member_rows(rows_ref, a_ref, groups)
    proj = rows_ref[pl.ds(4, 1), :]
    ntile = count // 8
    sub = lax.broadcasted_iota(jnp.int32, (8, LANES), 0)
    lane = lax.broadcasted_iota(jnp.int32, (8, LANES), 1)
    a, inv, diag = [], [], []
    for i in range(ntile):
        eye = (lane == sub + 8 * i).astype(jnp.float32)
        a.append(eye + a_ref[pl.ds(8 * i, 8), :] * (1.0 / (count - 1)))
        inv.append(eye)
        diag.append(jnp.ones((8, LANES), jnp.float32))

    def row_of(tile, r):
        return jnp.broadcast_to(tile[r : r + 1, :], (8, LANES))

    for j0 in range(0, count, GROUP):
        base = j0 // 8
        cols = [
            {i: jnp.broadcast_to(a[i][:, j0 + t : j0 + t + 1], (8, LANES)) for i in range(base, ntile)}
            for t in range(GROUP)
        ]
        r0 = j0 % 8
        arow = [row_of(a[base], r0 + t) for t in range(GROUP)]
        irow = [row_of(inv[base], r0 + t) for t in range(GROUP)]
        for t in range(GROUP):
            pivot = row_of(cols[t][base], r0 + t)
            recip = 1.0 / pivot
            diag[base] = jnp.where(sub == r0 + t, pivot, diag[base])
            for s in range(t + 1, GROUP):
                factor = row_of(cols[t][base], r0 + s) * recip
                for i in range(base, ntile):
                    cols[s][i] = cols[s][i] - factor * cols[t][i]
                arow[s] = arow[s] - factor * arow[t]
                irow[s] = irow[s] - factor * irow[t]
            arow[t] = arow[t] * recip
            irow[t] = irow[t] * recip
            cols[t][base] = jnp.where(sub > r0 + t, cols[t][base], 0.0)
        for i in range(base, ntile):
            for t in range(GROUP):
                a[i] = a[i] - cols[t][i] * arow[t]
                inv[i] = inv[i] - cols[t][i] * irow[t]
    for i in range(ntile):
        a_ref[pl.ds(8 * i, 8), :] = inv[i] / jnp.sqrt(diag[i])
    linv = a_ref[...]
    middle = _nt(jnp.broadcast_to(proj, (8, LANES)), linv)
    wmean = lax.dot_general(
        middle, linv, (((1,), (0,)), ((), ())), precision=lax.Precision.HIGHEST, preferred_element_type=jnp.float32
    ) * (1.0 / (count - 1))
    mix = linv + wmean[0:1]
    mix = mix + (1.0 - jnp.sum(mix, axis=1, keepdims=True)) * (1.0 / count)
    hi = mix.astype(jnp.bfloat16)
    hi_ref[...] = hi
    lo_ref[...] = (mix - hi.astype(jnp.float32)).astype(jnp.bfloat16)


def mix_matrices(recv):
    groups = recv.shape[0]
    count = 4 * groups
    shape = jax.ShapeDtypeStruct((count, count), jnp.bfloat16)
    return pl.pallas_call(
        _mix_body,
        out_shape=[shape, shape],
        scratch_shapes=[
            pltpu.VMEM((count, LANES), jnp.float32),
            pltpu.VMEM((2 * count, LANES), jnp.float32),
        ],
        cost_estimate=pl.CostEstimate(flops=200_000_000, bytes_accessed=600_000, transcendentals=0),
        name="mix",
    )(recv)


def _transform_body(f_ref, hi_ref, lo_ref, out_ref):
    count = hi_ref.shape[0]
    hi = hi_ref[...]
    lo = lo_ref[...]
    src = f_ref.reshape(count * 8, LANES)
    dst = out_ref.reshape(count * 8, LANES)
    for x in range(8):
        rows = pl.ds(x, count, stride=8)
        f = src[rows, :]
        fhi = f.astype(jnp.bfloat16)
        flo = (f - fhi.astype(jnp.float32)).astype(jnp.bfloat16)
        out = jnp.dot(hi, fhi, preferred_element_type=jnp.float32)
        out = out + jnp.dot(hi, flo, preferred_element_type=jnp.float32)
        out = out + jnp.dot(lo, fhi, preferred_element_type=jnp.float32)
        dst[rows, :] = out


def transform(block, hi, lo):
    count, planes, per = block.shape
    spec = pl.BlockSpec((count, 8, LANES), lambda x, c: (0, x, c))
    mat = pl.BlockSpec((count, count), lambda x, c: (0, 0))
    return pl.pallas_call(
        _transform_body,
        grid=(planes // 8, per // LANES),
        in_specs=[spec, mat, mat],
        out_specs=spec,
        out_shape=jax.ShapeDtypeStruct(block.shape, jnp.float32),
        compiler_params=pltpu.CompilerParams(
            dimension_semantics=("arbitrary", "arbitrary"), vmem_limit_bytes=32 << 20
        ),
        cost_estimate=pl.CostEstimate(flops=900_000_000, bytes_accessed=8_500_000, transcendentals=0),
        name="transform",
    )(block, hi, lo)


def heat_factors(laser_x, laser_y, first, planes, columns):
    xs = first - HALO_TILE + jnp.arange(planes + 2 * HALO_TILE, dtype=jnp.int32)
    dx = (xs[None, None, :] - laser_x[:, :, None]).astype(jnp.float32)
    ex = (step_dt * laser_power) * jnp.exp(-(dx * dx) / beam_spot_width)
    ex = jnp.broadcast_to(ex[..., None], ex.shape + (LANES,))
    col = jnp.arange(columns, dtype=jnp.int32)
    dy = (col // DEPTH - laser_y[:, :, None]).astype(jnp.float32)
    ey = jnp.where(col % DEPTH == DEPTH - 1, jnp.exp(-(dy * dy) / beam_spot_width), 0.0)
    return ex, ey


def per_device(initial_heat_matrix, conductivity, laser_x, laser_y, pixel_cell, observed, obs_var):
    members, planes, columns = initial_heat_matrix.shape
    blocks = 1
    for axis in MA:
        blocks *= lax.axis_size(axis)
    slabs = lax.axis_size("sa")
    first = lax.axis_index("sa") * planes
    u = initial_heat_matrix
    forward = [(i, i + 1) for i in range(slabs - 1)]
    backward = [(b, a) for a, b in forward]
    top = jnp.concatenate([u[:, planes - 2 :], conductivity[None, planes - 2 :]], axis=0)
    bottom = jnp.concatenate([u[:, :2], conductivity[None, :2]], axis=0)
    low = lax.ppermute(top, "sa", forward)
    high = lax.ppermute(bottom, "sa", backward)
    ex, ey = heat_factors(laser_x, laser_y, first, planes, columns)
    sent, surf = forecast(u, conductivity, low, high, ex, ey, pixel_cell, observed, obs_var, blocks)

    seen = lax.all_to_all(surf, MA, 0, 0, tiled=True)
    rows = gram_message(seen.reshape(blocks * 8, LANES))
    mine = lax.all_to_all(rows.reshape(blocks, 8, LANES), MA, 0, 0, tiled=True)
    copies = total_message(mine, blocks * slabs)
    every = lax.all_to_all(copies, MA_SA, 0, 0, tiled=True)
    hi, lo = mix_matrices(every.reshape(blocks, slabs, 8, LANES))

    held = lax.all_to_all(sent, MA, 0, 0, tiled=True)
    done = transform(held.reshape(blocks * members, planes, columns // blocks), hi, lo)
    back = lax.all_to_all(done.reshape(held.shape), MA, 0, 0, tiled=True)
    return back.transpose(1, 2, 0, 3).reshape(members, planes, columns)


def solution(mesh):
    torus = Mesh(mesh.devices.reshape(4, 4, 2, mesh.shape["sa"]), ("ma_0", "ma_1", "ma_2", "sa"))
    in_specs = (
        P(MA, "sa", None),
        P("sa", None),
        P(MA, None),
        P(MA, None),
        P("sa", MA),
        P("sa", MA),
        P("sa", MA),
    )
    out_specs = P(MA, "sa", None)
    return jax.shard_map(
        per_device, mesh=torus, in_specs=in_specs, out_specs=out_specs, check_vma=False
    )
```

```python
import functools

import jax
import jax.numpy as jnp
from jax import lax
from jax.experimental import pallas as pl
from jax.experimental.pallas import tpu as pltpu
from jax.sharding import Mesh
from jax.sharding import PartitionSpec as P

DEPTH = 64
STEPS = 2
LANES = 128
MA = ("ma_0", "ma_1", "ma_2")
MA_SA = ("ma_0", "ma_1", "ma_2", "sa")

step_dt = 0.025
alpha_cond = 0.05
laser_power = 12.0
beam_spot_width = 18.0

def _roll(x, shift, axis):
    return pltpu.roll(x, shift, axis)


def _wide_pair(a, b, low_half):
    return jnp.where(low_half, a, _roll(b, DEPTH, 1)), jnp.where(low_half, _roll(a, DEPTH, 1), b)


ROWS = 48
FIRST_ROW = 8
UNROLL = 4
FILL_UNROLL = 8
CHUNK = 5


def _stencil_step(src, cond, base, tiles, exs, ey_at, emit, extra):
    lane = lax.broadcasted_iota(jnp.int32, (8, LANES), 1)
    low_half = lane < DEPTH
    zpos = lane & (DEPTH - 1)
    z_last = zpos == DEPTH - 1
    z_first = zpos == 0

    def load(y, i):
        at = pl.ds(y * ROWS + (base + i), 8, stride=tiles)
        u = src[at, :]
        c = cond[at, :]
        return u, c + c * (alpha_cond * (u * u))

    def face(one, two):
        return (one[1] + two[1]) * (two[0] - one[0])

    results = []
    for i0 in range(0, tiles, CHUNK):
        some = range(i0, min(i0 + CHUNK, tiles))
        here, fys = [], []
        for i in some:
            u, k = load(DEPTH - 1, i)
            before = (
                jnp.where(low_half, 0.0, _roll(u, DEPTH, 1)),
                jnp.where(low_half, 0.0, _roll(k, DEPTH, 1)),
            )
            here.append(load(0, i))
            fys.append(face(before, here[-1]))

        def one(y, carry, some=some):
            here, fys, ext = carry
            after = [load(y + 1, i) for i in some]
            line = [load(y, some[0] - 1)] + list(here) + [load(y, some[-1] + 1)]
            ey = jnp.broadcast_to(ey_at(y), (8, LANES))
            fx = face(line[0], line[1])
            new_fys, values = [], []
            for j, i in enumerate(some):
                u, k = here[j]
                fy = face(here[j], after[j])
                new_fys.append(fy)
                fx_next = face(line[j + 1], line[j + 2])
                acc = (fy - fys[j]) + (fx_next - fx)
                fx = fx_next
                up = jnp.where(z_last, 0.0, _roll(u, LANES - 1, 1))
                kp = jnp.where(z_last, 0.0, _roll(k, LANES - 1, 1))
                fz = (k + kp) * (up - u)
                acc = acc + (fz - jnp.where(z_first, k * u, _roll(fz, 1, 1)))
                values.append(u + (0.5 * step_dt) * acc + exs[i] * ey)
            return (after, new_fys, ext), values

        def several(a, carry, one=one, some=some):
            body = 2 * UNROLL
            rows = []
            for q in range(UNROLL):
                carry, even = one(2 * (a * UNROLL + q), carry)
                carry, odd = one(2 * (a * UNROLL + q) + 1, carry)
                emit(a * UNROLL + q, some, even, odd)
                rows += [even, odd]
            here, fys, ext = carry
            if ext:
                kept = []
                for j in range(len(some)):
                    acc = _roll(ext[j], LANES - body, 1)
                    for q in range(body):
                        shift = (LANES - (body - 1 - q)) % LANES
                        moved = _roll(rows[q][j], shift, 1) if shift else rows[q][j]
                        acc = jnp.where(zpos == DEPTH - body + q, moved, acc)
                    kept.append(acc)
                ext = tuple(kept)
            return here, fys, ext

        ext = tuple(extra[i] for i in some) if extra else ()
        results += lax.fori_loop(0, DEPTH // 2 // UNROLL, several, (here, fys, ext))[2]
    return results


def _forecast_body(
    planes, u_ref, c_ref, lo_ref, hi_ref, clo_ref, chi_ref, ex_ref, ey_ref, out_ref, surf_ref, e_ref, ce_ref, u1_ref
):
    m = pl.program_id(0)
    lane = lax.broadcasted_iota(jnp.int32, (8, LANES), 1)
    low_half = lane < DEPTH
    tiles = planes // 8
    half = DEPTH // 2

    def close(ref):
        for r in range(0, ROWS, 8):
            first = ref[pl.ds(r, 8), :]
            ref[pl.ds(DEPTH * ROWS + r, 8), :] = jnp.where(low_half, _roll(first, DEPTH, 1), 0.0)

    def fill(ref, main, low, high):
        def some(a, carry):
            ca = pl.ds(pl.multiple_of(a * LANES, LANES), LANES)
            cb = pl.ds(pl.multiple_of((a + half) * LANES, LANES), LANES)
            for read, row, size in [(main, FIRST_ROW + 8 * i, 8) for i in range(tiles)] + [
                (low, FIRST_ROW - 2, 2),
                (high, FIRST_ROW + planes, 2),
            ]:
                start = row - FIRST_ROW if size == 8 else 0
                even, odd = _wide_pair(read(start, size, ca), read(start, size, cb), low_half[:size])
                ref[pl.ds(2 * a * ROWS + row, size), :] = even
                ref[pl.ds((2 * a + 1) * ROWS + row, size), :] = odd
            return carry

        def several(a, carry):
            for q in range(FILL_UNROLL):
                carry = some(a * FILL_UNROLL + q, carry)
            return carry

        lax.fori_loop(0, half // FILL_UNROLL, several, 0)
        close(ref)

    @pl.when(m == 0)
    def _():
        def blank(i, carry):
            for ref in (e_ref, ce_ref, u1_ref):
                for r in (0, ROWS - 8):
                    ref[pl.ds(i * ROWS + r, 8), :] = jnp.zeros((8, LANES), jnp.float32)
            return carry

        lax.fori_loop(0, DEPTH + 1, blank, 0, unroll=13)
        fill(
            ce_ref,
            lambda s, n, c: c_ref[pl.ds(s, n), c],
            lambda s, n, c: clo_ref[0, pl.ds(s, n), c],
            lambda s, n, c: chi_ref[0, pl.ds(s, n), c],
        )

    fill(
        e_ref,
        lambda s, n, c: u_ref[0, pl.ds(s, n), c],
        lambda s, n, c: lo_ref[0, pl.ds(s, n), c],
        lambda s, n, c: hi_ref[0, pl.ds(s, n), c],
    )

    def ey_row(t):
        return lambda y: ey_ref[0, t, pl.ds(y, 1), :]

    wide = tiles + 1
    base1 = FIRST_ROW - 4
    ex1 = [ex_ref[0, 0, pl.ds(base1 + i, 8, stride=wide), :] for i in range(wide)]

    def emit1(a, some, even, odd):
        for p, values in ((0, even), (1, odd)):
            for i, value in zip(some, values):
                at = pl.ds((2 * a + p) * ROWS + base1 + i, 8, stride=wide)
                u1_ref[at, :] = jnp.where(ce_ref[at, :] > 0.0, value, 0.0)

    _stencil_step(e_ref, ce_ref, base1, wide, ex1, ey_row(0), emit1, ())
    close(u1_ref)

    ex2 = [ex_ref[0, 1, pl.ds(FIRST_ROW + i, 8, stride=tiles), :] for i in range(tiles)]
    out = out_ref.reshape(DEPTH * planes, LANES)

    def emit2(a, some, even, odd):
        for j, i in enumerate(some):
            one, two = _wide_pair(even[j], odd[j], low_half)
            out[pl.ds(a * planes + i, 8, stride=tiles), :] = one
            out[pl.ds((a + half) * planes + i, 8, stride=tiles), :] = two

    start = tuple(jnp.zeros((8, LANES), jnp.float32) for _ in range(tiles))
    surface = _stencil_step(u1_ref, ce_ref, FIRST_ROW, tiles, ex2, ey_row(1), emit2, start)
    surf = surf_ref.reshape(planes, LANES)
    for i in range(tiles):
        surf[pl.ds(i, 8, stride=tiles), :] = surface[i]


def forecast(u, cond, low, high, ex, ey, blocks):
    members, planes, columns = u.shape
    halves = columns // blocks // LANES
    whole = lambda shape: pl.BlockSpec(shape, lambda m: (0,) * len(shape))
    scratch = pltpu.VMEM(((DEPTH + 1) * ROWS, LANES), jnp.float32)
    return pl.pallas_call(
        functools.partial(_forecast_body, planes),
        grid=(members,),
        in_specs=[
            pl.BlockSpec((1, planes, columns), lambda m: (m, 0, 0)),
            whole((planes, columns)),
            pl.BlockSpec((1, 2, columns), lambda m: (m, 0, 0)),
            pl.BlockSpec((1, 2, columns), lambda m: (m, 0, 0)),
            pl.BlockSpec((1, 2, columns), lambda m: (members, 0, 0)),
            pl.BlockSpec((1, 2, columns), lambda m: (members, 0, 0)),
            pl.BlockSpec((1, STEPS, ROWS, LANES), lambda m: (m, 0, 0, 0)),
            pl.BlockSpec((1, STEPS, DEPTH, LANES), lambda m: (m, 0, 0, 0)),
        ],
        out_specs=[
            pl.BlockSpec((blocks, 1, halves, planes, LANES), lambda m: (0, m, 0, 0, 0)),
            pl.BlockSpec((2, 1, planes // 2, LANES), lambda m: (0, m, 0, 0)),
        ],
        out_shape=[
            jax.ShapeDtypeStruct((blocks, members, halves, planes, LANES), jnp.float32),
            jax.ShapeDtypeStruct((2, members, planes // 2, LANES), jnp.float32),
        ],
        scratch_shapes=[scratch, scratch, scratch],
        compiler_params=pltpu.CompilerParams(
            dimension_semantics=("arbitrary",), vmem_limit_bytes=32 << 20
        ),
        cost_estimate=pl.CostEstimate(flops=200_000_000, bytes_accessed=10_000_000, transcendentals=0),
        name="forecast",
    )(u, cond, low, high, low, high, ex, ey)


def _nt(a, b):
    return lax.dot_general(
        a, b, (((1,), (1,)), ((), ())), precision=lax.Precision.HIGHEST, preferred_element_type=jnp.float32
    )


def _cell_sums_body(pc_ref, obs_ref, var_ref, out_ref):
    planes = pc_ref.shape[0]
    cell = lax.broadcasted_iota(jnp.int32, (planes, LANES), 1)
    weight = 1.0 / var_ref[...]
    value = weight * obs_ref[...]
    pc = pc_ref[...]
    wsum = jnp.zeros((planes, LANES), jnp.float32)
    rsum = jnp.zeros((planes, LANES), jnp.float32)
    for j in range(pc.shape[1]):
        hit = pc[:, j : j + 1] == cell
        wsum = wsum + jnp.where(hit, weight[:, j : j + 1], 0.0)
        rsum = rsum + jnp.where(hit, value[:, j : j + 1], 0.0)
    cut = planes // 2
    for part in range(2):
        out_ref[part, 0] = wsum[part * cut : (part + 1) * cut]
        out_ref[part, 1] = rsum[part * cut : (part + 1) * cut]


def cell_sums(pixel_cell, observed, obs_var):
    planes = pixel_cell.shape[0]
    return pl.pallas_call(
        _cell_sums_body,
        out_shape=jax.ShapeDtypeStruct((2, 2, planes // 2, LANES), jnp.float32),
        cost_estimate=pl.CostEstimate(flops=400_000, bytes_accessed=100_000, transcendentals=0),
        name="cell_sums",
    )(pixel_cell, observed, obs_var)


def _gram_body(seen_ref, sums_ref, out_ref):
    planes = sums_ref.shape[2]
    sources = sums_ref.shape[0]
    count = seen_ref.shape[0] // planes
    total = sums_ref[0]
    for i in range(1, sources):
        total = total + sums_ref[i]
    gram = jnp.zeros((count, count), jnp.float32)
    proj = jnp.zeros((8, count), jnp.float32)
    for x in range(planes):
        s = seen_ref[pl.ds(x, count, stride=planes), :]
        wsum = total[0, x : x + 1]
        rsum = total[1, x : x + 1]
        mean = jnp.sum(s, axis=0, keepdims=True) * (1.0 / count)
        anom = s - mean
        gram = gram + _nt(anom * wsum, anom)
        proj = proj + _nt(jnp.broadcast_to(rsum - wsum * mean, (8, LANES)), anom)
    out_ref[pl.ds(0, count), :] = gram
    out_ref[pl.ds(count, 8), :] = proj


def gram_part(seen, sums):
    planes = sums.shape[2]
    count = seen.shape[0] // planes
    return pl.pallas_call(
        _gram_body,
        out_shape=jax.ShapeDtypeStruct((count + 8, count), jnp.float32),
        cost_estimate=pl.CostEstimate(flops=80_000_000, bytes_accessed=1_700_000, transcendentals=0),
        name="gram",
    )(seen, sums)


GROUP = 4


def _mix_body(p0_ref, p1_ref, p2_ref, p3_ref, hi_ref, lo_ref, a_ref):
    count = hi_ref.shape[0]

    def total(rows):
        return (p0_ref[rows, :] + p1_ref[rows, :]) + (p2_ref[rows, :] + p3_ref[rows, :])

    proj = total(pl.ds(count, 8))
    ntile = count // 8
    sub = lax.broadcasted_iota(jnp.int32, (8, LANES), 0)
    lane = lax.broadcasted_iota(jnp.int32, (8, LANES), 1)
    a, inv, diag = [], [], []
    for i in range(ntile):
        eye = (lane == sub + 8 * i).astype(jnp.float32)
        a.append(eye + total(pl.ds(8 * i, 8)) * (1.0 / (count - 1)))
        inv.append(eye)
        diag.append(jnp.ones((8, LANES), jnp.float32))

    def row_of(tile, r):
        return jnp.broadcast_to(tile[r : r + 1, :], (8, LANES))

    for j0 in range(0, count, GROUP):
        base = j0 // 8
        cols = [
            {i: jnp.broadcast_to(a[i][:, j0 + t : j0 + t + 1], (8, LANES)) for i in range(base, ntile)}
            for t in range(GROUP)
        ]
        r0 = j0 % 8
        arow = [row_of(a[base], r0 + t) for t in range(GROUP)]
        irow = [row_of(inv[base], r0 + t) for t in range(GROUP)]
        for t in range(GROUP):
            pivot = row_of(cols[t][base], r0 + t)
            recip = 1.0 / pivot
            diag[base] = jnp.where(sub == r0 + t, pivot, diag[base])
            for s in range(t + 1, GROUP):
                factor = row_of(cols[t][base], r0 + s) * recip
                for i in range(base, ntile):
                    cols[s][i] = cols[s][i] - factor * cols[t][i]
                arow[s] = arow[s] - factor * arow[t]
                irow[s] = irow[s] - factor * irow[t]
            arow[t] = arow[t] * recip
            irow[t] = irow[t] * recip
            cols[t][base] = jnp.where(sub > r0 + t, cols[t][base], 0.0)
        for i in range(base, ntile):
            for t in range(GROUP):
                a[i] = a[i] - cols[t][i] * arow[t]
                inv[i] = inv[i] - cols[t][i] * irow[t]
    for i in range(ntile):
        a_ref[pl.ds(8 * i, 8), :] = inv[i] / jnp.sqrt(diag[i])
    linv = a_ref[...]
    middle = _nt(proj, linv)
    wmean = lax.dot_general(
        middle, linv, (((1,), (0,)), ((), ())), precision=lax.Precision.HIGHEST, preferred_element_type=jnp.float32
    ) * (1.0 / (count - 1))
    mix = linv + wmean[0:1]
    mix = mix + (1.0 - jnp.sum(mix, axis=1, keepdims=True)) * (1.0 / count)
    hi = mix.astype(jnp.bfloat16)
    hi_ref[...] = hi
    lo_ref[...] = (mix - hi.astype(jnp.float32)).astype(jnp.bfloat16)


def mix_matrices(parts):
    count = parts[0].shape[1]
    shape = jax.ShapeDtypeStruct((count, count), jnp.bfloat16)
    return pl.pallas_call(
        _mix_body,
        out_shape=[shape, shape],
        scratch_shapes=[pltpu.VMEM((count, LANES), jnp.float32)],
        cost_estimate=pl.CostEstimate(flops=200_000_000, bytes_accessed=600_000, transcendentals=0),
        name="mix",
    )(*parts)


def _transform_body(f_ref, hi_ref, lo_ref, out_ref):
    count = hi_ref.shape[0]
    hi = hi_ref[...]
    lo = lo_ref[...]
    src = f_ref.reshape(count * 8, LANES)
    dst = out_ref.reshape(count * 8, LANES)
    for x in range(8):
        rows = pl.ds(x, count, stride=8)
        f = src[rows, :]
        fhi = f.astype(jnp.bfloat16)
        flo = (f - fhi.astype(jnp.float32)).astype(jnp.bfloat16)
        out = jnp.dot(hi, fhi, preferred_element_type=jnp.float32)
        out = out + jnp.dot(hi, flo, preferred_element_type=jnp.float32)
        out = out + jnp.dot(lo, fhi, preferred_element_type=jnp.float32)
        dst[rows, :] = out


def transform(block, hi, lo):
    count, halves, planes, _ = block.shape
    spec = pl.BlockSpec((count, 1, 8, LANES), lambda x, c: (0, c, x, 0))
    mat = pl.BlockSpec((count, count), lambda x, c: (0, 0))
    return pl.pallas_call(
        _transform_body,
        grid=(planes // 8, halves),
        in_specs=[spec, mat, mat],
        out_specs=spec,
        out_shape=jax.ShapeDtypeStruct(block.shape, jnp.float32),
        compiler_params=pltpu.CompilerParams(
            dimension_semantics=("arbitrary", "arbitrary"), vmem_limit_bytes=32 << 20
        ),
        cost_estimate=pl.CostEstimate(flops=900_000_000, bytes_accessed=8_500_000, transcendentals=0),
        name="transform",
    )(block, hi, lo)


def heat_factors(laser_x, laser_y, first):
    xs = first - FIRST_ROW + jnp.arange(ROWS, dtype=jnp.int32)
    dx = (xs[None, None, :] - laser_x[:, :, None]).astype(jnp.float32)
    ex = (step_dt * laser_power) * jnp.exp(-(dx * dx) / beam_spot_width)
    ex = jnp.broadcast_to(ex[..., None], ex.shape + (LANES,))
    lane = jnp.arange(LANES, dtype=jnp.int32)
    ys = jnp.arange(DEPTH, dtype=jnp.int32)[:, None] + (lane // DEPTH * DEPTH)[None, :]
    dy = (ys - laser_y[:, :, None, None]).astype(jnp.float32)
    ey = jnp.where(lane % DEPTH == DEPTH - 1, jnp.exp(-(dy * dy) / beam_spot_width), 0.0)
    return ex, ey


def for_halves(x, blocks):
    return jnp.broadcast_to(x[None], (blocks // 2,) + x.shape).reshape((blocks,) + x.shape[1:])


def per_device(initial_heat_matrix, conductivity, laser_x, laser_y, pixel_cell, observed, obs_var):
    members, planes, columns = initial_heat_matrix.shape
    blocks = 1
    for axis in MA:
        blocks *= lax.axis_size(axis)
    slabs = lax.axis_size("sa")
    first = lax.axis_index("sa") * planes
    u = initial_heat_matrix
    forward = [(i, i + 1) for i in range(slabs - 1)]
    backward = [(b, a) for a, b in forward]
    top = jnp.concatenate([u[:, planes - 2 :], conductivity[None, planes - 2 :]], axis=0)
    bottom = jnp.concatenate([u[:, :2], conductivity[None, :2]], axis=0)
    low = lax.ppermute(top, "sa", forward)
    high = lax.ppermute(bottom, "sa", backward)
    sums = cell_sums(pixel_cell, observed, obs_var)
    sums = lax.all_to_all(for_halves(sums, blocks), MA, 0, 0, tiled=True)
    ex, ey = heat_factors(laser_x, laser_y, first)
    sent, surf = forecast(u, conductivity, low, high, ex, ey, blocks)

    seen = lax.all_to_all(for_halves(surf, blocks), MA, 0, 0, tiled=True)
    part = gram_part(seen.reshape(blocks * members * planes // 2, LANES), sums)
    part = part + lax.ppermute(part, "ma_2", [(0, 1), (1, 0)])
    parts = [part] + [
        lax.ppermute(part, "sa", [(i, (i + s) % slabs) for i in range(slabs)]) for s in range(1, slabs)
    ]
    hi, lo = mix_matrices(parts)

    held = lax.all_to_all(sent, MA, 0, 0, tiled=True)
    done = transform(held.reshape((blocks * members,) + held.shape[2:]), hi, lo)
    back = lax.all_to_all(done.reshape(held.shape), MA, 0, 0, tiled=True)
    return back.transpose(1, 3, 0, 2, 4).reshape(members, planes, columns)


def solution(mesh):
    torus = Mesh(mesh.devices.reshape(4, 4, 2, mesh.shape["sa"]), ("ma_0", "ma_1", "ma_2", "sa"))
    in_specs = (
        P(MA, "sa", None),
        P("sa", None),
        P(MA, None),
        P(MA, None),
        P("sa", MA),
        P("sa", MA),
        P("sa", MA),
    )
    out_specs = P(MA, "sa", None)
    return jax.shard_map(
        per_device, mesh=torus, in_specs=in_specs, out_specs=out_specs, check_vma=False
    )
```

```python
import functools

import jax
import jax.numpy as jnp
from jax import lax
from jax.experimental import pallas as pl
from jax.experimental.pallas import tpu as pltpu
from jax.sharding import Mesh
from jax.sharding import PartitionSpec as P

DEPTH = 64
STEPS = 2
LANES = 128
MA = ("ma_0", "ma_1", "ma_2")
MA_SA = ("ma_0", "ma_1", "ma_2", "sa")

step_dt = 0.025
alpha_cond = 0.05
laser_power = 12.0
beam_spot_width = 18.0

def _roll(x, shift, axis):
    return pltpu.roll(x, shift, axis)


def _wide_pair(a, b, low_half):
    return jnp.where(low_half, a, _roll(b, DEPTH, 1)), jnp.where(low_half, _roll(a, DEPTH, 1), b)


UNROLL = {2: 8, 3: 8}
FILL_UNROLL = 16


def _stencil_step(src, cond, pitch, base, tiles, apart, exs, ey_at, emit, surface):
    lane = lax.broadcasted_iota(jnp.int32, (8, LANES), 1)
    low_half = lane < DEPTH
    zpos = lane & (DEPTH - 1)
    z_last = zpos == DEPTH - 1
    z_first = zpos == 0
    unroll = UNROLL[tiles]

    def load(y, i):
        at = pl.ds(y * pitch + (base + i), 8, stride=tiles)
        u = src[at, :]
        c = cond[at, :]
        return u, c + c * (alpha_cond * (u * u))

    def face(one, two):
        return (one[1] + two[1]) * (two[0] - one[0])

    here = [load(0, i) for i in range(tiles)]
    fys = []
    for i in range(tiles):
        u, k = load(DEPTH - 1, i)
        before = (
            jnp.where(low_half, 0.0, _roll(u, DEPTH, 1)),
            jnp.where(low_half, 0.0, _roll(k, DEPTH, 1)),
        )
        fys.append(face(before, here[i]))

    def one(y, here, fys):
        after = [load(y + 1, i) for i in range(tiles)]
        line = {i: here[i] for i in range(tiles)}
        for i in range(-apart, tiles + apart):
            if i not in line and (i + apart in range(tiles) or i - apart in range(tiles)):
                line[i] = load(y, i)
        fx = {i: face(line[i], line[i + apart]) for i in range(-apart, tiles) if i in line}
        ey = jnp.broadcast_to(ey_at(y), (8, LANES))
        new_fys, values = [], []
        for i in range(tiles):
            u, k = here[i]
            fy = face(here[i], after[i])
            new_fys.append(fy)
            acc = (fy - fys[i]) + (fx[i] - fx[i - apart])
            up = jnp.where(z_last, 0.0, _roll(u, LANES - 1, 1))
            kp = jnp.where(z_last, 0.0, _roll(k, LANES - 1, 1))
            fz = (k + kp) * (up - u)
            acc = acc + (fz - jnp.where(z_first, k * u, _roll(fz, 1, 1)))
            values.append(u + (0.5 * step_dt) * acc + exs[i] * ey)
        return after, new_fys, values

    def several(a, carry):
        here, fys, tops = carry
        rows = []
        for q in range(unroll):
            here, fys, even = one(2 * (a * unroll + q), here, fys)
            here, fys, odd = one(2 * (a * unroll + q) + 1, here, fys)
            emit(a * unroll + q, even, odd)
            rows += [even, odd]
        if surface:
            kept = []
            for i in range(tiles):
                acc = _roll(tops[i], (LANES - len(rows)) % LANES, 1)
                for q, values in enumerate(rows):
                    shift = (LANES - (len(rows) - 1 - q)) % LANES
                    moved = _roll(values[i], shift, 1) if shift else values[i]
                    acc = jnp.where(zpos == DEPTH - len(rows) + q, moved, acc)
                kept.append(acc)
            tops = kept
        return here, fys, tops

    tops = [jnp.zeros((8, LANES), jnp.float32) for _ in range(tiles)] if surface else []
    return lax.fori_loop(0, DEPTH // 2 // unroll, several, (here, fys, tops))[2]


def _close(ref, pitch):
    lane = lax.broadcasted_iota(jnp.int32, (8, LANES), 1)
    for r in range(0, pitch, 8):
        first = ref[pl.ds(r, 8), :]
        ref[pl.ds(DEPTH * pitch + r, 8), :] = jnp.where(lane < DEPTH, _roll(first, DEPTH, 1), 0.0)


def _fill(ref, pitch, pieces):
    half = DEPTH // 2
    lane = lax.broadcasted_iota(jnp.int32, (8, LANES), 1)
    low_half = lane < DEPTH

    def several(b, carry):
        for q in range(FILL_UNROLL):
            a = b * FILL_UNROLL + q
            ca = pl.ds(pl.multiple_of(a * LANES, LANES), LANES)
            cb = pl.ds(pl.multiple_of((a + half) * LANES, LANES), LANES)
            for read, start, size, row, stride in pieces:
                even, odd = _wide_pair(read(pl.ds(start, size), ca), read(pl.ds(start, size), cb), low_half[:size])
                ref[pl.ds(2 * a * pitch + row, size, stride=stride), :] = even
                ref[pl.ds((2 * a + 1) * pitch + row, size, stride=stride), :] = odd
        return carry

    lax.fori_loop(0, half // FILL_UNROLL, several, 0)
    _close(ref, pitch)


def _two_steps(m, e_ref, ce_ref, u1_ref, ex_ref, ey_ref, surf_ref, pitch, step1, step2, edged, put):
    def ey_row(t):
        return lambda y: ey_ref[0, t, pl.ds(y, 1), :]

    def factors(t, base, tiles):
        return [ex_ref[0, t, pl.ds(base + i, 8, stride=tiles), :] for i in range(tiles)]

    base, tiles, apart = step1

    def emit1(a, even, odd):
        for p, values in ((0, even), (1, odd)):
            for i, value in enumerate(values):
                at = pl.ds((2 * a + p) * pitch + base + i, 8, stride=tiles)
                u1_ref[at, :] = jnp.where(ce_ref[at, :] > 0.0, value, 0.0) if edged else value

    _stencil_step(e_ref, ce_ref, pitch, base, tiles, apart, factors(0, base, tiles), ey_row(0), emit1, False)
    _close(u1_ref, pitch)
    base, count, apart = step2
    low_half = lax.broadcasted_iota(jnp.int32, (8, LANES), 1) < DEPTH

    def emit2(a, even, odd):
        for i in range(count):
            one, two = _wide_pair(even[i], odd[i], low_half)
            put(a, i, one)
            put(a + DEPTH // 2, i, two)

    tops = _stencil_step(u1_ref, ce_ref, pitch, base, count, apart, factors(1, base, count), ey_row(1), emit2, True)
    return tops


INNER_PITCH = 32
OUTER_PITCH = 40
OUTER_ROW = 8


def _inner_body(u_ref, c_ref, ex_ref, ey_ref, out_ref, surf_ref, e_ref, ce_ref, u1_ref):
    m = pl.program_id(0)
    planes = u_ref.shape[1]
    half = planes // 2
    pitch = INNER_PITCH

    @pl.when(m == 0)
    def _():
        _fill(ce_ref, pitch, [(lambda r, c: c_ref[r, c], 8 * i, 8, 8 * i, 1) for i in range(planes // 8)])

    _fill(e_ref, pitch, [(lambda r, c: u_ref[0, r, c], 8 * i, 8, 8 * i, 1) for i in range(planes // 8)])
    out = out_ref.reshape(DEPTH * half, LANES)

    def put(v, i, value):
        out[pl.ds(v * half + i, 8, stride=2), :] = value

    tops = _two_steps(
        m, e_ref, ce_ref, u1_ref, ex_ref, ey_ref, surf_ref, pitch, (4, 3, 1), (8, 2, 1), False, put
    )
    surf = surf_ref.reshape(half, LANES)
    for i in range(2):
        surf[pl.ds(i, 8, stride=2), :] = tops[i]


def _outer_body(
    u_ref, c_ref, lo_ref, hi_ref, clo_ref, chi_ref, ex_ref, ey_ref, out_ref, surf_ref, e_ref, ce_ref, u1_ref
):
    m = pl.program_id(0)
    planes = u_ref.shape[1]
    half = planes // 2
    pitch = OUTER_PITCH

    def pieces(main, low, high):
        row = OUTER_ROW
        return [
            (low, 0, 2, row, 2),
            (main, 0, 8, row + 4, 2),
            (main, 8, 2, row + 20, 2),
            (main, planes - 10, 2, row + 1, 2),
            (main, planes - 8, 8, row + 5, 2),
            (high, 0, 2, row + 21, 2),
        ]

    @pl.when(m == 0)
    def _():
        _fill(
            ce_ref,
            pitch,
            pieces(lambda r, c: c_ref[r, c], lambda r, c: clo_ref[0, r, c], lambda r, c: chi_ref[0, r, c]),
        )

    _fill(
        e_ref,
        pitch,
        pieces(lambda r, c: u_ref[0, r, c], lambda r, c: lo_ref[0, r, c], lambda r, c: hi_ref[0, r, c]),
    )
    out = out_ref.reshape(DEPTH * half, LANES)

    def put(v, i, value):
        out[pl.ds(pl.multiple_of(v * half + 8 * i, 8), 8), :] = value

    tops = _two_steps(
        m, e_ref, ce_ref, u1_ref, ex_ref, ey_ref, surf_ref, pitch,
        (OUTER_ROW, 3, 2), (OUTER_ROW + 4, 2, 2), True, put,
    )
    for i in range(2):
        surf_ref[0, pl.ds(8 * i, 8), :] = tops[i]


def _forecast_call(body, name, pitch, operands, specs, ex, ey, members, planes, blocks, halves):
    scratch = pltpu.VMEM(((DEPTH + 1) * pitch, LANES), jnp.float32)
    return pl.pallas_call(
        body,
        grid=(members,),
        in_specs=specs
        + [
            pl.BlockSpec((1, STEPS, pitch, LANES), lambda m: (m, 0, 0, 0)),
            pl.BlockSpec((1, STEPS, DEPTH, LANES), lambda m: (m, 0, 0, 0)),
        ],
        out_specs=[
            pl.BlockSpec((blocks, 1, halves, planes // 2, LANES), lambda m: (0, m, 0, 0, 0)),
            pl.BlockSpec((1, planes // 2, LANES), lambda m: (m, 0, 0)),
        ],
        out_shape=[
            jax.ShapeDtypeStruct((blocks, members, halves, planes // 2, LANES), jnp.float32),
            jax.ShapeDtypeStruct((members, planes // 2, LANES), jnp.float32),
        ],
        scratch_shapes=[scratch, scratch, scratch],
        compiler_params=pltpu.CompilerParams(
            dimension_semantics=("arbitrary",), vmem_limit_bytes=28 << 20
        ),
        cost_estimate=pl.CostEstimate(flops=100_000_000, bytes_accessed=7_000_000, transcendentals=0),
        name=name,
    )(*operands, ex, ey)


def forecast_inner(u, cond, ex, ey, blocks):
    members, planes, columns = u.shape
    specs = [
        pl.BlockSpec((1, planes, columns), lambda m: (m, 0, 0)),
        pl.BlockSpec((planes, columns), lambda m: (0, 0)),
    ]
    return _forecast_call(
        _inner_body, "inner", INNER_PITCH, (u, cond), specs, ex, ey, members, planes, blocks, columns // blocks // LANES
    )


def forecast_outer(u, cond, low, high, ex, ey, blocks):
    members, planes, columns = u.shape
    edge = lambda at: pl.BlockSpec((1, 2, columns), at)
    specs = [
        pl.BlockSpec((1, planes, columns), lambda m: (m, 0, 0)),
        pl.BlockSpec((planes, columns), lambda m: (0, 0)),
        edge(lambda m: (m, 0, 0)),
        edge(lambda m: (m, 0, 0)),
        edge(lambda m: (members, 0, 0)),
        edge(lambda m: (members, 0, 0)),
    ]
    operands = (u, cond, low, high, low, high)
    return _forecast_call(
        _outer_body, "outer", OUTER_PITCH, operands, specs, ex, ey, members, planes, blocks, columns // blocks // LANES
    )


def _nt(a, b):
    return lax.dot_general(
        a, b, (((1,), (1,)), ((), ())), precision=lax.Precision.HIGHEST, preferred_element_type=jnp.float32
    )


def _cell_sums_body(pc_ref, obs_ref, var_ref, out_ref):
    planes = pc_ref.shape[0]
    cell = lax.broadcasted_iota(jnp.int32, (planes, LANES), 1)
    weight = 1.0 / var_ref[...]
    value = weight * obs_ref[...]
    pc = pc_ref[...]
    wsum = jnp.zeros((planes, LANES), jnp.float32)
    rsum = jnp.zeros((planes, LANES), jnp.float32)
    for j in range(pc.shape[1]):
        hit = pc[:, j : j + 1] == cell
        wsum = wsum + jnp.where(hit, weight[:, j : j + 1], 0.0)
        rsum = rsum + jnp.where(hit, value[:, j : j + 1], 0.0)
    tiles = [8 * i for i in range(planes // 8)]
    inner, outer = tiles[1:-1], [tiles[0], tiles[-1]]
    for part, (one, two) in enumerate((inner, outer)):
        out_ref[part] = (
            wsum[one : one + 8]
            + _roll(rsum[one : one + 8], 64, 1)
            + _roll(wsum[two : two + 8], 32, 1)
            + _roll(rsum[two : two + 8], 96, 1)
        )


def cell_sums(pixel_cell, observed, obs_var):
    return pl.pallas_call(
        _cell_sums_body,
        out_shape=jax.ShapeDtypeStruct((2, 8, LANES), jnp.float32),
        cost_estimate=pl.CostEstimate(flops=400_000, bytes_accessed=100_000, transcendentals=0),
        name="cell_sums",
    )(pixel_cell, observed, obs_var)


def _gram_body(members, planes, seen_ref, out_ref, s_ref):
    sources = seen_ref.shape[0]
    count = sources * members
    group = lax.broadcasted_iota(jnp.int32, (8, LANES), 1) // 4
    sums = [jnp.zeros((8, LANES), jnp.float32) for _ in range(4)]
    for i in range(sources):
        row = seen_ref[i, pl.ds(members * planes, 8), :]
        for g in range(4):
            sums[g] = jnp.where(group == (i + 8 * g) % sources, row, sums[g])
        s_ref[pl.ds(i * members * planes, members * planes), :] = seen_ref[i, pl.ds(0, members * planes), :]
    w_one, w_two, r_one, r_two = (
        _roll(sums[g], (LANES - 32 * g) % LANES, 1) if g else sums[g] for g in range(4)
    )
    wsums = [w_one, w_two]
    rsums = [r_one, r_two]
    gram = jnp.zeros((count, count), jnp.float32)
    proj = jnp.zeros((8, count), jnp.float32)
    for x in range(planes):
        s = s_ref[pl.ds(x, count, stride=planes), :]
        wsum = wsums[x // 8][x % 8 : x % 8 + 1]
        rsum = rsums[x // 8][x % 8 : x % 8 + 1]
        mean = jnp.sum(s, axis=0, keepdims=True) * (1.0 / count)
        anom = s - mean
        gram = gram + _nt(anom * wsum, anom)
        proj = proj + _nt(jnp.broadcast_to(rsum - wsum * mean, (8, LANES)), anom)
    out_ref[pl.ds(0, count), :] = gram
    out_ref[pl.ds(count, 8), :] = proj


def gram_part(seen, members, planes):
    count = seen.shape[0] * members
    return pl.pallas_call(
        functools.partial(_gram_body, members, planes),
        out_shape=jax.ShapeDtypeStruct((count + 8, count), jnp.float32),
        scratch_shapes=[pltpu.VMEM((count * planes, LANES), jnp.float32)],
        cost_estimate=pl.CostEstimate(flops=80_000_000, bytes_accessed=1_700_000, transcendentals=0),
        name="gram",
    )(seen)


GROUP = 4


def _mix_body(p0_ref, p1_ref, p2_ref, p3_ref, hi_ref, lo_ref, a_ref):
    count = hi_ref.shape[0]

    def total(rows):
        return (p0_ref[rows, :] + p1_ref[rows, :]) + (p2_ref[rows, :] + p3_ref[rows, :])

    proj = total(pl.ds(count, 8))
    ntile = count // 8
    sub = lax.broadcasted_iota(jnp.int32, (8, LANES), 0)
    lane = lax.broadcasted_iota(jnp.int32, (8, LANES), 1)
    a, inv, diag = [], [], []
    for i in range(ntile):
        eye = (lane == sub + 8 * i).astype(jnp.float32)
        a.append(eye + total(pl.ds(8 * i, 8)) * (1.0 / (count - 1)))
        inv.append(eye)
        diag.append(jnp.ones((8, LANES), jnp.float32))

    def row_of(tile, r):
        return jnp.broadcast_to(tile[r : r + 1, :], (8, LANES))

    for j0 in range(0, count, GROUP):
        base = j0 // 8
        cols = [
            {i: jnp.broadcast_to(a[i][:, j0 + t : j0 + t + 1], (8, LANES)) for i in range(base, ntile)}
            for t in range(GROUP)
        ]
        r0 = j0 % 8
        arow = [row_of(a[base], r0 + t) for t in range(GROUP)]
        irow = [row_of(inv[base], r0 + t) for t in range(GROUP)]
        for t in range(GROUP):
            pivot = row_of(cols[t][base], r0 + t)
            recip = 1.0 / pivot
            diag[base] = jnp.where(sub == r0 + t, pivot, diag[base])
            for s in range(t + 1, GROUP):
                factor = row_of(cols[t][base], r0 + s) * recip
                for i in range(base, ntile):
                    cols[s][i] = cols[s][i] - factor * cols[t][i]
                arow[s] = arow[s] - factor * arow[t]
                irow[s] = irow[s] - factor * irow[t]
            arow[t] = arow[t] * recip
            irow[t] = irow[t] * recip
            cols[t][base] = jnp.where(sub > r0 + t, cols[t][base], 0.0)
        for i in range(base, ntile):
            for t in range(GROUP):
                a[i] = a[i] - cols[t][i] * arow[t]
                inv[i] = inv[i] - cols[t][i] * irow[t]
    for i in range(ntile):
        a_ref[pl.ds(8 * i, 8), :] = inv[i] / jnp.sqrt(diag[i])
    linv = a_ref[...]
    middle = _nt(proj, linv)
    wmean = lax.dot_general(
        middle, linv, (((1,), (0,)), ((), ())), precision=lax.Precision.HIGHEST, preferred_element_type=jnp.float32
    ) * (1.0 / (count - 1))
    mix = linv + wmean[0:1]
    mix = mix + (1.0 - jnp.sum(mix, axis=1, keepdims=True)) * (1.0 / count)
    hi = mix.astype(jnp.bfloat16)
    hi_ref[...] = hi
    lo_ref[...] = (mix - hi.astype(jnp.float32)).astype(jnp.bfloat16)


def mix_matrices(parts):
    count = parts[0].shape[1]
    shape = jax.ShapeDtypeStruct((count, count), jnp.bfloat16)
    return pl.pallas_call(
        _mix_body,
        out_shape=[shape, shape],
        scratch_shapes=[pltpu.VMEM((count, LANES), jnp.float32)],
        cost_estimate=pl.CostEstimate(flops=200_000_000, bytes_accessed=600_000, transcendentals=0),
        name="mix",
    )(*parts)


def _transform_body(f_ref, hi_ref, lo_ref, out_ref):
    count = hi_ref.shape[0]
    hi = hi_ref[...]
    lo = lo_ref[...]
    src = f_ref.reshape(count * 8, LANES)
    dst = out_ref.reshape(count * 8, LANES)
    for x in range(8):
        rows = pl.ds(x, count, stride=8)
        f = src[rows, :]
        fhi = f.astype(jnp.bfloat16)
        flo = (f - fhi.astype(jnp.float32)).astype(jnp.bfloat16)
        out = jnp.dot(hi, fhi, preferred_element_type=jnp.float32)
        out = out + jnp.dot(hi, flo, preferred_element_type=jnp.float32)
        out = out + jnp.dot(lo, fhi, preferred_element_type=jnp.float32)
        dst[rows, :] = out


def _transform_more(f_ref, hi_ref, lo_ref, _, out_ref):
    _transform_body(f_ref, hi_ref, lo_ref, out_ref)


def transform(block, hi, lo, onto=None):
    count, halves, planes, _ = block.shape
    first = 0 if onto is None else planes // 8
    mat = pl.BlockSpec((count, count), lambda x, c: (0, 0))
    in_specs = [pl.BlockSpec((count, 1, 8, LANES), lambda x, c: (0, c, x, 0)), mat, mat]
    operands = (block, hi, lo)
    if onto is not None:
        in_specs.append(pl.BlockSpec(memory_space=pl.ANY))
        operands += (onto,)
    return pl.pallas_call(
        _transform_body if onto is None else _transform_more,
        grid=(planes // 8, halves),
        in_specs=in_specs,
        out_specs=pl.BlockSpec((count, 1, 8, LANES), lambda x, c: (0, c, x + first, 0)),
        out_shape=jax.ShapeDtypeStruct((count, halves, 2 * planes, LANES), jnp.float32),
        input_output_aliases={} if onto is None else {3: 0},
        compiler_params=pltpu.CompilerParams(
            dimension_semantics=("arbitrary", "arbitrary"), vmem_limit_bytes=24 << 20
        ),
        cost_estimate=pl.CostEstimate(flops=450_000_000, bytes_accessed=4_300_000, transcendentals=0),
        name="transform",
    )(*operands)


def _place_body(in_ref, out_ref):
    group, _, halves, planes, _ = in_ref.shape
    inner = planes // 2
    order = list(range(inner, inner + 8, 8)) + list(range(0, inner, 8)) + list(range(inner + 8, planes, 8))
    for s in range(group):
        for h in range(halves):
            cols = pl.ds((s * halves + h) * LANES, LANES)
            for x, row in enumerate(order):
                out_ref[0, pl.ds(8 * x, 8), cols] = in_ref[s, 0, h, pl.ds(row, 8), :]


def place(back):
    blocks, members, halves, planes, _ = back.shape
    group = 8
    return pl.pallas_call(
        _place_body,
        grid=(members, blocks // group),
        in_specs=[pl.BlockSpec((group, 1, halves, planes, LANES), lambda m, b: (b, m, 0, 0, 0))],
        out_specs=pl.BlockSpec((1, planes, group * halves * LANES), lambda m, b: (m, 0, b)),
        out_shape=jax.ShapeDtypeStruct((members, planes, blocks * halves * LANES), jnp.float32),
        compiler_params=pltpu.CompilerParams(dimension_semantics=("arbitrary", "arbitrary")),
        cost_estimate=pl.CostEstimate(flops=0, bytes_accessed=8_400_000, transcendentals=0),
        name="place",
    )(back)


def heat_in_x(laser_x, xs):
    dx = (xs[None, None, :] - laser_x[:, :, None]).astype(jnp.float32)
    ex = (step_dt * laser_power) * jnp.exp(-(dx * dx) / beam_spot_width)
    return jnp.broadcast_to(ex[..., None], ex.shape + (LANES,))


def heat_in_y(laser_y):
    lane = jnp.arange(LANES, dtype=jnp.int32)
    ys = jnp.arange(DEPTH, dtype=jnp.int32)[:, None] + (lane // DEPTH * DEPTH)[None, :]
    dy = (ys - laser_y[:, :, None, None]).astype(jnp.float32)
    return jnp.where(lane % DEPTH == DEPTH - 1, jnp.exp(-(dy * dy) / beam_spot_width), 0.0)


def inner_planes(first):
    return first + jnp.arange(INNER_PITCH, dtype=jnp.int32)


def outer_planes(first, planes):
    row = jnp.arange(OUTER_PITCH, dtype=jnp.int32) - OUTER_ROW
    return first + row // 2 - 2 + (row % 2) * (planes - 8)


def per_device(initial_heat_matrix, conductivity, laser_x, laser_y, pixel_cell, observed, obs_var):
    members, planes, columns = initial_heat_matrix.shape
    blocks = 1
    for axis in MA:
        blocks *= lax.axis_size(axis)
    slabs = lax.axis_size("sa")
    first = lax.axis_index("sa") * planes
    u = initial_heat_matrix
    forward = [(i, i + 1) for i in range(slabs - 1)]
    backward = [(b, a) for a, b in forward]
    top = jnp.concatenate([u[:, planes - 2 :], conductivity[None, planes - 2 :]], axis=0)
    bottom = jnp.concatenate([u[:, :2], conductivity[None, :2]], axis=0)
    low = lax.ppermute(top, "sa", forward)
    high = lax.ppermute(bottom, "sa", backward)
    ey = heat_in_y(laser_y)
    sent_in, surf_in = forecast_inner(u, conductivity, heat_in_x(laser_x, inner_planes(first)), ey, blocks)
    held_in = lax.all_to_all(sent_in, MA, 0, 0, tiled=True)
    ex = heat_in_x(laser_x, outer_planes(first, planes))
    sent_out, surf_out = forecast_outer(u, conductivity, low, high, ex, ey, blocks)

    sums = cell_sums(pixel_cell, observed, obs_var)
    rows = jnp.concatenate([jnp.stack([surf_in, surf_out]).reshape(2, members * planes // 2, LANES), sums], axis=1)
    rows = jnp.broadcast_to(rows[None], (blocks // 2,) + rows.shape).reshape((blocks,) + rows.shape[1:])
    rows, held_in = lax.optimization_barrier((rows, held_in))
    seen = lax.all_to_all(rows, MA, 0, 0, tiled=True)
    part = gram_part(seen, members, planes // 2)
    part = part + lax.ppermute(part, "ma_2", [(0, 1), (1, 0)])
    parts = [part] + [
        lax.ppermute(part, "sa", [(i, (i + s) % slabs) for i in range(slabs)]) for s in range(1, slabs)
    ]
    hi, lo = mix_matrices(parts)

    held_out = lax.all_to_all(sent_out, MA, 0, 0, tiled=True)
    shape = (blocks * members,) + held_in.shape[2:]
    done = transform(held_in.reshape(shape), hi, lo)
    done = transform(held_out.reshape(shape), hi, lo, done)
    back = lax.all_to_all(done.reshape((blocks, members) + done.shape[1:]), MA, 0, 0, tiled=True)
    return place(back)


def solution(mesh):
    torus = Mesh(mesh.devices.reshape(4, 4, 2, mesh.shape["sa"]), ("ma_0", "ma_1", "ma_2", "sa"))
    in_specs = (
        P(MA, "sa", None),
        P("sa", None),
        P(MA, None),
        P(MA, None),
        P("sa", MA),
        P("sa", MA),
        P("sa", MA),
    )
    out_specs = P(MA, "sa", None)
    return jax.shard_map(
        per_device, mesh=torus, in_specs=in_specs, out_specs=out_specs, check_vma=False
    )
```

```python
import functools

import jax
import jax.numpy as jnp
from jax import lax
from jax.experimental import pallas as pl
from jax.experimental.pallas import tpu as pltpu
from jax.sharding import Mesh
from jax.sharding import PartitionSpec as P

DEPTH = 64
STEPS = 2
LANES = 128
VMEM_BYTES = 60 << 20
MA = ("ma_0", "ma_1", "ma_2")
MA_SA = ("ma_0", "ma_1", "ma_2", "sa")

step_dt = 0.025
alpha_cond = 0.05
laser_power = 12.0
beam_spot_width = 18.0

def _roll(x, shift, axis):
    return pltpu.roll(x, shift, axis)


def _wide_pair(a, b, low_half):
    return jnp.where(low_half, a, _roll(b, DEPTH, 1)), jnp.where(low_half, _roll(a, DEPTH, 1), b)


UNROLL = {2: 8, 3: 8}
FILL_UNROLL = 16


def _stencil_step(src, cond, pitch, base, tiles, apart, exs, ey_at, emit, surface):
    lane = lax.broadcasted_iota(jnp.int32, (8, LANES), 1)
    low_half = lane < DEPTH
    zpos = lane & (DEPTH - 1)
    z_last = zpos == DEPTH - 1
    z_first = zpos == 0
    unroll = UNROLL[tiles]

    def load(y, i):
        at = pl.ds(y * pitch + (base + i), 8, stride=tiles)
        u = src[at, :]
        c = cond[at, :]
        return u, c + c * (alpha_cond * (u * u))

    def face(one, two):
        return (one[1] + two[1]) * (two[0] - one[0])

    here = [load(0, i) for i in range(tiles)]
    fys = []
    for i in range(tiles):
        u, k = load(DEPTH - 1, i)
        before = (
            jnp.where(low_half, 0.0, _roll(u, DEPTH, 1)),
            jnp.where(low_half, 0.0, _roll(k, DEPTH, 1)),
        )
        fys.append(face(before, here[i]))

    def one(y, here, fys):
        after = [load(y + 1, i) for i in range(tiles)]
        line = {i: here[i] for i in range(tiles)}
        for i in range(-apart, tiles + apart):
            if i not in line and (i + apart in range(tiles) or i - apart in range(tiles)):
                line[i] = load(y, i)
        fx = {i: face(line[i], line[i + apart]) for i in range(-apart, tiles) if i in line}
        ey = jnp.broadcast_to(ey_at(y), (8, LANES))
        new_fys, values = [], []
        for i in range(tiles):
            u, k = here[i]
            fy = face(here[i], after[i])
            new_fys.append(fy)
            acc = (fy - fys[i]) + (fx[i] - fx[i - apart])
            up = jnp.where(z_last, 0.0, _roll(u, LANES - 1, 1))
            kp = jnp.where(z_last, 0.0, _roll(k, LANES - 1, 1))
            fz = (k + kp) * (up - u)
            acc = acc + (fz - jnp.where(z_first, k * u, _roll(fz, 1, 1)))
            values.append(u + (0.5 * step_dt) * acc + exs[i] * ey)
        return after, new_fys, values

    def several(a, carry):
        here, fys, tops = carry
        rows = []
        for q in range(unroll):
            here, fys, even = one(2 * (a * unroll + q), here, fys)
            here, fys, odd = one(2 * (a * unroll + q) + 1, here, fys)
            emit(a * unroll + q, even, odd)
            rows += [even, odd]
        if surface:
            kept = []
            for i in range(tiles):
                acc = _roll(tops[i], (LANES - len(rows)) % LANES, 1)
                for q, values in enumerate(rows):
                    shift = (LANES - (len(rows) - 1 - q)) % LANES
                    moved = _roll(values[i], shift, 1) if shift else values[i]
                    acc = jnp.where(zpos == DEPTH - len(rows) + q, moved, acc)
                kept.append(acc)
            tops = kept
        return here, fys, tops

    tops = [jnp.zeros((8, LANES), jnp.float32) for _ in range(tiles)] if surface else []
    return lax.fori_loop(0, DEPTH // 2 // unroll, several, (here, fys, tops))[2]


def _close(ref, pitch):
    lane = lax.broadcasted_iota(jnp.int32, (8, LANES), 1)
    for r in range(0, pitch, 8):
        first = ref[pl.ds(r, 8), :]
        ref[pl.ds(DEPTH * pitch + r, 8), :] = jnp.where(lane < DEPTH, _roll(first, DEPTH, 1), 0.0)


def _fill(ref, pitch, pieces):
    half = DEPTH // 2
    lane = lax.broadcasted_iota(jnp.int32, (8, LANES), 1)
    low_half = lane < DEPTH

    def several(b, carry):
        for q in range(FILL_UNROLL):
            a = b * FILL_UNROLL + q
            ca = pl.ds(pl.multiple_of(a * LANES, LANES), LANES)
            cb = pl.ds(pl.multiple_of((a + half) * LANES, LANES), LANES)
            for read, start, size, row, stride in pieces:
                even, odd = _wide_pair(read(pl.ds(start, size), ca), read(pl.ds(start, size), cb), low_half[:size])
                ref[pl.ds(2 * a * pitch + row, size, stride=stride), :] = even
                ref[pl.ds((2 * a + 1) * pitch + row, size, stride=stride), :] = odd
        return carry

    lax.fori_loop(0, half // FILL_UNROLL, several, 0)
    _close(ref, pitch)


def _two_steps(m, e_ref, ce_ref, u1_ref, ex_ref, ey_ref, surf_ref, pitch, step1, step2, edged, put):
    def ey_row(t):
        return lambda y: ey_ref[0, t, pl.ds(y, 1), :]

    def factors(t, base, tiles):
        return [ex_ref[0, t, pl.ds(base + i, 8, stride=tiles), :] for i in range(tiles)]

    base, tiles, apart = step1

    def emit1(a, even, odd):
        for p, values in ((0, even), (1, odd)):
            for i, value in enumerate(values):
                at = pl.ds((2 * a + p) * pitch + base + i, 8, stride=tiles)
                u1_ref[at, :] = jnp.where(ce_ref[at, :] > 0.0, value, 0.0) if edged else value

    _stencil_step(e_ref, ce_ref, pitch, base, tiles, apart, factors(0, base, tiles), ey_row(0), emit1, False)
    _close(u1_ref, pitch)
    base, count, apart = step2
    low_half = lax.broadcasted_iota(jnp.int32, (8, LANES), 1) < DEPTH

    def emit2(a, even, odd):
        for i in range(count):
            one, two = _wide_pair(even[i], odd[i], low_half)
            put(a, i, one)
            put(a + DEPTH // 2, i, two)

    tops = _stencil_step(u1_ref, ce_ref, pitch, base, count, apart, factors(1, base, count), ey_row(1), emit2, True)
    return tops


INNER_PITCH = 32
OUTER_PITCH = 40
OUTER_ROW = 8


def _inner_body(u_ref, c_ref, ex_ref, ey_ref, out_ref, surf_ref, e_ref, ce_ref, u1_ref):
    m = pl.program_id(0)
    planes = u_ref.shape[1]
    half = planes // 2
    pitch = INNER_PITCH

    @pl.when(m == 0)
    def _():
        _fill(ce_ref, pitch, [(lambda r, c: c_ref[r, c], 8 * i, 8, 8 * i, 1) for i in range(planes // 8)])

    _fill(e_ref, pitch, [(lambda r, c: u_ref[0, r, c], 8 * i, 8, 8 * i, 1) for i in range(planes // 8)])
    out = out_ref.reshape(DEPTH * half, LANES)

    def put(v, i, value):
        out[pl.ds(v * half + i, 8, stride=2), :] = value

    tops = _two_steps(
        m, e_ref, ce_ref, u1_ref, ex_ref, ey_ref, surf_ref, pitch, (4, 3, 1), (8, 2, 1), False, put
    )
    surf = surf_ref.reshape(half, LANES)
    for i in range(2):
        surf[pl.ds(i, 8, stride=2), :] = tops[i]


def _outer_body(
    u_ref, c_ref, lo_ref, hi_ref, clo_ref, chi_ref, ex_ref, ey_ref, out_ref, surf_ref, e_ref, ce_ref, u1_ref
):
    m = pl.program_id(0)
    planes = u_ref.shape[1]
    half = planes // 2
    pitch = OUTER_PITCH

    def pieces(main, low, high):
        row = OUTER_ROW
        return [
            (low, 0, 2, row, 2),
            (main, 0, 8, row + 4, 2),
            (main, 8, 2, row + 20, 2),
            (main, planes - 10, 2, row + 1, 2),
            (main, planes - 8, 8, row + 5, 2),
            (high, 0, 2, row + 21, 2),
        ]

    @pl.when(m == 0)
    def _():
        _fill(
            ce_ref,
            pitch,
            pieces(lambda r, c: c_ref[r, c], lambda r, c: clo_ref[0, r, c], lambda r, c: chi_ref[0, r, c]),
        )

    _fill(
        e_ref,
        pitch,
        pieces(lambda r, c: u_ref[0, r, c], lambda r, c: lo_ref[0, r, c], lambda r, c: hi_ref[0, r, c]),
    )
    out = out_ref.reshape(DEPTH * half, LANES)

    def put(v, i, value):
        out[pl.ds(pl.multiple_of(v * half + 8 * i, 8), 8), :] = value

    tops = _two_steps(
        m, e_ref, ce_ref, u1_ref, ex_ref, ey_ref, surf_ref, pitch,
        (OUTER_ROW, 3, 2), (OUTER_ROW + 4, 2, 2), True, put,
    )
    for i in range(2):
        surf_ref[0, pl.ds(8 * i, 8), :] = tops[i]


def _forecast_call(body, name, pitch, operands, specs, ex, ey, members, planes, blocks, halves):
    scratch = pltpu.VMEM(((DEPTH + 1) * pitch, LANES), jnp.float32)
    return pl.pallas_call(
        body,
        grid=(members,),
        in_specs=specs
        + [
            pl.BlockSpec((1, STEPS, pitch, LANES), lambda m: (m, 0, 0, 0)),
            pl.BlockSpec((1, STEPS, DEPTH, LANES), lambda m: (m, 0, 0, 0)),
        ],
        out_specs=[
            pl.BlockSpec((blocks, 1, halves, planes // 2, LANES), lambda m: (0, m, 0, 0, 0)),
            pl.BlockSpec((1, planes // 2, LANES), lambda m: (m, 0, 0)),
        ],
        out_shape=[
            jax.ShapeDtypeStruct((blocks, members, halves, planes // 2, LANES), jnp.float32),
            jax.ShapeDtypeStruct((members, planes // 2, LANES), jnp.float32),
        ],
        scratch_shapes=[scratch, scratch, scratch],
        compiler_params=pltpu.CompilerParams(
            dimension_semantics=("arbitrary",), vmem_limit_bytes=VMEM_BYTES
        ),
        cost_estimate=pl.CostEstimate(flops=100_000_000, bytes_accessed=7_000_000, transcendentals=0),
        name=name,
    )(*operands, ex, ey)


def forecast_inner(u, cond, ex, ey, blocks):
    members, planes, columns = u.shape
    specs = [
        pl.BlockSpec((1, planes, columns), lambda m: (m, 0, 0)),
        pl.BlockSpec((planes, columns), lambda m: (0, 0)),
    ]
    return _forecast_call(
        _inner_body, "inner", INNER_PITCH, (u, cond), specs, ex, ey, members, planes, blocks, columns // blocks // LANES
    )


def forecast_outer(u, cond, low, high, ex, ey, blocks):
    members, planes, columns = u.shape
    edge = lambda at: pl.BlockSpec((1, 2, columns), at)
    specs = [
        pl.BlockSpec((1, planes, columns), lambda m: (m, 0, 0)),
        pl.BlockSpec((planes, columns), lambda m: (0, 0)),
        edge(lambda m: (m, 0, 0)),
        edge(lambda m: (m, 0, 0)),
        edge(lambda m: (members, 0, 0)),
        edge(lambda m: (members, 0, 0)),
    ]
    operands = (u, cond, low, high, low, high)
    return _forecast_call(
        _outer_body, "outer", OUTER_PITCH, operands, specs, ex, ey, members, planes, blocks, columns // blocks // LANES
    )


def _nt(a, b):
    return lax.dot_general(
        a, b, (((1,), (1,)), ((), ())), precision=lax.Precision.HIGHEST, preferred_element_type=jnp.float32
    )


def _cell_sums_body(pc_ref, obs_ref, var_ref, out_ref):
    planes = pc_ref.shape[0]
    cell = lax.broadcasted_iota(jnp.int32, (planes, LANES), 1)
    weight = 1.0 / var_ref[...]
    value = weight * obs_ref[...]
    pc = pc_ref[...]
    wsum = jnp.zeros((planes, LANES), jnp.float32)
    rsum = jnp.zeros((planes, LANES), jnp.float32)
    for j in range(pc.shape[1]):
        hit = pc[:, j : j + 1] == cell
        wsum = wsum + jnp.where(hit, weight[:, j : j + 1], 0.0)
        rsum = rsum + jnp.where(hit, value[:, j : j + 1], 0.0)
    tiles = [8 * i for i in range(planes // 8)]
    inner, outer = tiles[1:-1], [tiles[0], tiles[-1]]
    for part, (one, two) in enumerate((inner, outer)):
        out_ref[part] = (
            wsum[one : one + 8]
            + _roll(rsum[one : one + 8], 64, 1)
            + _roll(wsum[two : two + 8], 32, 1)
            + _roll(rsum[two : two + 8], 96, 1)
        )


def cell_sums(pixel_cell, observed, obs_var):
    return pl.pallas_call(
        _cell_sums_body,
        out_shape=jax.ShapeDtypeStruct((2, 8, LANES), jnp.float32),
        cost_estimate=pl.CostEstimate(flops=400_000, bytes_accessed=100_000, transcendentals=0),
        compiler_params=pltpu.CompilerParams(vmem_limit_bytes=VMEM_BYTES),
        name="cell_sums",
    )(pixel_cell, observed, obs_var)


def _gram_body(members, planes, seen_ref, out_ref, s_ref):
    sources = seen_ref.shape[0]
    count = sources * members
    group = lax.broadcasted_iota(jnp.int32, (8, LANES), 1) // 4
    sums = [jnp.zeros((8, LANES), jnp.float32) for _ in range(4)]
    for i in range(sources):
        row = seen_ref[i, pl.ds(members * planes, 8), :]
        for g in range(4):
            sums[g] = jnp.where(group == (i + 8 * g) % sources, row, sums[g])
        s_ref[pl.ds(i * members * planes, members * planes), :] = seen_ref[i, pl.ds(0, members * planes), :]
    w_one, w_two, r_one, r_two = (
        _roll(sums[g], (LANES - 32 * g) % LANES, 1) if g else sums[g] for g in range(4)
    )
    wsums = [w_one, w_two]
    rsums = [r_one, r_two]
    gram = jnp.zeros((count, count), jnp.float32)
    proj = jnp.zeros((8, count), jnp.float32)
    for x in range(planes):
        s = s_ref[pl.ds(x, count, stride=planes), :]
        wsum = wsums[x // 8][x % 8 : x % 8 + 1]
        rsum = rsums[x // 8][x % 8 : x % 8 + 1]
        mean = jnp.sum(s, axis=0, keepdims=True) * (1.0 / count)
        anom = s - mean
        gram = gram + _nt(anom * wsum, anom)
        proj = proj + _nt(jnp.broadcast_to(rsum - wsum * mean, (8, LANES)), anom)
    out_ref[pl.ds(0, count), :] = gram
    out_ref[pl.ds(count, 8), :] = proj


def gram_part(seen, members, planes):
    count = seen.shape[0] * members
    return pl.pallas_call(
        functools.partial(_gram_body, members, planes),
        out_shape=jax.ShapeDtypeStruct((count + 8, count), jnp.float32),
        scratch_shapes=[pltpu.VMEM((count * planes, LANES), jnp.float32)],
        cost_estimate=pl.CostEstimate(flops=80_000_000, bytes_accessed=1_700_000, transcendentals=0),
        compiler_params=pltpu.CompilerParams(vmem_limit_bytes=VMEM_BYTES),
        name="gram",
    )(seen)


GROUP = 4


def _mix_body(p0_ref, p1_ref, p2_ref, p3_ref, hi_ref, lo_ref, a_ref):
    count = hi_ref.shape[0]

    def total(rows):
        return (p0_ref[rows, :] + p1_ref[rows, :]) + (p2_ref[rows, :] + p3_ref[rows, :])

    proj = total(pl.ds(count, 8))
    ntile = count // 8
    sub = lax.broadcasted_iota(jnp.int32, (8, LANES), 0)
    lane = lax.broadcasted_iota(jnp.int32, (8, LANES), 1)
    a, inv, diag = [], [], []
    for i in range(ntile):
        eye = (lane == sub + 8 * i).astype(jnp.float32)
        a.append(eye + total(pl.ds(8 * i, 8)) * (1.0 / (count - 1)))
        inv.append(eye)
        diag.append(jnp.ones((8, LANES), jnp.float32))

    def row_of(tile, r):
        return jnp.broadcast_to(tile[r : r + 1, :], (8, LANES))

    for j0 in range(0, count, GROUP):
        base = j0 // 8
        cols = [
            {i: jnp.broadcast_to(a[i][:, j0 + t : j0 + t + 1], (8, LANES)) for i in range(base, ntile)}
            for t in range(GROUP)
        ]
        r0 = j0 % 8
        arow = [row_of(a[base], r0 + t) for t in range(GROUP)]
        irow = [row_of(inv[base], r0 + t) for t in range(GROUP)]
        for t in range(GROUP):
            pivot = row_of(cols[t][base], r0 + t)
            recip = 1.0 / pivot
            diag[base] = jnp.where(sub == r0 + t, pivot, diag[base])
            for s in range(t + 1, GROUP):
                factor = row_of(cols[t][base], r0 + s) * recip
                for i in range(base, ntile):
                    cols[s][i] = cols[s][i] - factor * cols[t][i]
                arow[s] = arow[s] - factor * arow[t]
                irow[s] = irow[s] - factor * irow[t]
            arow[t] = arow[t] * recip
            irow[t] = irow[t] * recip
            cols[t][base] = jnp.where(sub > r0 + t, cols[t][base], 0.0)
        for i in range(base, ntile):
            for t in range(GROUP):
                a[i] = a[i] - cols[t][i] * arow[t]
                inv[i] = inv[i] - cols[t][i] * irow[t]
    for i in range(ntile):
        a_ref[pl.ds(8 * i, 8), :] = inv[i] / jnp.sqrt(diag[i])
    linv = a_ref[...]
    middle = _nt(proj, linv)
    wmean = lax.dot_general(
        middle, linv, (((1,), (0,)), ((), ())), precision=lax.Precision.HIGHEST, preferred_element_type=jnp.float32
    ) * (1.0 / (count - 1))
    mix = linv + wmean[0:1]
    mix = mix + (1.0 - jnp.sum(mix, axis=1, keepdims=True)) * (1.0 / count)
    hi = mix.astype(jnp.bfloat16)
    hi_ref[...] = hi
    lo_ref[...] = (mix - hi.astype(jnp.float32)).astype(jnp.bfloat16)


def mix_matrices(parts):
    count = parts[0].shape[1]
    shape = jax.ShapeDtypeStruct((count, count), jnp.bfloat16)
    return pl.pallas_call(
        _mix_body,
        out_shape=[shape, shape],
        scratch_shapes=[pltpu.VMEM((count, LANES), jnp.float32)],
        cost_estimate=pl.CostEstimate(flops=200_000_000, bytes_accessed=600_000, transcendentals=0),
        compiler_params=pltpu.CompilerParams(vmem_limit_bytes=VMEM_BYTES),
        name="mix",
    )(*parts)


def _transform_body(f_ref, hi_ref, lo_ref, out_ref):
    count = hi_ref.shape[0]
    hi = hi_ref[...]
    lo = lo_ref[...]
    src = f_ref.reshape(count * 8, LANES)
    dst = out_ref.reshape(count * 8, LANES)
    for x in range(8):
        rows = pl.ds(x, count, stride=8)
        f = src[rows, :]
        fhi = f.astype(jnp.bfloat16)
        flo = (f - fhi.astype(jnp.float32)).astype(jnp.bfloat16)
        out = jnp.dot(hi, fhi, preferred_element_type=jnp.float32)
        out = out + jnp.dot(hi, flo, preferred_element_type=jnp.float32)
        out = out + jnp.dot(lo, fhi, preferred_element_type=jnp.float32)
        dst[rows, :] = out


def _transform_more(f_ref, hi_ref, lo_ref, _, out_ref):
    _transform_body(f_ref, hi_ref, lo_ref, out_ref)


def transform(block, hi, lo, onto=None):
    count, halves, planes, _ = block.shape
    tiles = planes // 8
    mat = pl.BlockSpec((count, count), lambda x, c: (0, 0))
    in_specs = [pl.BlockSpec((count, 1, 8, LANES), lambda x, c: (0, c, x, 0)), mat, mat]
    operands = (block, hi, lo)
    if onto is None:
        out_map = lambda x, c: (0, x + 1, c)
    else:
        out_map = lambda x, c: (0, x * (tiles + 1), c)
        in_specs.append(pl.BlockSpec(memory_space=pl.ANY))
        operands += (onto,)
    return pl.pallas_call(
        _transform_body if onto is None else _transform_more,
        grid=(tiles, halves),
        in_specs=in_specs,
        out_specs=pl.BlockSpec((count, 8, LANES), out_map),
        out_shape=jax.ShapeDtypeStruct((count, 2 * planes, halves * LANES), jnp.float32),
        input_output_aliases={} if onto is None else {3: 0},
        compiler_params=pltpu.CompilerParams(
            dimension_semantics=("arbitrary", "arbitrary"), vmem_limit_bytes=VMEM_BYTES
        ),
        cost_estimate=pl.CostEstimate(flops=450_000_000, bytes_accessed=4_300_000, transcendentals=0),
        name="transform",
    )(*operands)


def heat_in_x(laser_x, xs):
    dx = (xs[None, None, :] - laser_x[:, :, None]).astype(jnp.float32)
    ex = (step_dt * laser_power) * jnp.exp(-(dx * dx) / beam_spot_width)
    return jnp.broadcast_to(ex[..., None], ex.shape + (LANES,))


def heat_in_y(laser_y):
    lane = jnp.arange(LANES, dtype=jnp.int32)
    ys = jnp.arange(DEPTH, dtype=jnp.int32)[:, None] + (lane // DEPTH * DEPTH)[None, :]
    dy = (ys - laser_y[:, :, None, None]).astype(jnp.float32)
    return jnp.where(lane % DEPTH == DEPTH - 1, jnp.exp(-(dy * dy) / beam_spot_width), 0.0)


def inner_planes(first):
    return first + jnp.arange(INNER_PITCH, dtype=jnp.int32)


def outer_planes(first, planes):
    row = jnp.arange(OUTER_PITCH, dtype=jnp.int32) - OUTER_ROW
    return first + row // 2 - 2 + (row % 2) * (planes - 8)


def per_device(initial_heat_matrix, conductivity, laser_x, laser_y, pixel_cell, observed, obs_var):
    members, planes, columns = initial_heat_matrix.shape
    blocks = 1
    for axis in MA:
        blocks *= lax.axis_size(axis)
    slabs = lax.axis_size("sa")
    first = lax.axis_index("sa") * planes
    u = initial_heat_matrix
    forward = [(i, i + 1) for i in range(slabs - 1)]
    backward = [(b, a) for a, b in forward]
    top = jnp.concatenate([u[:, planes - 2 :], conductivity[None, planes - 2 :]], axis=0)
    bottom = jnp.concatenate([u[:, :2], conductivity[None, :2]], axis=0)
    low = lax.ppermute(top, "sa", forward)
    high = lax.ppermute(bottom, "sa", backward)
    ey = heat_in_y(laser_y)
    sent_in, surf_in = forecast_inner(u, conductivity, heat_in_x(laser_x, inner_planes(first)), ey, blocks)
    sent_in, low, high = lax.optimization_barrier((sent_in, low, high))
    held_in = lax.all_to_all(sent_in, MA, 0, 0, tiled=True)
    ex = heat_in_x(laser_x, outer_planes(first, planes))
    sent_out, surf_out = forecast_outer(u, conductivity, low, high, ex, ey, blocks)

    sums = cell_sums(pixel_cell, observed, obs_var)
    rows = jnp.concatenate([jnp.stack([surf_in, surf_out]).reshape(2, members * planes // 2, LANES), sums], axis=1)
    rows = jnp.broadcast_to(rows[None], (blocks // 2,) + rows.shape).reshape((blocks,) + rows.shape[1:])
    rows, held_in = lax.optimization_barrier((rows, held_in))
    seen = lax.all_to_all(rows, MA, 0, 0, tiled=True)
    part = gram_part(seen, members, planes // 2)
    part = part + lax.ppermute(part, "ma_2", [(0, 1), (1, 0)])
    parts = [part] + [
        lax.ppermute(part, "sa", [(i, (i + s) % slabs) for i in range(slabs)]) for s in range(1, slabs)
    ]
    hi, lo = mix_matrices(parts)

    held_out = lax.all_to_all(sent_out, MA, 0, 0, tiled=True)
    shape = (blocks * members,) + held_in.shape[2:]
    done = transform(held_in.reshape(shape), hi, lo)
    done = transform(held_out.reshape(shape), hi, lo, done)
    back = lax.all_to_all(done.reshape((blocks, members) + done.shape[1:]), MA, 0, 0, tiled=True)
    return back.transpose(1, 2, 0, 3).reshape(members, planes, columns)


def solution(mesh):
    torus = Mesh(mesh.devices.reshape(4, 4, 2, mesh.shape["sa"]), ("ma_0", "ma_1", "ma_2", "sa"))
    in_specs = (
        P(MA, "sa", None),
        P("sa", None),
        P(MA, None),
        P(MA, None),
        P("sa", MA),
        P("sa", MA),
        P("sa", MA),
    )
    out_specs = P(MA, "sa", None)
    return jax.shard_map(
        per_device, mesh=torus, in_specs=in_specs, out_specs=out_specs, check_vma=False
    )
```

```python
import functools

import jax
import jax.numpy as jnp
from jax import lax
from jax.experimental import pallas as pl
from jax.experimental.pallas import tpu as pltpu
from jax.sharding import Mesh
from jax.sharding import PartitionSpec as P

DEPTH = 64
STEPS = 2
LANES = 128
VMEM_BYTES = 60 << 20
MA = ("ma_0", "ma_1", "ma_2")
MA_SA = ("ma_0", "ma_1", "ma_2", "sa")

step_dt = 0.025
alpha_cond = 0.05
laser_power = 12.0
beam_spot_width = 18.0

def _roll(x, shift, axis):
    return pltpu.roll(x, shift, axis)


def _wide_pair(a, b, low_half):
    return jnp.where(low_half, a, _roll(b, DEPTH, 1)), jnp.where(low_half, _roll(a, DEPTH, 1), b)


UNROLL = {2: 8, 3: 8}
FILL_UNROLL = 16


def _stencil_step(src, cond, pitch, base, tiles, apart, exs, ey_at, emit, surface):
    lane = lax.broadcasted_iota(jnp.int32, (8, LANES), 1)
    low_half = lane < DEPTH
    zpos = lane & (DEPTH - 1)
    z_last = zpos == DEPTH - 1
    z_first = zpos == 0
    unroll = UNROLL[tiles]

    def load(y, i):
        at = pl.ds(y * pitch + (base + i), 8, stride=tiles)
        u = src[at, :]
        c = cond[at, :]
        return u, c + c * (alpha_cond * (u * u))

    def face(one, two):
        return (one[1] + two[1]) * (two[0] - one[0])

    here = [load(0, i) for i in range(tiles)]
    fys = []
    for i in range(tiles):
        u, k = load(DEPTH - 1, i)
        before = (
            jnp.where(low_half, 0.0, _roll(u, DEPTH, 1)),
            jnp.where(low_half, 0.0, _roll(k, DEPTH, 1)),
        )
        fys.append(face(before, here[i]))

    def one(y, here, fys):
        after = [load(y + 1, i) for i in range(tiles)]
        line = {i: here[i] for i in range(tiles)}
        for i in range(-apart, tiles + apart):
            if i not in line and (i + apart in range(tiles) or i - apart in range(tiles)):
                line[i] = load(y, i)
        fx = {i: face(line[i], line[i + apart]) for i in range(-apart, tiles) if i in line}
        ey = jnp.broadcast_to(ey_at(y), (8, LANES))
        new_fys, values = [], []
        for i in range(tiles):
            u, k = here[i]
            fy = face(here[i], after[i])
            new_fys.append(fy)
            acc = (fy - fys[i]) + (fx[i] - fx[i - apart])
            up = jnp.where(z_last, 0.0, _roll(u, LANES - 1, 1))
            kp = jnp.where(z_last, 0.0, _roll(k, LANES - 1, 1))
            fz = (k + kp) * (up - u)
            acc = acc + (fz - jnp.where(z_first, k * u, _roll(fz, 1, 1)))
            values.append(u + (0.5 * step_dt) * acc + exs[i] * ey)
        return after, new_fys, values

    def several(a, carry):
        here, fys, tops = carry
        rows = []
        for q in range(unroll):
            here, fys, even = one(2 * (a * unroll + q), here, fys)
            here, fys, odd = one(2 * (a * unroll + q) + 1, here, fys)
            emit(a * unroll + q, even, odd)
            rows += [even, odd]
        if surface:
            kept = []
            for i in range(tiles):
                acc = _roll(tops[i], (LANES - len(rows)) % LANES, 1)
                for q, values in enumerate(rows):
                    shift = (LANES - (len(rows) - 1 - q)) % LANES
                    moved = _roll(values[i], shift, 1) if shift else values[i]
                    acc = jnp.where(zpos == DEPTH - len(rows) + q, moved, acc)
                kept.append(acc)
            tops = kept
        return here, fys, tops

    tops = [jnp.zeros((8, LANES), jnp.float32) for _ in range(tiles)] if surface else []
    return lax.fori_loop(0, DEPTH // 2 // unroll, several, (here, fys, tops))[2]


def _close(ref, pitch):
    lane = lax.broadcasted_iota(jnp.int32, (8, LANES), 1)
    for r in range(0, pitch, 8):
        first = ref[pl.ds(r, 8), :]
        ref[pl.ds(DEPTH * pitch + r, 8), :] = jnp.where(lane < DEPTH, _roll(first, DEPTH, 1), 0.0)


def _fill(ref, pitch, pieces):
    half = DEPTH // 2
    lane = lax.broadcasted_iota(jnp.int32, (8, LANES), 1)
    low_half = lane < DEPTH

    def several(b, carry):
        for q in range(FILL_UNROLL):
            a = b * FILL_UNROLL + q
            ca = pl.ds(pl.multiple_of(a * LANES, LANES), LANES)
            cb = pl.ds(pl.multiple_of((a + half) * LANES, LANES), LANES)
            for read, start, size, row, stride in pieces:
                even, odd = _wide_pair(read(pl.ds(start, size), ca), read(pl.ds(start, size), cb), low_half[:size])
                ref[pl.ds(2 * a * pitch + row, size, stride=stride), :] = even
                ref[pl.ds((2 * a + 1) * pitch + row, size, stride=stride), :] = odd
        return carry

    lax.fori_loop(0, half // FILL_UNROLL, several, 0)
    _close(ref, pitch)


def _two_steps(m, members, laser_ref, e_ref, ce_ref, u1_ref, ey_ref, pitch, plane_at, step1, step2, edged, put):
    sub = lax.broadcasted_iota(jnp.int32, (8, LANES), 0)
    lane = lax.broadcasted_iota(jnp.int32, (8, LANES), 1)
    last_layer = (lane & (DEPTH - 1)) == DEPTH - 1
    for t in range(STEPS):
        for g in range(0, DEPTH, 8):
            y = sub + g + jnp.where(lane < DEPTH, 0, DEPTH)
            dy = (y - laser_ref[members + m, t]).astype(jnp.float32)
            ey_ref[t, pl.ds(g, 8), :] = jnp.where(last_layer, jnp.exp(-(dy * dy) / beam_spot_width), 0.0)

    def ey_row(t):
        return lambda y: ey_ref[t, pl.ds(y, 1), :]

    def factors(t, base, tiles):
        found = []
        for i in range(tiles):
            dx = (plane_at(base + i + tiles * sub) - laser_ref[m, t]).astype(jnp.float32)
            found.append((step_dt * laser_power) * jnp.exp(-(dx * dx) / beam_spot_width))
        return found

    base, tiles, apart = step1

    def emit1(a, even, odd):
        for p, values in ((0, even), (1, odd)):
            for i, value in enumerate(values):
                at = pl.ds((2 * a + p) * pitch + base + i, 8, stride=tiles)
                u1_ref[at, :] = jnp.where(ce_ref[at, :] > 0.0, value, 0.0) if edged else value

    _stencil_step(e_ref, ce_ref, pitch, base, tiles, apart, factors(0, base, tiles), ey_row(0), emit1, False)
    _close(u1_ref, pitch)
    base, count, apart = step2
    low_half = lax.broadcasted_iota(jnp.int32, (8, LANES), 1) < DEPTH

    def emit2(a, even, odd):
        for i in range(count):
            one, two = _wide_pair(even[i], odd[i], low_half)
            put(a, i, one)
            put(a + DEPTH // 2, i, two)

    tops = _stencil_step(u1_ref, ce_ref, pitch, base, count, apart, factors(1, base, count), ey_row(1), emit2, True)
    return tops


INNER_PITCH = 32
OUTER_PITCH = 40
OUTER_ROW = 8


def _inner_body(laser_ref, u_ref, c_ref, out_ref, surf_ref, e_ref, ce_ref, u1_ref, ey_ref):
    m = pl.program_id(0)
    planes = u_ref.shape[1]
    half = planes // 2
    pitch = INNER_PITCH

    @pl.when(m == 0)
    def _():
        _fill(ce_ref, pitch, [(lambda r, c: c_ref[r, c], 8 * i, 8, 8 * i, 1) for i in range(planes // 8)])

    _fill(e_ref, pitch, [(lambda r, c: u_ref[0, r, c], 8 * i, 8, 8 * i, 1) for i in range(planes // 8)])
    out = out_ref.reshape(DEPTH * half, LANES)

    def put(v, i, value):
        out[pl.ds(v * half + i, 8, stride=2), :] = value

    tops = _two_steps(
        m, pl.num_programs(0), laser_ref, e_ref, ce_ref, u1_ref, ey_ref, pitch,
        lambda row: laser_ref[laser_ref.shape[0] - 1, 0] + row, (4, 3, 1), (8, 2, 1), False, put,
    )
    surf = surf_ref.reshape(half, LANES)
    for i in range(2):
        surf[pl.ds(i, 8, stride=2), :] = tops[i]


def _outer_body(
    laser_ref, u_ref, c_ref, lo_ref, hi_ref, clo_ref, chi_ref, out_ref, surf_ref, e_ref, ce_ref, u1_ref,
    ey_ref,
):
    m = pl.program_id(0)
    planes = u_ref.shape[1]
    half = planes // 2
    pitch = OUTER_PITCH

    def pieces(main, low, high):
        row = OUTER_ROW
        return [
            (low, 0, 2, row, 2),
            (main, 0, 8, row + 4, 2),
            (main, 8, 2, row + 20, 2),
            (main, planes - 10, 2, row + 1, 2),
            (main, planes - 8, 8, row + 5, 2),
            (high, 0, 2, row + 21, 2),
        ]

    @pl.when(m == 0)
    def _():
        _fill(
            ce_ref,
            pitch,
            pieces(lambda r, c: c_ref[r, c], lambda r, c: clo_ref[0, r, c], lambda r, c: chi_ref[0, r, c]),
        )

    _fill(
        e_ref,
        pitch,
        pieces(lambda r, c: u_ref[0, r, c], lambda r, c: lo_ref[0, r, c], lambda r, c: hi_ref[0, r, c]),
    )
    out = out_ref.reshape(DEPTH * half, LANES)

    def put(v, i, value):
        out[pl.ds(pl.multiple_of(v * half + 8 * i, 8), 8), :] = value

    def plane_at(row):
        return laser_ref[laser_ref.shape[0] - 1, 0] + ((row - OUTER_ROW) >> 1) - 2 + (row & 1) * (planes - 8)

    tops = _two_steps(
        m, pl.num_programs(0), laser_ref, e_ref, ce_ref, u1_ref, ey_ref, pitch, plane_at,
        (OUTER_ROW, 3, 2), (OUTER_ROW + 4, 2, 2), True, put,
    )
    for i in range(2):
        surf_ref[0, pl.ds(8 * i, 8), :] = tops[i]


def _forecast_call(body, name, pitch, lasers, operands, specs, shape, blocks):
    members, planes, columns = shape
    halves = columns // blocks // LANES
    scratch = pltpu.VMEM(((DEPTH + 1) * pitch, LANES), jnp.float32)
    return pl.pallas_call(
        body,
        grid=(members,),
        in_specs=[pl.BlockSpec(memory_space=pltpu.SMEM)] + specs,
        out_specs=[
            pl.BlockSpec((blocks, 1, halves, planes // 2, LANES), lambda m: (0, m, 0, 0, 0)),
            pl.BlockSpec((1, planes // 2, LANES), lambda m: (m, 0, 0)),
        ],
        out_shape=[
            jax.ShapeDtypeStruct((blocks, members, halves, planes // 2, LANES), jnp.float32),
            jax.ShapeDtypeStruct((members, planes // 2, LANES), jnp.float32),
        ],
        scratch_shapes=[scratch, scratch, scratch, pltpu.VMEM((STEPS, DEPTH, LANES), jnp.float32)],
        compiler_params=pltpu.CompilerParams(
            dimension_semantics=("arbitrary",), vmem_limit_bytes=VMEM_BYTES
        ),
        cost_estimate=pl.CostEstimate(flops=100_000_000, bytes_accessed=7_000_000, transcendentals=0),
        name=name,
    )(lasers, *operands)


def forecast_inner(lasers, u, cond, blocks):
    members, planes, columns = u.shape
    specs = [
        pl.BlockSpec((1, planes, columns), lambda m: (m, 0, 0)),
        pl.BlockSpec((planes, columns), lambda m: (0, 0)),
    ]
    return _forecast_call(_inner_body, "inner", INNER_PITCH, lasers, (u, cond), specs, u.shape, blocks)


def forecast_outer(lasers, u, cond, low, high, blocks):
    members, planes, columns = u.shape
    edge = lambda at: pl.BlockSpec((1, 2, columns), at)
    specs = [
        pl.BlockSpec((1, planes, columns), lambda m: (m, 0, 0)),
        pl.BlockSpec((planes, columns), lambda m: (0, 0)),
        edge(lambda m: (m, 0, 0)),
        edge(lambda m: (m, 0, 0)),
        edge(lambda m: (members, 0, 0)),
        edge(lambda m: (members, 0, 0)),
    ]
    operands = (u, cond, low, high, low, high)
    return _forecast_call(_outer_body, "outer", OUTER_PITCH, lasers, operands, specs, u.shape, blocks)


def _nt(a, b):
    return lax.dot_general(
        a, b, (((1,), (1,)), ((), ())), precision=lax.Precision.HIGHEST, preferred_element_type=jnp.float32
    )


def _cell_sums_body(pc_ref, obs_ref, var_ref, out_ref):
    planes = pc_ref.shape[0]
    cell = lax.broadcasted_iota(jnp.int32, (planes, LANES), 1)
    weight = 1.0 / var_ref[...]
    value = weight * obs_ref[...]
    pc = pc_ref[...]
    wsum = jnp.zeros((planes, LANES), jnp.float32)
    rsum = jnp.zeros((planes, LANES), jnp.float32)
    for j in range(pc.shape[1]):
        hit = pc[:, j : j + 1] == cell
        wsum = wsum + jnp.where(hit, weight[:, j : j + 1], 0.0)
        rsum = rsum + jnp.where(hit, value[:, j : j + 1], 0.0)
    tiles = [8 * i for i in range(planes // 8)]
    inner, outer = tiles[1:-1], [tiles[0], tiles[-1]]
    for part, (one, two) in enumerate((inner, outer)):
        out_ref[part] = (
            wsum[one : one + 8]
            + _roll(rsum[one : one + 8], 64, 1)
            + _roll(wsum[two : two + 8], 32, 1)
            + _roll(rsum[two : two + 8], 96, 1)
        )


def cell_sums(pixel_cell, observed, obs_var):
    return pl.pallas_call(
        _cell_sums_body,
        out_shape=jax.ShapeDtypeStruct((2, 8, LANES), jnp.float32),
        cost_estimate=pl.CostEstimate(flops=400_000, bytes_accessed=100_000, transcendentals=0),
        compiler_params=pltpu.CompilerParams(vmem_limit_bytes=VMEM_BYTES),
        name="cell_sums",
    )(pixel_cell, observed, obs_var)


def _gram_body(members, planes, seen_ref, out_ref, s_ref):
    sources = seen_ref.shape[0]
    count = sources * members
    group = lax.broadcasted_iota(jnp.int32, (8, LANES), 1) // 4
    sums = [jnp.zeros((8, LANES), jnp.float32) for _ in range(4)]
    for i in range(sources):
        row = seen_ref[i, pl.ds(members * planes, 8), :]
        for g in range(4):
            sums[g] = jnp.where(group == (i + 8 * g) % sources, row, sums[g])
        s_ref[pl.ds(i * members * planes, members * planes), :] = seen_ref[i, pl.ds(0, members * planes), :]
    w_one, w_two, r_one, r_two = (
        _roll(sums[g], (LANES - 32 * g) % LANES, 1) if g else sums[g] for g in range(4)
    )
    wsums = [w_one, w_two]
    rsums = [r_one, r_two]
    both = jnp.zeros((count + 8, count), jnp.float32)
    for x0 in range(0, planes, 2):
        left, right = [], []
        for x in (x0, x0 + 1):
            s = s_ref[pl.ds(x, count, stride=planes), :]
            wsum = wsums[x // 8][x % 8 : x % 8 + 1]
            rsum = rsums[x // 8][x % 8 : x % 8 + 1]
            mean = jnp.sum(s, axis=0, keepdims=True) * (1.0 / count)
            anom = s - mean
            q = jnp.broadcast_to(rsum - wsum * mean, (8, LANES))
            left.append(jnp.concatenate([anom * wsum, q], axis=0))
            right.append(anom)
        both = both + _nt(jnp.concatenate(left, axis=1), jnp.concatenate(right, axis=1))
    out_ref[...] = both


def gram_part(seen, members, planes):
    count = seen.shape[0] * members
    return pl.pallas_call(
        functools.partial(_gram_body, members, planes),
        out_shape=jax.ShapeDtypeStruct((count + 8, count), jnp.float32),
        scratch_shapes=[pltpu.VMEM((count * planes, LANES), jnp.float32)],
        cost_estimate=pl.CostEstimate(flops=80_000_000, bytes_accessed=1_700_000, transcendentals=0),
        compiler_params=pltpu.CompilerParams(vmem_limit_bytes=VMEM_BYTES),
        name="gram",
    )(seen)


GROUP = 8


def _mix_body(p0_ref, p1_ref, p2_ref, p3_ref, hi_ref, lo_ref, a_ref):
    count = hi_ref.shape[0]

    def total(rows):
        return (p0_ref[rows, :] + p1_ref[rows, :]) + (p2_ref[rows, :] + p3_ref[rows, :])

    proj = total(pl.ds(count, 8))
    ntile = count // 8
    sub = lax.broadcasted_iota(jnp.int32, (8, LANES), 0)
    lane = lax.broadcasted_iota(jnp.int32, (8, LANES), 1)
    a, inv, diag = [], [], []
    for i in range(ntile):
        eye = (lane == sub + 8 * i).astype(jnp.float32)
        a.append(eye + total(pl.ds(8 * i, 8)) * (1.0 / (count - 1)))
        inv.append(eye)
        diag.append(jnp.ones((8, LANES), jnp.float32))

    def row_of(tile, r):
        return jnp.broadcast_to(tile[r : r + 1, :], (8, LANES))

    for j0 in range(0, count, GROUP):
        base = j0 // 8
        cols = [
            {i: jnp.broadcast_to(a[i][:, j0 + t : j0 + t + 1], (8, LANES)) for i in range(base, ntile)}
            for t in range(GROUP)
        ]
        r0 = j0 % 8
        arow = [row_of(a[base], r0 + t) for t in range(GROUP)]
        irow = [row_of(inv[base], r0 + t) for t in range(GROUP)]
        for t in range(GROUP):
            pivot = row_of(cols[t][base], r0 + t)
            recip = 1.0 / pivot
            diag[base] = jnp.where(sub == r0 + t, pivot, diag[base])
            for s in range(t + 1, GROUP):
                factor = row_of(cols[t][base], r0 + s) * recip
                for i in range(base, ntile):
                    cols[s][i] = cols[s][i] - factor * cols[t][i]
                arow[s] = arow[s] - factor * arow[t]
                irow[s] = irow[s] - factor * irow[t]
            arow[t] = arow[t] * recip
            irow[t] = irow[t] * recip
            cols[t][base] = jnp.where(sub > r0 + t, cols[t][base], 0.0)
        for i in range(base, ntile):
            for t in range(GROUP):
                a[i] = a[i] - cols[t][i] * arow[t]
                inv[i] = inv[i] - cols[t][i] * irow[t]
    for i in range(ntile):
        a_ref[pl.ds(8 * i, 8), :] = inv[i] / jnp.sqrt(diag[i])
    linv = a_ref[...]
    middle = _nt(proj, linv)
    wmean = lax.dot_general(
        middle, linv, (((1,), (0,)), ((), ())), precision=lax.Precision.HIGHEST, preferred_element_type=jnp.float32
    ) * (1.0 / (count - 1))
    mix = linv + wmean[0:1]
    mix = mix + (1.0 - jnp.sum(mix, axis=1, keepdims=True)) * (1.0 / count)
    hi = mix.astype(jnp.bfloat16)
    hi_ref[...] = hi
    lo_ref[...] = (mix - hi.astype(jnp.float32)).astype(jnp.bfloat16)


def mix_matrices(parts):
    count = parts[0].shape[1]
    shape = jax.ShapeDtypeStruct((count, count), jnp.bfloat16)
    return pl.pallas_call(
        _mix_body,
        out_shape=[shape, shape],
        scratch_shapes=[pltpu.VMEM((count, LANES), jnp.float32)],
        cost_estimate=pl.CostEstimate(flops=200_000_000, bytes_accessed=600_000, transcendentals=0),
        compiler_params=pltpu.CompilerParams(vmem_limit_bytes=VMEM_BYTES),
        name="mix",
    )(*parts)


def _transform_body(f_ref, hi_ref, lo_ref, out_ref):
    count = hi_ref.shape[0]
    hi = hi_ref[...]
    lo = lo_ref[...]
    src = f_ref.reshape(count * 8, LANES)
    dst = out_ref.reshape(count * 8, LANES)
    wide = jnp.concatenate([hi, hi], axis=1)
    for x in range(0, 8, 2):
        f = jnp.concatenate([src[pl.ds(x + i, count, stride=8), :] for i in range(2)], axis=1)
        fhi = f.astype(jnp.bfloat16)
        flo = (f - fhi.astype(jnp.float32)).astype(jnp.bfloat16)
        out = jnp.dot(wide, jnp.concatenate([fhi, flo], axis=0), preferred_element_type=jnp.float32)
        out = out + jnp.dot(lo, fhi, preferred_element_type=jnp.float32)
        for i in range(2):
            dst[pl.ds(x + i, count, stride=8), :] = out[:, i * LANES : (i + 1) * LANES]


def _transform_more(f_ref, hi_ref, lo_ref, _, out_ref):
    _transform_body(f_ref, hi_ref, lo_ref, out_ref)


def transform(block, hi, lo, onto=None):
    count, halves, planes, _ = block.shape
    tiles = planes // 8
    mat = pl.BlockSpec((count, count), lambda x, c: (0, 0))
    in_specs = [pl.BlockSpec((count, 1, 8, LANES), lambda x, c: (0, c, x, 0)), mat, mat]
    operands = (block, hi, lo)
    if onto is None:
        out_map = lambda x, c: (0, x + 1, c)
    else:
        out_map = lambda x, c: (0, x * (tiles + 1), c)
        in_specs.append(pl.BlockSpec(memory_space=pl.ANY))
        operands += (onto,)
    return pl.pallas_call(
        _transform_body if onto is None else _transform_more,
        grid=(tiles, halves),
        in_specs=in_specs,
        out_specs=pl.BlockSpec((count, 8, LANES), out_map),
        out_shape=jax.ShapeDtypeStruct((count, 2 * planes, halves * LANES), jnp.float32),
        input_output_aliases={} if onto is None else {3: 0},
        compiler_params=pltpu.CompilerParams(
            dimension_semantics=("arbitrary", "arbitrary"), vmem_limit_bytes=VMEM_BYTES
        ),
        cost_estimate=pl.CostEstimate(flops=450_000_000, bytes_accessed=4_300_000, transcendentals=0),
        name="transform",
    )(*operands)


def per_device(initial_heat_matrix, conductivity, laser_x, laser_y, pixel_cell, observed, obs_var):
    members, planes, columns = initial_heat_matrix.shape
    blocks = 1
    for axis in MA:
        blocks *= lax.axis_size(axis)
    slabs = lax.axis_size("sa")
    first = lax.axis_index("sa") * planes
    u = initial_heat_matrix
    forward = [(i, i + 1) for i in range(slabs - 1)]
    backward = [(b, a) for a, b in forward]
    top = jnp.concatenate([u[:, planes - 2 :], conductivity[None, planes - 2 :]], axis=0)
    bottom = jnp.concatenate([u[:, :2], conductivity[None, :2]], axis=0)
    low = lax.ppermute(top, "sa", forward)
    high = lax.ppermute(bottom, "sa", backward)
    lasers = jnp.concatenate([laser_x, laser_y, jnp.broadcast_to(first, (1, STEPS))], axis=0)
    sent_in, surf_in = forecast_inner(lasers, u, conductivity, blocks)
    sent_in, low, high = lax.optimization_barrier((sent_in, low, high))
    held_in = lax.all_to_all(sent_in, MA, 0, 0, tiled=True)
    sent_out, surf_out = forecast_outer(lasers, u, conductivity, low, high, blocks)

    sums = cell_sums(pixel_cell, observed, obs_var)
    rows = jnp.concatenate([jnp.stack([surf_in, surf_out]).reshape(2, members * planes // 2, LANES), sums], axis=1)
    rows = jnp.broadcast_to(rows[None], (blocks // 2,) + rows.shape).reshape((blocks,) + rows.shape[1:])
    rows, held_in = lax.optimization_barrier((rows, held_in))
    seen = lax.all_to_all(rows, MA, 0, 0, tiled=True)
    part = gram_part(seen, members, planes // 2)
    part = part + lax.ppermute(part, "ma_2", [(0, 1), (1, 0)])
    parts = [part] + [
        lax.ppermute(part, "sa", [(i, (i + s) % slabs) for i in range(slabs)]) for s in range(1, slabs)
    ]
    hi, lo = mix_matrices(parts)

    held_out = lax.all_to_all(sent_out, MA, 0, 0, tiled=True)
    shape = (blocks * members,) + held_in.shape[2:]
    done = transform(held_in.reshape(shape), hi, lo)
    done = transform(held_out.reshape(shape), hi, lo, done)
    back = lax.all_to_all(done.reshape((blocks, members) + done.shape[1:]), MA, 0, 0, tiled=True)
    return back.transpose(1, 2, 0, 3).reshape(members, planes, columns)


def solution(mesh):
    torus = Mesh(mesh.devices.reshape(4, 4, 2, mesh.shape["sa"]), ("ma_0", "ma_1", "ma_2", "sa"))
    in_specs = (
        P(MA, "sa", None),
        P("sa", None),
        P(MA, None),
        P(MA, None),
        P("sa", MA),
        P("sa", MA),
        P("sa", MA),
    )
    out_specs = P(MA, "sa", None)
    return jax.shard_map(
        per_device, mesh=torus, in_specs=in_specs, out_specs=out_specs, check_vma=False
    )
```

```python
import functools

import jax
import jax.numpy as jnp
from jax import lax
from jax.experimental import pallas as pl
from jax.experimental.pallas import tpu as pltpu
from jax.sharding import Mesh
from jax.sharding import PartitionSpec as P

DEPTH = 64
STEPS = 2
LANES = 128
VMEM_BYTES = 60 << 20
MA = ("ma_0", "ma_1", "ma_2")
MA_SA = ("ma_0", "ma_1", "ma_2", "sa")

step_dt = 0.025
alpha_cond = 0.05
laser_power = 12.0
beam_spot_width = 18.0

def _roll(x, shift, axis):
    return pltpu.roll(x, shift, axis)


def _wide_pair(a, b, low_half):
    return jnp.where(low_half, a, _roll(b, DEPTH, 1)), jnp.where(low_half, _roll(a, DEPTH, 1), b)


UNROLL = {2: 8, 3: 8}
FILL_UNROLL = 16


def _stencil_step(src, cond, pitch, base, tiles, apart, exs, ey_at, emit, surface):
    lane = lax.broadcasted_iota(jnp.int32, (8, LANES), 1)
    low_half = lane < DEPTH
    zpos = lane & (DEPTH - 1)
    z_last = zpos == DEPTH - 1
    z_first = zpos == 0
    unroll = UNROLL[tiles]

    def load(y, i):
        at = pl.ds(y * pitch + (base + i), 8, stride=tiles)
        u = src[at, :]
        c = cond[at, :]
        return u, c + c * (alpha_cond * (u * u))

    def face(one, two):
        return (one[1] + two[1]) * (two[0] - one[0])

    here = [load(0, i) for i in range(tiles)]
    fys = []
    for i in range(tiles):
        u, k = load(DEPTH - 1, i)
        before = (
            jnp.where(low_half, 0.0, _roll(u, DEPTH, 1)),
            jnp.where(low_half, 0.0, _roll(k, DEPTH, 1)),
        )
        fys.append(face(before, here[i]))

    def one(y, here, fys):
        after = [load(y + 1, i) for i in range(tiles)]
        line = {i: here[i] for i in range(tiles)}
        for i in range(-apart, tiles + apart):
            if i not in line and (i + apart in range(tiles) or i - apart in range(tiles)):
                line[i] = load(y, i)
        fx = {i: face(line[i], line[i + apart]) for i in range(-apart, tiles) if i in line}
        ey = jnp.broadcast_to(ey_at(y), (8, LANES))
        new_fys, values = [], []
        for i in range(tiles):
            u, k = here[i]
            fy = face(here[i], after[i])
            new_fys.append(fy)
            acc = (fy - fys[i]) + (fx[i] - fx[i - apart])
            up = jnp.where(z_last, 0.0, _roll(u, LANES - 1, 1))
            kp = jnp.where(z_last, 0.0, _roll(k, LANES - 1, 1))
            fz = (k + kp) * (up - u)
            acc = acc + (fz - jnp.where(z_first, k * u, _roll(fz, 1, 1)))
            values.append(u + (0.5 * step_dt) * acc + exs[i] * ey)
        return after, new_fys, values

    def several(a, carry):
        here, fys, tops = carry
        rows = []
        for q in range(unroll):
            here, fys, even = one(2 * (a * unroll + q), here, fys)
            here, fys, odd = one(2 * (a * unroll + q) + 1, here, fys)
            emit(a * unroll + q, even, odd)
            rows += [even, odd]
        if surface:
            kept = []
            for i in range(tiles):
                acc = _roll(tops[i], (LANES - len(rows)) % LANES, 1)
                for q, values in enumerate(rows):
                    shift = (LANES - (len(rows) - 1 - q)) % LANES
                    moved = _roll(values[i], shift, 1) if shift else values[i]
                    acc = jnp.where(zpos == DEPTH - len(rows) + q, moved, acc)
                kept.append(acc)
            tops = kept
        return here, fys, tops

    tops = [jnp.zeros((8, LANES), jnp.float32) for _ in range(tiles)] if surface else []
    return lax.fori_loop(0, DEPTH // 2 // unroll, several, (here, fys, tops))[2]


def _close(ref, pitch):
    lane = lax.broadcasted_iota(jnp.int32, (8, LANES), 1)
    for r in range(0, pitch, 8):
        first = ref[pl.ds(r, 8), :]
        ref[pl.ds(DEPTH * pitch + r, 8), :] = jnp.where(lane < DEPTH, _roll(first, DEPTH, 1), 0.0)


def _fill(ref, pitch, pieces):
    half = DEPTH // 2
    lane = lax.broadcasted_iota(jnp.int32, (8, LANES), 1)
    low_half = lane < DEPTH

    def several(b, carry):
        for q in range(FILL_UNROLL):
            a = b * FILL_UNROLL + q
            ca = pl.ds(pl.multiple_of(a * LANES, LANES), LANES)
            cb = pl.ds(pl.multiple_of((a + half) * LANES, LANES), LANES)
            for read, start, size, row, stride in pieces:
                even, odd = _wide_pair(read(pl.ds(start, size), ca), read(pl.ds(start, size), cb), low_half[:size])
                ref[pl.ds(2 * a * pitch + row, size, stride=stride), :] = even
                ref[pl.ds((2 * a + 1) * pitch + row, size, stride=stride), :] = odd
        return carry

    lax.fori_loop(0, half // FILL_UNROLL, several, 0)
    _close(ref, pitch)


def _two_steps(m, members, laser_ref, e_ref, ce_ref, u1_ref, ey_ref, pitch, plane_at, step1, step2, edged, put):
    sub = lax.broadcasted_iota(jnp.int32, (8, LANES), 0)
    lane = lax.broadcasted_iota(jnp.int32, (8, LANES), 1)
    last_layer = (lane & (DEPTH - 1)) == DEPTH - 1
    for t in range(STEPS):
        for g in range(0, DEPTH, 8):
            y = sub + g + jnp.where(lane < DEPTH, 0, DEPTH)
            dy = (y - laser_ref[members + m, t]).astype(jnp.float32)
            ey_ref[t, pl.ds(g, 8), :] = jnp.where(last_layer, jnp.exp(-(dy * dy) / beam_spot_width), 0.0)

    def ey_row(t):
        return lambda y: ey_ref[t, pl.ds(y, 1), :]

    def factors(t, base, tiles):
        found = []
        for i in range(tiles):
            dx = (plane_at(base + i + tiles * sub) - laser_ref[m, t]).astype(jnp.float32)
            found.append((step_dt * laser_power) * jnp.exp(-(dx * dx) / beam_spot_width))
        return found

    base, tiles, apart = step1

    def emit1(a, even, odd):
        for p, values in ((0, even), (1, odd)):
            for i, value in enumerate(values):
                at = pl.ds((2 * a + p) * pitch + base + i, 8, stride=tiles)
                u1_ref[at, :] = jnp.where(ce_ref[at, :] > 0.0, value, 0.0) if edged else value

    _stencil_step(e_ref, ce_ref, pitch, base, tiles, apart, factors(0, base, tiles), ey_row(0), emit1, False)
    _close(u1_ref, pitch)
    base, count, apart = step2
    low_half = lax.broadcasted_iota(jnp.int32, (8, LANES), 1) < DEPTH

    def emit2(a, even, odd):
        for i in range(count):
            one, two = _wide_pair(even[i], odd[i], low_half)
            put(a, i, one)
            put(a + DEPTH // 2, i, two)

    tops = _stencil_step(u1_ref, ce_ref, pitch, base, count, apart, factors(1, base, count), ey_row(1), emit2, True)
    return tops


INNER_PITCH = 32
OUTER_PITCH = 40
OUTER_ROW = 8


def _inner_body(
    laser_ref, u_ref, c_ref, out_ref, surf_ref, bottom_ref, top_ref, e_ref, ce_ref, u1_ref, ey_ref
):
    m = pl.program_id(0)
    planes = u_ref.shape[1]
    half = planes // 2
    pitch = INNER_PITCH

    @pl.when(m == 0)
    def _():
        _fill(ce_ref, pitch, [(lambda r, c: c_ref[r, c], 8 * i, 8, 8 * i, 1) for i in range(planes // 8)])
        bottom_ref[bottom_ref.shape[0] - 1] = c_ref[pl.ds(0, 2), :]
        top_ref[top_ref.shape[0] - 1] = c_ref[pl.ds(planes - 2, 2), :]

    bottom_ref[m] = u_ref[0, pl.ds(0, 2), :]
    top_ref[m] = u_ref[0, pl.ds(planes - 2, 2), :]
    _fill(e_ref, pitch, [(lambda r, c: u_ref[0, r, c], 8 * i, 8, 8 * i, 1) for i in range(planes // 8)])
    out = out_ref.reshape(DEPTH * half, LANES)

    def put(v, i, value):
        out[pl.ds(v * half + i, 8, stride=2), :] = value

    tops = _two_steps(
        m, pl.num_programs(0), laser_ref, e_ref, ce_ref, u1_ref, ey_ref, pitch,
        lambda row: laser_ref[laser_ref.shape[0] - 1, 0] + row, (4, 3, 1), (8, 2, 1), False, put,
    )
    surf = surf_ref.reshape(half, LANES)
    for i in range(2):
        surf[pl.ds(i, 8, stride=2), :] = tops[i]


def _outer_body(
    laser_ref, u_ref, c_ref, lo_ref, hi_ref, clo_ref, chi_ref, out_ref, surf_ref, e_ref, ce_ref, u1_ref,
    ey_ref,
):
    m = pl.program_id(0)
    planes = u_ref.shape[1]
    half = planes // 2
    pitch = OUTER_PITCH

    def pieces(main, low, high):
        row = OUTER_ROW
        return [
            (low, 0, 2, row, 2),
            (main, 0, 8, row + 4, 2),
            (main, 8, 2, row + 20, 2),
            (main, planes - 10, 2, row + 1, 2),
            (main, planes - 8, 8, row + 5, 2),
            (high, 0, 2, row + 21, 2),
        ]

    @pl.when(m == 0)
    def _():
        _fill(
            ce_ref,
            pitch,
            pieces(lambda r, c: c_ref[r, c], lambda r, c: clo_ref[0, r, c], lambda r, c: chi_ref[0, r, c]),
        )

    _fill(
        e_ref,
        pitch,
        pieces(lambda r, c: u_ref[0, r, c], lambda r, c: lo_ref[0, r, c], lambda r, c: hi_ref[0, r, c]),
    )
    out = out_ref.reshape(DEPTH * half, LANES)

    def put(v, i, value):
        out[pl.ds(pl.multiple_of(v * half + 8 * i, 8), 8), :] = value

    def plane_at(row):
        return laser_ref[laser_ref.shape[0] - 1, 0] + ((row - OUTER_ROW) >> 1) - 2 + (row & 1) * (planes - 8)

    tops = _two_steps(
        m, pl.num_programs(0), laser_ref, e_ref, ce_ref, u1_ref, ey_ref, pitch, plane_at,
        (OUTER_ROW, 3, 2), (OUTER_ROW + 4, 2, 2), True, put,
    )
    for i in range(2):
        surf_ref[0, pl.ds(8 * i, 8), :] = tops[i]


def _forecast_call(body, name, pitch, lasers, operands, specs, shape, blocks, edges=False):
    members, planes, columns = shape
    halves = columns // blocks // LANES
    scratch = pltpu.VMEM(((DEPTH + 1) * pitch, LANES), jnp.float32)
    edge_spec = [pl.BlockSpec((members + 1, 2, columns), lambda m: (0, 0, 0))] * 2 if edges else []
    edge_shape = [jax.ShapeDtypeStruct((members + 1, 2, columns), jnp.float32)] * 2 if edges else []
    return pl.pallas_call(
        body,
        grid=(members,),
        in_specs=[pl.BlockSpec(memory_space=pltpu.SMEM)] + specs,
        out_specs=[
            pl.BlockSpec((blocks, 1, halves, planes // 2, LANES), lambda m: (0, m, 0, 0, 0)),
            pl.BlockSpec((1, planes // 2, LANES), lambda m: (m, 0, 0)),
        ]
        + edge_spec,
        out_shape=[
            jax.ShapeDtypeStruct((blocks, members, halves, planes // 2, LANES), jnp.float32),
            jax.ShapeDtypeStruct((members, planes // 2, LANES), jnp.float32),
        ]
        + edge_shape,
        scratch_shapes=[scratch, scratch, scratch, pltpu.VMEM((STEPS, DEPTH, LANES), jnp.float32)],
        compiler_params=pltpu.CompilerParams(
            dimension_semantics=("arbitrary",), vmem_limit_bytes=VMEM_BYTES
        ),
        cost_estimate=pl.CostEstimate(flops=100_000_000, bytes_accessed=7_000_000, transcendentals=0),
        name=name,
    )(lasers, *operands)


def forecast_inner(lasers, u, cond, blocks):
    members, planes, columns = u.shape
    specs = [
        pl.BlockSpec((1, planes, columns), lambda m: (m, 0, 0)),
        pl.BlockSpec((planes, columns), lambda m: (0, 0)),
    ]
    return _forecast_call(_inner_body, "inner", INNER_PITCH, lasers, (u, cond), specs, u.shape, blocks, True)


def forecast_outer(lasers, u, cond, low, high, blocks):
    members, planes, columns = u.shape
    edge = lambda at: pl.BlockSpec((1, 2, columns), at)
    specs = [
        pl.BlockSpec((1, planes, columns), lambda m: (m, 0, 0)),
        pl.BlockSpec((planes, columns), lambda m: (0, 0)),
        edge(lambda m: (m, 0, 0)),
        edge(lambda m: (m, 0, 0)),
        edge(lambda m: (members, 0, 0)),
        edge(lambda m: (members, 0, 0)),
    ]
    operands = (u, cond, low, high, low, high)
    return _forecast_call(_outer_body, "outer", OUTER_PITCH, lasers, operands, specs, u.shape, blocks)


def _nt(a, b):
    return lax.dot_general(
        a, b, (((1,), (1,)), ((), ())), precision=lax.Precision.HIGHEST, preferred_element_type=jnp.float32
    )


def _cell_sums_body(pc_ref, obs_ref, var_ref, out_ref):
    planes = pc_ref.shape[0]
    cell = lax.broadcasted_iota(jnp.int32, (planes, LANES), 1)
    weight = 1.0 / var_ref[...]
    value = weight * obs_ref[...]
    pc = pc_ref[...]
    wsum = jnp.zeros((planes, LANES), jnp.float32)
    rsum = jnp.zeros((planes, LANES), jnp.float32)
    for j in range(pc.shape[1]):
        hit = pc[:, j : j + 1] == cell
        wsum = wsum + jnp.where(hit, weight[:, j : j + 1], 0.0)
        rsum = rsum + jnp.where(hit, value[:, j : j + 1], 0.0)
    tiles = [8 * i for i in range(planes // 8)]
    inner, outer = tiles[1:-1], [tiles[0], tiles[-1]]
    for part, (one, two) in enumerate((inner, outer)):
        out_ref[part] = (
            wsum[one : one + 8]
            + _roll(rsum[one : one + 8], 64, 1)
            + _roll(wsum[two : two + 8], 32, 1)
            + _roll(rsum[two : two + 8], 96, 1)
        )


def cell_sums(pixel_cell, observed, obs_var):
    return pl.pallas_call(
        _cell_sums_body,
        out_shape=jax.ShapeDtypeStruct((2, 8, LANES), jnp.float32),
        cost_estimate=pl.CostEstimate(flops=400_000, bytes_accessed=100_000, transcendentals=0),
        compiler_params=pltpu.CompilerParams(vmem_limit_bytes=VMEM_BYTES),
        name="cell_sums",
    )(pixel_cell, observed, obs_var)


def _gram_body(members, planes, seen_ref, out_ref, s_ref):
    sources = seen_ref.shape[0]
    count = sources * members
    group = lax.broadcasted_iota(jnp.int32, (8, LANES), 1) // 4
    sums = [jnp.zeros((8, LANES), jnp.float32) for _ in range(4)]
    for i in range(sources):
        row = seen_ref[i, pl.ds(members * planes, 8), :]
        for g in range(4):
            sums[g] = jnp.where(group == (i + 8 * g) % sources, row, sums[g])
        s_ref[pl.ds(i * members * planes, members * planes), :] = seen_ref[i, pl.ds(0, members * planes), :]
    w_one, w_two, r_one, r_two = (
        _roll(sums[g], (LANES - 32 * g) % LANES, 1) if g else sums[g] for g in range(4)
    )
    wsums = [w_one, w_two]
    rsums = [r_one, r_two]
    both = jnp.zeros((count + 8, count), jnp.float32)
    for x0 in range(0, planes, 2):
        left, right = [], []
        for x in (x0, x0 + 1):
            s = s_ref[pl.ds(x, count, stride=planes), :]
            wsum = wsums[x // 8][x % 8 : x % 8 + 1]
            rsum = rsums[x // 8][x % 8 : x % 8 + 1]
            mean = jnp.sum(s, axis=0, keepdims=True) * (1.0 / count)
            anom = s - mean
            q = jnp.broadcast_to(rsum - wsum * mean, (8, LANES))
            left.append(jnp.concatenate([anom * wsum, q], axis=0))
            right.append(anom)
        both = both + _nt(jnp.concatenate(left, axis=1), jnp.concatenate(right, axis=1))
    out_ref[...] = both


def gram_part(seen, members, planes):
    count = seen.shape[0] * members
    return pl.pallas_call(
        functools.partial(_gram_body, members, planes),
        out_shape=jax.ShapeDtypeStruct((count + 8, count), jnp.float32),
        scratch_shapes=[pltpu.VMEM((count * planes, LANES), jnp.float32)],
        cost_estimate=pl.CostEstimate(flops=80_000_000, bytes_accessed=1_700_000, transcendentals=0),
        compiler_params=pltpu.CompilerParams(vmem_limit_bytes=VMEM_BYTES),
        name="gram",
    )(seen)


GROUP = 8


def _mix_body(p0_ref, p1_ref, p2_ref, p3_ref, hi_ref, lo_ref, a_ref):
    count = hi_ref.shape[0]

    def total(rows):
        return (p0_ref[rows, :] + p1_ref[rows, :]) + (p2_ref[rows, :] + p3_ref[rows, :])

    proj = total(pl.ds(count, 8))
    ntile = count // 8
    sub = lax.broadcasted_iota(jnp.int32, (8, LANES), 0)
    lane = lax.broadcasted_iota(jnp.int32, (8, LANES), 1)
    a, inv, diag = [], [], []
    for i in range(ntile):
        eye = (lane == sub + 8 * i).astype(jnp.float32)
        a.append(eye + total(pl.ds(8 * i, 8)) * (1.0 / (count - 1)))
        inv.append(eye)
        diag.append(jnp.ones((8, LANES), jnp.float32))

    def row_of(tile, r):
        return jnp.broadcast_to(tile[r : r + 1, :], (8, LANES))

    for j0 in range(0, count, GROUP):
        base = j0 // 8
        cols = [
            {i: jnp.broadcast_to(a[i][:, j0 + t : j0 + t + 1], (8, LANES)) for i in range(base, ntile)}
            for t in range(GROUP)
        ]
        r0 = j0 % 8
        arow = [row_of(a[base], r0 + t) for t in range(GROUP)]
        irow = [row_of(inv[base], r0 + t) for t in range(GROUP)]
        for t in range(GROUP):
            pivot = row_of(cols[t][base], r0 + t)
            recip = 1.0 / pivot
            diag[base] = jnp.where(sub == r0 + t, pivot, diag[base])
            for s in range(t + 1, GROUP):
                factor = row_of(cols[t][base], r0 + s) * recip
                for i in range(base, ntile):
                    cols[s][i] = cols[s][i] - factor * cols[t][i]
                arow[s] = arow[s] - factor * arow[t]
                irow[s] = irow[s] - factor * irow[t]
            arow[t] = arow[t] * recip
            irow[t] = irow[t] * recip
            cols[t][base] = jnp.where(sub > r0 + t, cols[t][base], 0.0)
        for i in range(base, ntile):
            for t in range(GROUP):
                a[i] = a[i] - cols[t][i] * arow[t]
                inv[i] = inv[i] - cols[t][i] * irow[t]
    for i in range(ntile):
        a_ref[pl.ds(8 * i, 8), :] = inv[i] / jnp.sqrt(diag[i])
    linv = a_ref[...]
    middle = _nt(proj, linv)
    wmean = lax.dot_general(
        middle, linv, (((1,), (0,)), ((), ())), precision=lax.Precision.HIGHEST, preferred_element_type=jnp.float32
    ) * (1.0 / (count - 1))
    mix = linv + wmean[0:1]
    mix = mix + (1.0 - jnp.sum(mix, axis=1, keepdims=True)) * (1.0 / count)
    hi = mix.astype(jnp.bfloat16)
    hi_ref[...] = hi
    lo_ref[...] = (mix - hi.astype(jnp.float32)).astype(jnp.bfloat16)


def mix_matrices(parts):
    count = parts[0].shape[1]
    shape = jax.ShapeDtypeStruct((count, count), jnp.bfloat16)
    return pl.pallas_call(
        _mix_body,
        out_shape=[shape, shape],
        scratch_shapes=[pltpu.VMEM((count, LANES), jnp.float32)],
        cost_estimate=pl.CostEstimate(flops=200_000_000, bytes_accessed=600_000, transcendentals=0),
        compiler_params=pltpu.CompilerParams(vmem_limit_bytes=VMEM_BYTES),
        name="mix",
    )(*parts)


def _transform_body(f_ref, hi_ref, lo_ref, out_ref):
    count = hi_ref.shape[0]
    hi = hi_ref[...]
    lo = lo_ref[...]
    src = f_ref.reshape(count * 8, LANES)
    dst = out_ref.reshape(count * 8, LANES)
    wide = jnp.concatenate([hi, hi], axis=1)
    for x in range(0, 8, 2):
        f = jnp.concatenate([src[pl.ds(x + i, count, stride=8), :] for i in range(2)], axis=1)
        fhi = f.astype(jnp.bfloat16)
        flo = (f - fhi.astype(jnp.float32)).astype(jnp.bfloat16)
        out = jnp.dot(wide, jnp.concatenate([fhi, flo], axis=0), preferred_element_type=jnp.float32)
        out = out + jnp.dot(lo, fhi, preferred_element_type=jnp.float32)
        for i in range(2):
            dst[pl.ds(x + i, count, stride=8), :] = out[:, i * LANES : (i + 1) * LANES]


def _transform_more(f_ref, hi_ref, lo_ref, _, out_ref):
    _transform_body(f_ref, hi_ref, lo_ref, out_ref)


def transform(block, hi, lo, onto=None):
    count, halves, planes, _ = block.shape
    tiles = planes // 8
    mat = pl.BlockSpec((count, count), lambda x, c: (0, 0))
    in_specs = [pl.BlockSpec((count, 1, 8, LANES), lambda x, c: (0, c, x, 0)), mat, mat]
    operands = (block, hi, lo)
    if onto is None:
        out_map = lambda x, c: (0, x + 1, c)
    else:
        out_map = lambda x, c: (0, x * (tiles + 1), c)
        in_specs.append(pl.BlockSpec(memory_space=pl.ANY))
        operands += (onto,)
    return pl.pallas_call(
        _transform_body if onto is None else _transform_more,
        grid=(tiles, halves),
        in_specs=in_specs,
        out_specs=pl.BlockSpec((count, 8, LANES), out_map),
        out_shape=jax.ShapeDtypeStruct((count, 2 * planes, halves * LANES), jnp.float32),
        input_output_aliases={} if onto is None else {3: 0},
        compiler_params=pltpu.CompilerParams(
            dimension_semantics=("arbitrary", "arbitrary"), vmem_limit_bytes=VMEM_BYTES
        ),
        cost_estimate=pl.CostEstimate(flops=450_000_000, bytes_accessed=4_300_000, transcendentals=0),
        name="transform",
    )(*operands)


def per_device(initial_heat_matrix, conductivity, laser_x, laser_y, pixel_cell, observed, obs_var):
    members, planes, columns = initial_heat_matrix.shape
    blocks = 1
    for axis in MA:
        blocks *= lax.axis_size(axis)
    slabs = lax.axis_size("sa")
    first = lax.axis_index("sa") * planes
    u = initial_heat_matrix
    forward = [(i, i + 1) for i in range(slabs - 1)]
    backward = [(b, a) for a, b in forward]
    lasers = jnp.concatenate([laser_x, laser_y, jnp.broadcast_to(first, (1, STEPS))], axis=0)
    sent_in, surf_in, bottom, top = forecast_inner(lasers, u, conductivity, blocks)
    low = lax.ppermute(top, "sa", forward)
    high = lax.ppermute(bottom, "sa", backward)
    held_in = lax.all_to_all(sent_in, MA, 0, 0, tiled=True)
    sent_out, surf_out = forecast_outer(lasers, u, conductivity, low, high, blocks)

    sums = cell_sums(pixel_cell, observed, obs_var)
    rows = jnp.concatenate([jnp.stack([surf_in, surf_out]).reshape(2, members * planes // 2, LANES), sums], axis=1)
    rows = jnp.broadcast_to(rows[None], (blocks // 2,) + rows.shape).reshape((blocks,) + rows.shape[1:])
    rows, held_in = lax.optimization_barrier((rows, held_in))
    seen = lax.all_to_all(rows, MA, 0, 0, tiled=True)
    part = gram_part(seen, members, planes // 2)
    part = part + lax.ppermute(part, "ma_2", [(0, 1), (1, 0)])
    parts = [part] + [
        lax.ppermute(part, "sa", [(i, (i + s) % slabs) for i in range(slabs)]) for s in range(1, slabs)
    ]
    hi, lo = mix_matrices(parts)

    held_out = lax.all_to_all(sent_out, MA, 0, 0, tiled=True)
    shape = (blocks * members,) + held_in.shape[2:]
    done = transform(held_in.reshape(shape), hi, lo)
    done = transform(held_out.reshape(shape), hi, lo, done)
    back = lax.all_to_all(done.reshape((blocks, members) + done.shape[1:]), MA, 0, 0, tiled=True)
    return back.transpose(1, 2, 0, 3).reshape(members, planes, columns)


def solution(mesh):
    torus = Mesh(mesh.devices.reshape(4, 4, 2, mesh.shape["sa"]), ("ma_0", "ma_1", "ma_2", "sa"))
    in_specs = (
        P(MA, "sa", None),
        P("sa", None),
        P(MA, None),
        P(MA, None),
        P("sa", MA),
        P("sa", MA),
        P("sa", MA),
    )
    out_specs = P(MA, "sa", None)
    return jax.shard_map(
        per_device, mesh=torus, in_specs=in_specs, out_specs=out_specs, check_vma=False
    )
```

```python
import functools

import jax
import jax.numpy as jnp
from jax import lax
from jax.experimental import pallas as pl
from jax.experimental.pallas import tpu as pltpu
from jax.sharding import Mesh
from jax.sharding import PartitionSpec as P

DEPTH = 64
STEPS = 2
LANES = 128
VMEM_BYTES = 60 << 20
MA = ("ma_0", "ma_1", "ma_2")
MA_SA = ("ma_0", "ma_1", "ma_2", "sa")

step_dt = 0.025
alpha_cond = 0.05
laser_power = 12.0
beam_spot_width = 18.0

def _roll(x, shift, axis):
    return pltpu.roll(x, shift, axis)


def _wide_pair(a, b, low_half):
    return jnp.where(low_half, a, _roll(b, DEPTH, 1)), jnp.where(low_half, _roll(a, DEPTH, 1), b)


UNROLL = {2: 8, 3: 8}
FILL_UNROLL = 16


def _stencil_step(src, cond, pitch, base, tiles, apart, exs, ey_at, emit, surface):
    lane = lax.broadcasted_iota(jnp.int32, (8, LANES), 1)
    low_half = lane < DEPTH
    zpos = lane & (DEPTH - 1)
    z_last = zpos == DEPTH - 1
    z_first = zpos == 0
    unroll = UNROLL[tiles]

    def load(y, i):
        at = pl.ds(y * pitch + (base + i), 8, stride=tiles)
        u = src[at, :]
        c = cond[at, :]
        return u, c + c * (alpha_cond * (u * u))

    def face(one, two):
        return (one[1] + two[1]) * (two[0] - one[0])

    here = [load(0, i) for i in range(tiles)]
    fys = []
    for i in range(tiles):
        u, k = load(DEPTH - 1, i)
        before = (
            jnp.where(low_half, 0.0, _roll(u, DEPTH, 1)),
            jnp.where(low_half, 0.0, _roll(k, DEPTH, 1)),
        )
        fys.append(face(before, here[i]))

    def one(y, here, fys):
        after = [load(y + 1, i) for i in range(tiles)]
        line = {i: here[i] for i in range(tiles)}
        for i in range(-apart, tiles + apart):
            if i not in line and (i + apart in range(tiles) or i - apart in range(tiles)):
                line[i] = load(y, i)
        fx = {i: face(line[i], line[i + apart]) for i in range(-apart, tiles) if i in line}
        ey = jnp.broadcast_to(ey_at(y), (8, LANES))
        new_fys, values = [], []
        for i in range(tiles):
            u, k = here[i]
            fy = face(here[i], after[i])
            new_fys.append(fy)
            acc = (fy - fys[i]) + (fx[i] - fx[i - apart])
            up = jnp.where(z_last, 0.0, _roll(u, LANES - 1, 1))
            kp = jnp.where(z_last, 0.0, _roll(k, LANES - 1, 1))
            fz = (k + kp) * (up - u)
            acc = acc + (fz - jnp.where(z_first, k * u, _roll(fz, 1, 1)))
            values.append(u + (0.5 * step_dt) * acc + exs[i] * ey)
        return after, new_fys, values

    def several(a, carry):
        here, fys, tops = carry
        rows = []
        for q in range(unroll):
            here, fys, even = one(2 * (a * unroll + q), here, fys)
            here, fys, odd = one(2 * (a * unroll + q) + 1, here, fys)
            emit(a * unroll + q, even, odd)
            rows += [even, odd]
        if surface:
            kept = []
            for i in range(tiles):
                acc = _roll(tops[i], (LANES - len(rows)) % LANES, 1)
                for q, values in enumerate(rows):
                    shift = (LANES - (len(rows) - 1 - q)) % LANES
                    moved = _roll(values[i], shift, 1) if shift else values[i]
                    acc = jnp.where(zpos == DEPTH - len(rows) + q, moved, acc)
                kept.append(acc)
            tops = kept
        return here, fys, tops

    tops = [jnp.zeros((8, LANES), jnp.float32) for _ in range(tiles)] if surface else []
    return lax.fori_loop(0, DEPTH // 2 // unroll, several, (here, fys, tops))[2]


def _close(ref, pitch):
    lane = lax.broadcasted_iota(jnp.int32, (8, LANES), 1)
    for r in range(0, pitch, 8):
        first = ref[pl.ds(r, 8), :]
        ref[pl.ds(DEPTH * pitch + r, 8), :] = jnp.where(lane < DEPTH, _roll(first, DEPTH, 1), 0.0)


def _fill(ref, pitch, pieces):
    half = DEPTH // 2
    lane = lax.broadcasted_iota(jnp.int32, (8, LANES), 1)
    low_half = lane < DEPTH

    def several(b, carry):
        for q in range(FILL_UNROLL):
            a = b * FILL_UNROLL + q
            ca = pl.ds(pl.multiple_of(a * LANES, LANES), LANES)
            cb = pl.ds(pl.multiple_of((a + half) * LANES, LANES), LANES)
            for read, start, size, row, stride in pieces:
                even, odd = _wide_pair(read(pl.ds(start, size), ca), read(pl.ds(start, size), cb), low_half[:size])
                ref[pl.ds(2 * a * pitch + row, size, stride=stride), :] = even
                ref[pl.ds((2 * a + 1) * pitch + row, size, stride=stride), :] = odd
        return carry

    lax.fori_loop(0, half // FILL_UNROLL, several, 0)
    _close(ref, pitch)


def _two_steps(m, members, laser_ref, e_ref, ce_ref, u1_ref, ey_ref, pitch, plane_at, step1, step2, edged, put):
    sub = lax.broadcasted_iota(jnp.int32, (8, LANES), 0)
    lane = lax.broadcasted_iota(jnp.int32, (8, LANES), 1)
    last_layer = (lane & (DEPTH - 1)) == DEPTH - 1
    for t in range(STEPS):
        for g in range(0, DEPTH, 8):
            y = sub + g + jnp.where(lane < DEPTH, 0, DEPTH)
            dy = (y - laser_ref[members + m, t]).astype(jnp.float32)
            ey_ref[t, pl.ds(g, 8), :] = jnp.where(last_layer, jnp.exp(-(dy * dy) / beam_spot_width), 0.0)

    def ey_row(t):
        return lambda y: ey_ref[t, pl.ds(y, 1), :]

    def factors(t, base, tiles):
        found = []
        for i in range(tiles):
            dx = (plane_at(base + i + tiles * sub) - laser_ref[m, t]).astype(jnp.float32)
            found.append((step_dt * laser_power) * jnp.exp(-(dx * dx) / beam_spot_width))
        return found

    base, tiles, apart = step1

    def emit1(a, even, odd):
        for p, values in ((0, even), (1, odd)):
            for i, value in enumerate(values):
                at = pl.ds((2 * a + p) * pitch + base + i, 8, stride=tiles)
                u1_ref[at, :] = jnp.where(ce_ref[at, :] > 0.0, value, 0.0) if edged else value

    _stencil_step(e_ref, ce_ref, pitch, base, tiles, apart, factors(0, base, tiles), ey_row(0), emit1, False)
    _close(u1_ref, pitch)
    base, count, apart = step2
    low_half = lax.broadcasted_iota(jnp.int32, (8, LANES), 1) < DEPTH

    def emit2(a, even, odd):
        for i in range(count):
            one, two = _wide_pair(even[i], odd[i], low_half)
            put(a, i, one)
            put(a + DEPTH // 2, i, two)

    tops = _stencil_step(u1_ref, ce_ref, pitch, base, count, apart, factors(1, base, count), ey_row(1), emit2, True)
    return tops


INNER_PITCH = 32
OUTER_PITCH = 40
OUTER_ROW = 8


def _inner_body(
    laser_ref, u_ref, c_ref, out_ref, bottom_ref, top_ref, e_ref, ce_ref, u1_ref, ey_ref, rows_ref
):
    m = pl.program_id(0)
    planes = u_ref.shape[1]
    half = planes // 2
    pitch = INNER_PITCH

    @pl.when(m == 0)
    def _():
        _fill(ce_ref, pitch, [(lambda r, c: c_ref[r, c], 8 * i, 8, 8 * i, 1) for i in range(planes // 8)])
        bottom_ref[bottom_ref.shape[0] - 1] = c_ref[pl.ds(0, 2), :]
        top_ref[top_ref.shape[0] - 1] = c_ref[pl.ds(planes - 2, 2), :]

    bottom_ref[m] = u_ref[0, pl.ds(0, 2), :]
    top_ref[m] = u_ref[0, pl.ds(planes - 2, 2), :]
    _fill(e_ref, pitch, [(lambda r, c: u_ref[0, r, c], 8 * i, 8, 8 * i, 1) for i in range(planes // 8)])
    blocks, _, rows, _ = out_ref.shape
    halves = DEPTH // blocks
    out = out_ref.reshape(blocks * rows, LANES)

    def put(v, i, value):
        row = v * half + lax.div(v, halves) * (rows - halves * half)
        out[pl.ds(row + i, 8, stride=2), :] = value

    tops = _two_steps(
        m, pl.num_programs(0), laser_ref, e_ref, ce_ref, u1_ref, ey_ref, pitch,
        lambda row: laser_ref[laser_ref.shape[0] - 1, 0] + row, (4, 3, 1), (8, 2, 1), False, put,
    )
    for i in range(2):
        rows_ref[pl.ds(i, 8, stride=2), :] = tops[i]
    for d in range(blocks):
        out_ref[d, 0, pl.ds(halves * half, 8), :] = rows_ref[pl.ds(8 * (d % 2), 8), :]


def _outer_body(
    laser_ref, u_ref, c_ref, lo_ref, hi_ref, clo_ref, chi_ref, out_ref, surf_ref, e_ref, ce_ref, u1_ref,
    ey_ref,
):
    m = pl.program_id(0)
    planes = u_ref.shape[1]
    half = planes // 2
    pitch = OUTER_PITCH

    def pieces(main, low, high):
        row = OUTER_ROW
        return [
            (low, 0, 2, row, 2),
            (main, 0, 8, row + 4, 2),
            (main, 8, 2, row + 20, 2),
            (main, planes - 10, 2, row + 1, 2),
            (main, planes - 8, 8, row + 5, 2),
            (high, 0, 2, row + 21, 2),
        ]

    @pl.when(m == 0)
    def _():
        _fill(
            ce_ref,
            pitch,
            pieces(lambda r, c: c_ref[r, c], lambda r, c: clo_ref[0, r, c], lambda r, c: chi_ref[0, r, c]),
        )

    _fill(
        e_ref,
        pitch,
        pieces(lambda r, c: u_ref[0, r, c], lambda r, c: lo_ref[0, r, c], lambda r, c: hi_ref[0, r, c]),
    )
    out = out_ref.reshape(DEPTH * half, LANES)

    def put(v, i, value):
        out[pl.ds(pl.multiple_of(v * half + 8 * i, 8), 8), :] = value

    def plane_at(row):
        return laser_ref[laser_ref.shape[0] - 1, 0] + ((row - OUTER_ROW) >> 1) - 2 + (row & 1) * (planes - 8)

    tops = _two_steps(
        m, pl.num_programs(0), laser_ref, e_ref, ce_ref, u1_ref, ey_ref, pitch, plane_at,
        (OUTER_ROW, 3, 2), (OUTER_ROW + 4, 2, 2), True, put,
    )
    for i in range(2):
        surf_ref[0, pl.ds(8 * i, 8), :] = tops[i]


def _forecast_call(body, name, pitch, lasers, operands, specs, out_specs, out_shape, more_scratch):
    scratch = pltpu.VMEM(((DEPTH + 1) * pitch, LANES), jnp.float32)
    return pl.pallas_call(
        body,
        grid=(operands[0].shape[0],),
        in_specs=[pl.BlockSpec(memory_space=pltpu.SMEM)] + specs,
        out_specs=out_specs,
        out_shape=[jax.ShapeDtypeStruct(shape, jnp.float32) for shape in out_shape],
        scratch_shapes=[scratch, scratch, scratch, pltpu.VMEM((STEPS, DEPTH, LANES), jnp.float32)] + more_scratch,
        compiler_params=pltpu.CompilerParams(
            dimension_semantics=("arbitrary",), vmem_limit_bytes=VMEM_BYTES
        ),
        cost_estimate=pl.CostEstimate(flops=100_000_000, bytes_accessed=7_000_000, transcendentals=0),
        name=name,
    )(lasers, *operands)


def forecast_inner(lasers, u, cond, blocks):
    members, planes, columns = u.shape
    rows = columns // blocks // LANES * (planes // 2) + 8
    edge = (members + 1, 2, columns)
    specs = [
        pl.BlockSpec((1, planes, columns), lambda m: (m, 0, 0)),
        pl.BlockSpec((planes, columns), lambda m: (0, 0)),
    ]
    out_specs = [
        pl.BlockSpec((blocks, 1, rows, LANES), lambda m: (0, m, 0, 0)),
        pl.BlockSpec(edge, lambda m: (0, 0, 0)),
        pl.BlockSpec(edge, lambda m: (0, 0, 0)),
    ]
    return _forecast_call(
        _inner_body, "inner", INNER_PITCH, lasers, (u, cond), specs, out_specs,
        [(blocks, members, rows, LANES), edge, edge], [pltpu.VMEM((planes // 2, LANES), jnp.float32)],
    )


def forecast_outer(lasers, u, cond, low, high, blocks):
    members, planes, columns = u.shape
    halves = columns // blocks // LANES
    edge = lambda at: pl.BlockSpec((1, 2, columns), at)
    specs = [
        pl.BlockSpec((1, planes, columns), lambda m: (m, 0, 0)),
        pl.BlockSpec((planes, columns), lambda m: (0, 0)),
        edge(lambda m: (m, 0, 0)),
        edge(lambda m: (m, 0, 0)),
        edge(lambda m: (members, 0, 0)),
        edge(lambda m: (members, 0, 0)),
    ]
    out_specs = [
        pl.BlockSpec((blocks, 1, halves, planes // 2, LANES), lambda m: (0, m, 0, 0, 0)),
        pl.BlockSpec((1, planes // 2, LANES), lambda m: (m, 0, 0)),
    ]
    return _forecast_call(
        _outer_body, "outer", OUTER_PITCH, lasers, (u, cond, low, high, low, high), specs, out_specs,
        [(blocks, members, halves, planes // 2, LANES), (members, planes // 2, LANES)], [],
    )


def _nt(a, b):
    return lax.dot_general(
        a, b, (((1,), (1,)), ((), ())), precision=lax.Precision.HIGHEST, preferred_element_type=jnp.float32
    )


def _cell_sums_body(pc_ref, obs_ref, var_ref, out_ref):
    planes = pc_ref.shape[0]
    cell = lax.broadcasted_iota(jnp.int32, (planes, LANES), 1)
    weight = 1.0 / var_ref[...]
    value = weight * obs_ref[...]
    pc = pc_ref[...]
    wsum = jnp.zeros((planes, LANES), jnp.float32)
    rsum = jnp.zeros((planes, LANES), jnp.float32)
    for j in range(pc.shape[1]):
        hit = pc[:, j : j + 1] == cell
        wsum = wsum + jnp.where(hit, weight[:, j : j + 1], 0.0)
        rsum = rsum + jnp.where(hit, value[:, j : j + 1], 0.0)
    tiles = [8 * i for i in range(planes // 8)]
    for part, (one, two) in enumerate(((tiles[1], tiles[0]), (tiles[-2], tiles[-1]))):
        out_ref[part] = (
            wsum[one : one + 8]
            + _roll(rsum[one : one + 8], 64, 1)
            + _roll(wsum[two : two + 8], 32, 1)
            + _roll(rsum[two : two + 8], 96, 1)
        )


def cell_sums(pixel_cell, observed, obs_var):
    return pl.pallas_call(
        _cell_sums_body,
        out_shape=jax.ShapeDtypeStruct((2, 8, LANES), jnp.float32),
        cost_estimate=pl.CostEstimate(flops=400_000, bytes_accessed=100_000, transcendentals=0),
        compiler_params=pltpu.CompilerParams(vmem_limit_bytes=VMEM_BYTES),
        name="cell_sums",
    )(pixel_cell, observed, obs_var)


def _gram_body(members, inner_ref, seen_ref, out_ref, s_ref):
    sources = seen_ref.shape[0]
    count = sources * members
    outer = members * 8
    group = lax.broadcasted_iota(jnp.int32, (8, LANES), 1) // 4
    sums = [jnp.zeros((8, LANES), jnp.float32) for _ in range(4)]
    for i in range(sources):
        row = seen_ref[i, pl.ds(outer, 8), :]
        for g in range(4):
            sums[g] = jnp.where(group == (i + 8 * g) % sources, row, sums[g])
        s_ref[pl.ds(i * outer, outer), :] = seen_ref[i, pl.ds(0, outer), :]
    w_in, w_out, r_in, r_out = (
        _roll(sums[g], (LANES - 32 * g) % LANES, 1) if g else sums[g] for g in range(4)
    )
    both = jnp.zeros((count + 8, count), jnp.float32)
    for x in range(8):
        left, right = [], []
        for cells, wsums, rsums in ((inner_ref.reshape(count * 8, LANES), w_in, r_in), (s_ref, w_out, r_out)):
            s = cells[pl.ds(x, count, stride=8), :]
            wsum = wsums[x : x + 1]
            rsum = rsums[x : x + 1]
            mean = jnp.sum(s, axis=0, keepdims=True) * (1.0 / count)
            anom = s - mean
            q = jnp.broadcast_to(rsum - wsum * mean, (8, LANES))
            left.append(jnp.concatenate([anom * wsum, q], axis=0))
            right.append(anom)
        both = both + _nt(jnp.concatenate(left, axis=1), jnp.concatenate(right, axis=1))
    out_ref[...] = both


def gram_part(inner, seen, members):
    count, rows, _ = inner.shape
    last = rows // 8 - 1
    return pl.pallas_call(
        functools.partial(_gram_body, members),
        grid=(1,),
        in_specs=[
            pl.BlockSpec((count, 8, LANES), lambda i: (0, last, 0)),
            pl.BlockSpec(seen.shape, lambda i: (0, 0, 0)),
        ],
        out_specs=pl.BlockSpec((count + 8, count), lambda i: (0, 0)),
        out_shape=jax.ShapeDtypeStruct((count + 8, count), jnp.float32),
        scratch_shapes=[pltpu.VMEM((count * 8, LANES), jnp.float32)],
        cost_estimate=pl.CostEstimate(flops=80_000_000, bytes_accessed=1_700_000, transcendentals=0),
        compiler_params=pltpu.CompilerParams(vmem_limit_bytes=VMEM_BYTES),
        name="gram",
    )(inner, seen)


GROUP = 8


def _mix_body(p0_ref, p1_ref, p2_ref, p3_ref, hi_ref, lo_ref, a_ref):
    count = hi_ref.shape[0]

    def total(rows):
        return (p0_ref[rows, :] + p1_ref[rows, :]) + (p2_ref[rows, :] + p3_ref[rows, :])

    proj = total(pl.ds(count, 8))
    ntile = count // 8
    sub = lax.broadcasted_iota(jnp.int32, (8, LANES), 0)
    lane = lax.broadcasted_iota(jnp.int32, (8, LANES), 1)
    a, inv, diag = [], [], []
    for i in range(ntile):
        eye = (lane == sub + 8 * i).astype(jnp.float32)
        a.append(eye + total(pl.ds(8 * i, 8)) * (1.0 / (count - 1)))
        inv.append(eye)
        diag.append(jnp.ones((8, LANES), jnp.float32))

    def row_of(tile, r):
        return jnp.broadcast_to(tile[r : r + 1, :], (8, LANES))

    for j0 in range(0, count, GROUP):
        base = j0 // 8
        cols = [
            {i: jnp.broadcast_to(a[i][:, j0 + t : j0 + t + 1], (8, LANES)) for i in range(base, ntile)}
            for t in range(GROUP)
        ]
        r0 = j0 % 8
        arow = [row_of(a[base], r0 + t) for t in range(GROUP)]
        irow = [row_of(inv[base], r0 + t) for t in range(GROUP)]
        for t in range(GROUP):
            pivot = row_of(cols[t][base], r0 + t)
            recip = 1.0 / pivot
            diag[base] = jnp.where(sub == r0 + t, pivot, diag[base])
            for s in range(t + 1, GROUP):
                factor = row_of(cols[t][base], r0 + s) * recip
                for i in range(base, ntile):
                    cols[s][i] = cols[s][i] - factor * cols[t][i]
                arow[s] = arow[s] - factor * arow[t]
                irow[s] = irow[s] - factor * irow[t]
            arow[t] = arow[t] * recip
            irow[t] = irow[t] * recip
            cols[t][base] = jnp.where(sub > r0 + t, cols[t][base], 0.0)
        for i in range(base, ntile):
            for t in range(GROUP):
                a[i] = a[i] - cols[t][i] * arow[t]
                inv[i] = inv[i] - cols[t][i] * irow[t]
    for i in range(ntile):
        a_ref[pl.ds(8 * i, 8), :] = inv[i] / jnp.sqrt(diag[i])
    linv = a_ref[...]
    middle = _nt(proj, linv)
    wmean = lax.dot_general(
        middle, linv, (((1,), (0,)), ((), ())), precision=lax.Precision.HIGHEST, preferred_element_type=jnp.float32
    ) * (1.0 / (count - 1))
    mix = linv + wmean[0:1]
    mix = mix + (1.0 - jnp.sum(mix, axis=1, keepdims=True)) * (1.0 / count)
    hi = mix.astype(jnp.bfloat16)
    hi_ref[...] = hi
    lo_ref[...] = (mix - hi.astype(jnp.float32)).astype(jnp.bfloat16)


def mix_matrices(parts):
    count = parts[0].shape[1]
    shape = jax.ShapeDtypeStruct((count, count), jnp.bfloat16)
    return pl.pallas_call(
        _mix_body,
        out_shape=[shape, shape],
        scratch_shapes=[pltpu.VMEM((count, LANES), jnp.float32)],
        cost_estimate=pl.CostEstimate(flops=200_000_000, bytes_accessed=600_000, transcendentals=0),
        compiler_params=pltpu.CompilerParams(vmem_limit_bytes=VMEM_BYTES),
        name="mix",
    )(*parts)


def _transform_body(f_ref, hi_ref, lo_ref, out_ref):
    count = hi_ref.shape[0]
    hi = hi_ref[...]
    lo = lo_ref[...]
    src = f_ref.reshape(count * 8, LANES)
    dst = out_ref.reshape(count * 8, LANES)
    wide = jnp.concatenate([hi, hi], axis=1)
    for x in range(0, 8, 2):
        f = jnp.concatenate([src[pl.ds(x + i, count, stride=8), :] for i in range(2)], axis=1)
        fhi = f.astype(jnp.bfloat16)
        flo = (f - fhi.astype(jnp.float32)).astype(jnp.bfloat16)
        out = jnp.dot(wide, jnp.concatenate([fhi, flo], axis=0), preferred_element_type=jnp.float32)
        out = out + jnp.dot(lo, fhi, preferred_element_type=jnp.float32)
        for i in range(2):
            dst[pl.ds(x + i, count, stride=8), :] = out[:, i * LANES : (i + 1) * LANES]


def _transform_more(f_ref, hi_ref, lo_ref, _, out_ref):
    _transform_body(f_ref, hi_ref, lo_ref, out_ref)


def transform(block, planes, hi, lo, onto=None):
    count = block.shape[0]
    tiles = planes // 8
    halves = 2
    mat = pl.BlockSpec((count, count), lambda x, c: (0, 0))
    in_specs = [pl.BlockSpec((count, 8, LANES), lambda x, c: (0, c * tiles + x, 0)), mat, mat]
    operands = (block, hi, lo)
    if onto is None:
        out_map = lambda x, c: (0, x + 1, c)
    else:
        out_map = lambda x, c: (0, x * (tiles + 1), c)
        in_specs.append(pl.BlockSpec(memory_space=pl.ANY))
        operands += (onto,)
    return pl.pallas_call(
        _transform_body if onto is None else _transform_more,
        grid=(tiles, halves),
        in_specs=in_specs,
        out_specs=pl.BlockSpec((count, 8, LANES), out_map),
        out_shape=jax.ShapeDtypeStruct((count, 2 * planes, halves * LANES), jnp.float32),
        input_output_aliases={} if onto is None else {3: 0},
        compiler_params=pltpu.CompilerParams(
            dimension_semantics=("arbitrary", "arbitrary"), vmem_limit_bytes=VMEM_BYTES
        ),
        cost_estimate=pl.CostEstimate(flops=450_000_000, bytes_accessed=4_300_000, transcendentals=0),
        name="transform",
    )(*operands)


def per_device(initial_heat_matrix, conductivity, laser_x, laser_y, pixel_cell, observed, obs_var):
    members, planes, columns = initial_heat_matrix.shape
    blocks = 1
    for axis in MA:
        blocks *= lax.axis_size(axis)
    slabs = lax.axis_size("sa")
    first = lax.axis_index("sa") * planes
    u = initial_heat_matrix
    forward = [(i, i + 1) for i in range(slabs - 1)]
    backward = [(b, a) for a, b in forward]
    lasers = jnp.concatenate([laser_x, laser_y, jnp.broadcast_to(first, (1, STEPS))], axis=0)
    sent_in, bottom, top = forecast_inner(lasers, u, conductivity, blocks)
    low = lax.ppermute(top, "sa", forward)
    high = lax.ppermute(bottom, "sa", backward)
    held_in = lax.all_to_all(sent_in, MA, 0, 0, tiled=True)
    sent_out, surf_out = forecast_outer(lasers, u, conductivity, low, high, blocks)

    sums = cell_sums(pixel_cell, observed, obs_var)
    surf = surf_out.reshape(members, 2, planes // 4, LANES).transpose(1, 0, 2, 3)
    rows = jnp.concatenate([surf.reshape(2, members * planes // 4, LANES), sums], axis=1)
    rows = jnp.broadcast_to(rows[None], (blocks // 2,) + rows.shape).reshape((blocks,) + rows.shape[1:])
    rows, held_in = lax.optimization_barrier((rows, held_in))
    seen = lax.all_to_all(rows, MA, 0, 0, tiled=True)
    inner = held_in.reshape((blocks * members,) + held_in.shape[2:])
    part = gram_part(inner, seen, members)
    part = part + lax.ppermute(part, "ma_2", [(0, 1), (1, 0)])
    parts = [part] + [
        lax.ppermute(part, "sa", [(i, (i + s) % slabs) for i in range(slabs)]) for s in range(1, slabs)
    ]
    hi, lo = mix_matrices(parts)

    held_out = lax.all_to_all(sent_out, MA, 0, 0, tiled=True)
    done = transform(inner, planes // 2, hi, lo)
    done = transform(held_out.reshape(blocks * members, -1, LANES), planes // 2, hi, lo, done)
    back = lax.all_to_all(done.reshape((blocks, members) + done.shape[1:]), MA, 0, 0, tiled=True)
    return back.transpose(1, 2, 0, 3).reshape(members, planes, columns)


def solution(mesh):
    torus = Mesh(mesh.devices.reshape(4, 4, 2, mesh.shape["sa"]), ("ma_0", "ma_1", "ma_2", "sa"))
    in_specs = (
        P(MA, "sa", None),
        P("sa", None),
        P(MA, None),
        P(MA, None),
        P("sa", MA),
        P("sa", MA),
        P("sa", MA),
    )
    out_specs = P(MA, "sa", None)
    return jax.shard_map(
        per_device, mesh=torus, in_specs=in_specs, out_specs=out_specs, check_vma=False
    )
```

```python
import functools

import jax
import jax.numpy as jnp
from jax import lax
from jax.experimental import pallas as pl
from jax.experimental.pallas import tpu as pltpu
from jax.sharding import Mesh
from jax.sharding import PartitionSpec as P

DEPTH = 64
STEPS = 2
LANES = 128
VMEM_BYTES = 60 << 20
MA = ("ma_0", "ma_1", "ma_2")
MA_SA = ("ma_0", "ma_1", "ma_2", "sa")

step_dt = 0.025
alpha_cond = 0.05
laser_power = 12.0
beam_spot_width = 18.0

def _roll(x, shift, axis):
    return pltpu.roll(x, shift, axis)


def _wide_pair(a, b, low_half):
    return jnp.where(low_half, a, _roll(b, DEPTH, 1)), jnp.where(low_half, _roll(a, DEPTH, 1), b)


UNROLL = {2: 8, 3: 8}
FILL_UNROLL = 32


def _stencil_step(src, cond, pitch, base, tiles, apart, exs, ey_at, emit, surface):
    lane = lax.broadcasted_iota(jnp.int32, (8, LANES), 1)
    low_half = lane < DEPTH
    zpos = lane & (DEPTH - 1)
    z_last = zpos == DEPTH - 1
    z_first = zpos == 0
    unroll = UNROLL[tiles]

    def load(y, i):
        at = pl.ds(y * pitch + (base + i), 8, stride=tiles)
        u = src[at, :]
        c = cond[at, :]
        return u, c + c * (alpha_cond * (u * u))

    def face(one, two):
        return (one[1] + two[1]) * (two[0] - one[0])

    here = [load(0, i) for i in range(tiles)]
    fys = []
    for i in range(tiles):
        u, k = load(DEPTH - 1, i)
        before = (
            jnp.where(low_half, 0.0, _roll(u, DEPTH, 1)),
            jnp.where(low_half, 0.0, _roll(k, DEPTH, 1)),
        )
        fys.append(face(before, here[i]))

    def one(y, here, fys):
        after = [load(y + 1, i) for i in range(tiles)]
        line = {i: here[i] for i in range(tiles)}
        for i in range(-apart, tiles + apart):
            if i not in line and (i + apart in range(tiles) or i - apart in range(tiles)):
                line[i] = load(y, i)
        fx = {i: face(line[i], line[i + apart]) for i in range(-apart, tiles) if i in line}
        ey = jnp.broadcast_to(ey_at(y), (8, LANES))
        new_fys, values = [], []
        for i in range(tiles):
            u, k = here[i]
            fy = face(here[i], after[i])
            new_fys.append(fy)
            acc = (fy - fys[i]) + (fx[i] - fx[i - apart])
            up = jnp.where(z_last, 0.0, _roll(u, LANES - 1, 1))
            kp = jnp.where(z_last, 0.0, _roll(k, LANES - 1, 1))
            fz = (k + kp) * (up - u)
            acc = acc + (fz - jnp.where(z_first, k * u, _roll(fz, 1, 1)))
            values.append(u + (0.5 * step_dt) * acc + exs[i] * ey)
        return after, new_fys, values

    def several(a, carry):
        here, fys, tops = carry
        rows = []
        for q in range(unroll):
            here, fys, even = one(2 * (a * unroll + q), here, fys)
            here, fys, odd = one(2 * (a * unroll + q) + 1, here, fys)
            emit(a * unroll + q, even, odd)
            rows += [even, odd]
        if surface:
            kept = []
            for i in range(tiles):
                acc = _roll(tops[i], (LANES - len(rows)) % LANES, 1)
                for q, values in enumerate(rows):
                    shift = (LANES - (len(rows) - 1 - q)) % LANES
                    moved = _roll(values[i], shift, 1) if shift else values[i]
                    acc = jnp.where(zpos == DEPTH - len(rows) + q, moved, acc)
                kept.append(acc)
            tops = kept
        return here, fys, tops

    tops = [jnp.zeros((8, LANES), jnp.float32) for _ in range(tiles)] if surface else []
    return lax.fori_loop(0, DEPTH // 2 // unroll, several, (here, fys, tops))[2]


def _close(ref, pitch):
    lane = lax.broadcasted_iota(jnp.int32, (8, LANES), 1)
    for r in range(0, pitch, 8):
        first = ref[pl.ds(r, 8), :]
        ref[pl.ds(DEPTH * pitch + r, 8), :] = jnp.where(lane < DEPTH, _roll(first, DEPTH, 1), 0.0)


def _fill(ref, pitch, pieces):
    half = DEPTH // 2
    lane = lax.broadcasted_iota(jnp.int32, (8, LANES), 1)
    low_half = lane < DEPTH

    def several(b, carry):
        for q in range(FILL_UNROLL):
            a = b * FILL_UNROLL + q
            ca = pl.ds(pl.multiple_of(a * LANES, LANES), LANES)
            cb = pl.ds(pl.multiple_of((a + half) * LANES, LANES), LANES)
            for read, start, size, row, stride in pieces:
                even, odd = _wide_pair(read(pl.ds(start, size), ca), read(pl.ds(start, size), cb), low_half[:size])
                ref[pl.ds(2 * a * pitch + row, size, stride=stride), :] = even
                ref[pl.ds((2 * a + 1) * pitch + row, size, stride=stride), :] = odd
        return carry

    lax.fori_loop(0, half // FILL_UNROLL, several, 0)
    _close(ref, pitch)


def _two_steps(m, members, laser_ref, e_ref, ce_ref, u1_ref, ey_ref, pitch, plane_at, step1, step2, edged, put):
    sub = lax.broadcasted_iota(jnp.int32, (8, LANES), 0)
    lane = lax.broadcasted_iota(jnp.int32, (8, LANES), 1)
    last_layer = (lane & (DEPTH - 1)) == DEPTH - 1
    for t in range(STEPS):
        for g in range(0, DEPTH, 8):
            y = sub + g + jnp.where(lane < DEPTH, 0, DEPTH)
            dy = (y - laser_ref[members + m, t]).astype(jnp.float32)
            ey_ref[t, pl.ds(g, 8), :] = jnp.where(last_layer, jnp.exp(-(dy * dy) / beam_spot_width), 0.0)

    def ey_row(t):
        return lambda y: ey_ref[t, pl.ds(y, 1), :]

    def factors(t, base, tiles):
        found = []
        for i in range(tiles):
            dx = (plane_at(base + i + tiles * sub) - laser_ref[m, t]).astype(jnp.float32)
            found.append((step_dt * laser_power) * jnp.exp(-(dx * dx) / beam_spot_width))
        return found

    base, tiles, apart = step1

    def emit1(a, even, odd):
        for p, values in ((0, even), (1, odd)):
            for i, value in enumerate(values):
                at = pl.ds((2 * a + p) * pitch + base + i, 8, stride=tiles)
                u1_ref[at, :] = jnp.where(ce_ref[at, :] > 0.0, value, 0.0) if edged else value

    _stencil_step(e_ref, ce_ref, pitch, base, tiles, apart, factors(0, base, tiles), ey_row(0), emit1, False)
    _close(u1_ref, pitch)
    base, count, apart = step2
    low_half = lax.broadcasted_iota(jnp.int32, (8, LANES), 1) < DEPTH

    def emit2(a, even, odd):
        for i in range(count):
            one, two = _wide_pair(even[i], odd[i], low_half)
            put(a, i, one)
            put(a + DEPTH // 2, i, two)

    tops = _stencil_step(u1_ref, ce_ref, pitch, base, count, apart, factors(1, base, count), ey_row(1), emit2, True)
    return tops


INNER_PITCH = 32
OUTER_PITCH = 40
OUTER_ROW = 8


def _inner_body(
    laser_ref, u_ref, c_ref, out_ref, bottom_ref, top_ref, e_ref, ce_ref, u1_ref, ey_ref, rows_ref
):
    m = pl.program_id(0)
    planes = u_ref.shape[1]
    half = planes // 2
    pitch = INNER_PITCH

    @pl.when(m == 0)
    def _():
        _fill(ce_ref, pitch, [(lambda r, c: c_ref[r, c], 8 * i, 8, 8 * i, 1) for i in range(planes // 8)])
        bottom_ref[bottom_ref.shape[0] - 1] = c_ref[pl.ds(0, 2), :]
        top_ref[top_ref.shape[0] - 1] = c_ref[pl.ds(planes - 2, 2), :]

    bottom_ref[m] = u_ref[0, pl.ds(0, 2), :]
    top_ref[m] = u_ref[0, pl.ds(planes - 2, 2), :]
    _fill(e_ref, pitch, [(lambda r, c: u_ref[0, r, c], 8 * i, 8, 8 * i, 1) for i in range(planes // 8)])
    blocks, _, rows, _ = out_ref.shape
    halves = DEPTH // blocks
    out = out_ref.reshape(blocks * rows, LANES)

    def put(v, i, value):
        row = v * half + lax.div(v, halves) * (rows - halves * half)
        out[pl.ds(row + i, 8, stride=2), :] = value

    tops = _two_steps(
        m, pl.num_programs(0), laser_ref, e_ref, ce_ref, u1_ref, ey_ref, pitch,
        lambda row: laser_ref[laser_ref.shape[0] - 1, 0] + row, (4, 3, 1), (8, 2, 1), False, put,
    )
    for i in range(2):
        rows_ref[pl.ds(i, 8, stride=2), :] = tops[i]
    for d in range(blocks):
        out_ref[d, 0, pl.ds(halves * half, 8), :] = rows_ref[pl.ds(8 * (d % 2), 8), :]


def _outer_body(
    laser_ref, u_ref, c_ref, lo_ref, hi_ref, clo_ref, chi_ref, out_ref, surf_ref, e_ref, ce_ref, u1_ref,
    ey_ref,
):
    m = pl.program_id(0)
    planes = u_ref.shape[1]
    half = planes // 2
    pitch = OUTER_PITCH

    def pieces(main, low, high):
        row = OUTER_ROW
        return [
            (low, 0, 2, row, 2),
            (main, 0, 8, row + 4, 2),
            (main, 8, 2, row + 20, 2),
            (main, planes - 10, 2, row + 1, 2),
            (main, planes - 8, 8, row + 5, 2),
            (high, 0, 2, row + 21, 2),
        ]

    @pl.when(m == 0)
    def _():
        _fill(
            ce_ref,
            pitch,
            pieces(lambda r, c: c_ref[r, c], lambda r, c: clo_ref[0, r, c], lambda r, c: chi_ref[0, r, c]),
        )

    _fill(
        e_ref,
        pitch,
        pieces(lambda r, c: u_ref[0, r, c], lambda r, c: lo_ref[0, r, c], lambda r, c: hi_ref[0, r, c]),
    )
    out = out_ref.reshape(DEPTH * half, LANES)

    def put(v, i, value):
        out[pl.ds(pl.multiple_of(v * half + 8 * i, 8), 8), :] = value

    def plane_at(row):
        return laser_ref[laser_ref.shape[0] - 1, 0] + ((row - OUTER_ROW) >> 1) - 2 + (row & 1) * (planes - 8)

    tops = _two_steps(
        m, pl.num_programs(0), laser_ref, e_ref, ce_ref, u1_ref, ey_ref, pitch, plane_at,
        (OUTER_ROW, 3, 2), (OUTER_ROW + 4, 2, 2), True, put,
    )
    for i in range(2):
        surf_ref[0, pl.ds(8 * i, 8), :] = tops[i]


def _forecast_call(body, name, pitch, lasers, operands, specs, out_specs, out_shape, more_scratch):
    scratch = pltpu.VMEM(((DEPTH + 1) * pitch, LANES), jnp.float32)
    return pl.pallas_call(
        body,
        grid=(operands[0].shape[0],),
        in_specs=[pl.BlockSpec(memory_space=pltpu.SMEM)] + specs,
        out_specs=out_specs,
        out_shape=[jax.ShapeDtypeStruct(shape, jnp.float32) for shape in out_shape],
        scratch_shapes=[scratch, scratch, scratch, pltpu.VMEM((STEPS, DEPTH, LANES), jnp.float32)] + more_scratch,
        compiler_params=pltpu.CompilerParams(
            dimension_semantics=("arbitrary",), vmem_limit_bytes=VMEM_BYTES
        ),
        cost_estimate=pl.CostEstimate(flops=100_000_000, bytes_accessed=7_000_000, transcendentals=0),
        name=name,
    )(lasers, *operands)


def forecast_inner(lasers, u, cond, blocks):
    members, planes, columns = u.shape
    rows = columns // blocks // LANES * (planes // 2) + 8
    edge = (members + 1, 2, columns)
    specs = [
        pl.BlockSpec((1, planes, columns), lambda m: (m, 0, 0)),
        pl.BlockSpec((planes, columns), lambda m: (0, 0)),
    ]
    out_specs = [
        pl.BlockSpec((blocks, 1, rows, LANES), lambda m: (0, m, 0, 0)),
        pl.BlockSpec(edge, lambda m: (0, 0, 0)),
        pl.BlockSpec(edge, lambda m: (0, 0, 0)),
    ]
    return _forecast_call(
        _inner_body, "inner", INNER_PITCH, lasers, (u, cond), specs, out_specs,
        [(blocks, members, rows, LANES), edge, edge], [pltpu.VMEM((planes // 2, LANES), jnp.float32)],
    )


def forecast_outer(lasers, u, cond, low, high, blocks):
    members, planes, columns = u.shape
    halves = columns // blocks // LANES
    edge = lambda at: pl.BlockSpec((1, 2, columns), at)
    specs = [
        pl.BlockSpec((1, planes, columns), lambda m: (m, 0, 0)),
        pl.BlockSpec((planes, columns), lambda m: (0, 0)),
        edge(lambda m: (m, 0, 0)),
        edge(lambda m: (m, 0, 0)),
        edge(lambda m: (members, 0, 0)),
        edge(lambda m: (members, 0, 0)),
    ]
    out_specs = [
        pl.BlockSpec((blocks, 1, halves, planes // 2, LANES), lambda m: (0, m, 0, 0, 0)),
        pl.BlockSpec((1, planes // 2, LANES), lambda m: (m, 0, 0)),
    ]
    return _forecast_call(
        _outer_body, "outer", OUTER_PITCH, lasers, (u, cond, low, high, low, high), specs, out_specs,
        [(blocks, members, halves, planes // 2, LANES), (members, planes // 2, LANES)], [],
    )


def _nt(a, b):
    return lax.dot_general(
        a, b, (((1,), (1,)), ((), ())), precision=lax.Precision.HIGHEST, preferred_element_type=jnp.float32
    )


def _cell_sums_body(pc_ref, obs_ref, var_ref, out_ref):
    planes = pc_ref.shape[0]
    cell = lax.broadcasted_iota(jnp.int32, (planes, LANES), 1)
    weight = 1.0 / var_ref[...]
    value = weight * obs_ref[...]
    pc = pc_ref[...]
    wsum = jnp.zeros((planes, LANES), jnp.float32)
    rsum = jnp.zeros((planes, LANES), jnp.float32)
    for j in range(pc.shape[1]):
        hit = pc[:, j : j + 1] == cell
        wsum = wsum + jnp.where(hit, weight[:, j : j + 1], 0.0)
        rsum = rsum + jnp.where(hit, value[:, j : j + 1], 0.0)
    tiles = [8 * i for i in range(planes // 8)]
    for part, (one, two) in enumerate(((tiles[1], tiles[0]), (tiles[-2], tiles[-1]))):
        out_ref[part] = (
            wsum[one : one + 8]
            + _roll(rsum[one : one + 8], 64, 1)
            + _roll(wsum[two : two + 8], 32, 1)
            + _roll(rsum[two : two + 8], 96, 1)
        )


def cell_sums(pixel_cell, observed, obs_var):
    return pl.pallas_call(
        _cell_sums_body,
        out_shape=jax.ShapeDtypeStruct((2, 8, LANES), jnp.float32),
        cost_estimate=pl.CostEstimate(flops=400_000, bytes_accessed=100_000, transcendentals=0),
        compiler_params=pltpu.CompilerParams(vmem_limit_bytes=VMEM_BYTES),
        name="cell_sums",
    )(pixel_cell, observed, obs_var)


def _gram_body(members, inner_ref, seen_ref, out_ref, s_ref):
    sources = seen_ref.shape[0]
    count = sources * members
    outer = members * 8
    group = lax.broadcasted_iota(jnp.int32, (8, LANES), 1) // 4
    sums = [jnp.zeros((8, LANES), jnp.float32) for _ in range(4)]
    for i in range(sources):
        row = seen_ref[i, pl.ds(outer, 8), :]
        for g in range(4):
            sums[g] = jnp.where(group == (i + 8 * g) % sources, row, sums[g])
        s_ref[pl.ds(i * outer, outer), :] = seen_ref[i, pl.ds(0, outer), :]
    w_in, w_out, r_in, r_out = (
        _roll(sums[g], (LANES - 32 * g) % LANES, 1) if g else sums[g] for g in range(4)
    )
    both = jnp.zeros((count + 8, count), jnp.float32)
    for x in range(8):
        left, right = [], []
        for cells, wsums, rsums in ((inner_ref.reshape(count * 8, LANES), w_in, r_in), (s_ref, w_out, r_out)):
            s = cells[pl.ds(x, count, stride=8), :]
            wsum = wsums[x : x + 1]
            rsum = rsums[x : x + 1]
            mean = jnp.sum(s, axis=0, keepdims=True) * (1.0 / count)
            anom = s - mean
            q = jnp.broadcast_to(rsum - wsum * mean, (8, LANES))
            left.append(jnp.concatenate([anom * wsum, q], axis=0))
            right.append(anom)
        both = both + _nt(jnp.concatenate(left, axis=1), jnp.concatenate(right, axis=1))
    out_ref[...] = both


def gram_part(inner, seen, members):
    count, rows, _ = inner.shape
    last = rows // 8 - 1
    return pl.pallas_call(
        functools.partial(_gram_body, members),
        grid=(1,),
        in_specs=[
            pl.BlockSpec((count, 8, LANES), lambda i: (0, last, 0)),
            pl.BlockSpec(seen.shape, lambda i: (0, 0, 0)),
        ],
        out_specs=pl.BlockSpec((count + 8, count), lambda i: (0, 0)),
        out_shape=jax.ShapeDtypeStruct((count + 8, count), jnp.float32),
        scratch_shapes=[pltpu.VMEM((count * 8, LANES), jnp.float32)],
        cost_estimate=pl.CostEstimate(flops=80_000_000, bytes_accessed=1_700_000, transcendentals=0),
        compiler_params=pltpu.CompilerParams(vmem_limit_bytes=VMEM_BYTES),
        name="gram",
    )(inner, seen)


GROUP = 8


def _mix_body(p0_ref, p1_ref, p2_ref, p3_ref, hi_ref, lo_ref, a_ref):
    count = hi_ref.shape[0]

    def total(rows):
        return (p0_ref[rows, :] + p1_ref[rows, :]) + (p2_ref[rows, :] + p3_ref[rows, :])

    proj = total(pl.ds(count, 8))
    ntile = count // 8
    sub = lax.broadcasted_iota(jnp.int32, (8, LANES), 0)
    lane = lax.broadcasted_iota(jnp.int32, (8, LANES), 1)
    a, inv, diag = [], [], []
    for i in range(ntile):
        eye = (lane == sub + 8 * i).astype(jnp.float32)
        a.append(eye + total(pl.ds(8 * i, 8)) * (1.0 / (count - 1)))
        inv.append(eye)
        diag.append(jnp.ones((8, LANES), jnp.float32))

    def row_of(tile, r):
        return jnp.broadcast_to(tile[r : r + 1, :], (8, LANES))

    for j0 in range(0, count, GROUP):
        base = j0 // 8
        cols = [
            {i: jnp.broadcast_to(a[i][:, j0 + t : j0 + t + 1], (8, LANES)) for i in range(base, ntile)}
            for t in range(GROUP)
        ]
        r0 = j0 % 8
        arow = [row_of(a[base], r0 + t) for t in range(GROUP)]
        irow = [row_of(inv[base], r0 + t) for t in range(GROUP)]
        for t in range(GROUP):
            pivot = row_of(cols[t][base], r0 + t)
            recip = 1.0 / pivot
            diag[base] = jnp.where(sub == r0 + t, pivot, diag[base])
            for s in range(t + 1, GROUP):
                factor = row_of(cols[t][base], r0 + s) * recip
                for i in range(base, ntile):
                    cols[s][i] = cols[s][i] - factor * cols[t][i]
                arow[s] = arow[s] - factor * arow[t]
                irow[s] = irow[s] - factor * irow[t]
            arow[t] = arow[t] * recip
            irow[t] = irow[t] * recip
            cols[t][base] = jnp.where(sub > r0 + t, cols[t][base], 0.0)
        for i in range(base, ntile):
            for t in range(GROUP):
                a[i] = a[i] - cols[t][i] * arow[t]
                inv[i] = inv[i] - cols[t][i] * irow[t]
    for i in range(ntile):
        a_ref[pl.ds(8 * i, 8), :] = inv[i] / jnp.sqrt(diag[i])
    linv = a_ref[...]
    middle = _nt(proj, linv)
    wmean = lax.dot_general(
        middle, linv, (((1,), (0,)), ((), ())), precision=lax.Precision.HIGHEST, preferred_element_type=jnp.float32
    ) * (1.0 / (count - 1))
    mix = linv + wmean[0:1]
    mix = mix + (1.0 - jnp.sum(mix, axis=1, keepdims=True)) * (1.0 / count)
    hi = mix.astype(jnp.bfloat16)
    hi_ref[...] = hi
    lo_ref[...] = (mix - hi.astype(jnp.float32)).astype(jnp.bfloat16)


def mix_matrices(parts):
    count = parts[0].shape[1]
    shape = jax.ShapeDtypeStruct((count, count), jnp.bfloat16)
    return pl.pallas_call(
        _mix_body,
        out_shape=[shape, shape],
        scratch_shapes=[pltpu.VMEM((count, LANES), jnp.float32)],
        cost_estimate=pl.CostEstimate(flops=200_000_000, bytes_accessed=600_000, transcendentals=0),
        compiler_params=pltpu.CompilerParams(vmem_limit_bytes=VMEM_BYTES),
        name="mix",
    )(*parts)


def _transform_body(f_ref, hi_ref, lo_ref, out_ref):
    count = hi_ref.shape[0]
    hi = hi_ref[...]
    lo = lo_ref[...]
    src = f_ref.reshape(count * 8, LANES)
    dst = out_ref.reshape(count * 8, LANES)
    wide = jnp.concatenate([hi, hi], axis=1)
    for x in range(0, 8, 2):
        f = jnp.concatenate([src[pl.ds(x + i, count, stride=8), :] for i in range(2)], axis=1)
        fhi = f.astype(jnp.bfloat16)
        flo = (f - fhi.astype(jnp.float32)).astype(jnp.bfloat16)
        out = jnp.dot(wide, jnp.concatenate([fhi, flo], axis=0), preferred_element_type=jnp.float32)
        out = out + jnp.dot(lo, fhi, preferred_element_type=jnp.float32)
        for i in range(2):
            dst[pl.ds(x + i, count, stride=8), :] = out[:, i * LANES : (i + 1) * LANES]


def _transform_more(f_ref, hi_ref, lo_ref, _, out_ref):
    _transform_body(f_ref, hi_ref, lo_ref, out_ref)


def transform(block, planes, hi, lo, onto=None):
    count = block.shape[0]
    tiles = planes // 8
    halves = 2
    mat = pl.BlockSpec((count, count), lambda x, c: (0, 0))
    in_specs = [pl.BlockSpec((count, 8, LANES), lambda x, c: (0, c * tiles + x, 0)), mat, mat]
    operands = (block, hi, lo)
    if onto is None:
        out_map = lambda x, c: (0, x + 1, c)
    else:
        out_map = lambda x, c: (0, x * (tiles + 1), c)
        in_specs.append(pl.BlockSpec(memory_space=pl.ANY))
        operands += (onto,)
    return pl.pallas_call(
        _transform_body if onto is None else _transform_more,
        grid=(tiles, halves),
        in_specs=in_specs,
        out_specs=pl.BlockSpec((count, 8, LANES), out_map),
        out_shape=jax.ShapeDtypeStruct((count, 2 * planes, halves * LANES), jnp.float32),
        input_output_aliases={} if onto is None else {3: 0},
        compiler_params=pltpu.CompilerParams(
            dimension_semantics=("arbitrary", "arbitrary"), vmem_limit_bytes=VMEM_BYTES
        ),
        cost_estimate=pl.CostEstimate(flops=450_000_000, bytes_accessed=4_300_000, transcendentals=0),
        name="transform",
    )(*operands)


def per_device(initial_heat_matrix, conductivity, laser_x, laser_y, pixel_cell, observed, obs_var):
    members, planes, columns = initial_heat_matrix.shape
    blocks = 1
    for axis in MA:
        blocks *= lax.axis_size(axis)
    slabs = lax.axis_size("sa")
    first = lax.axis_index("sa") * planes
    u = initial_heat_matrix
    forward = [(i, i + 1) for i in range(slabs - 1)]
    backward = [(b, a) for a, b in forward]
    lasers = jnp.concatenate([laser_x, laser_y, jnp.broadcast_to(first, (1, STEPS))], axis=0)
    sent_in, bottom, top = forecast_inner(lasers, u, conductivity, blocks)
    low = lax.ppermute(top, "sa", forward)
    high = lax.ppermute(bottom, "sa", backward)
    held_in = lax.all_to_all(sent_in, MA, 0, 0, tiled=True)
    sent_out, surf_out = forecast_outer(lasers, u, conductivity, low, high, blocks)

    sums = cell_sums(pixel_cell, observed, obs_var)
    surf = surf_out.reshape(members, 2, planes // 4, LANES).transpose(1, 0, 2, 3)
    rows = jnp.concatenate([surf.reshape(2, members * planes // 4, LANES), sums], axis=1)
    rows = jnp.broadcast_to(rows[None], (blocks // 2,) + rows.shape).reshape((blocks,) + rows.shape[1:])
    rows, held_in = lax.optimization_barrier((rows, held_in))
    seen = lax.all_to_all(rows, MA, 0, 0, tiled=True)
    inner = held_in.reshape((blocks * members,) + held_in.shape[2:])
    part = gram_part(inner, seen, members)
    part = part + lax.ppermute(part, "ma_2", [(0, 1), (1, 0)])
    parts = [part] + [
        lax.ppermute(part, "sa", [(i, (i + s) % slabs) for i in range(slabs)]) for s in range(1, slabs)
    ]
    hi, lo = mix_matrices(parts)

    held_out = lax.all_to_all(sent_out, MA, 0, 0, tiled=True)
    done = transform(inner, planes // 2, hi, lo)
    done = transform(held_out.reshape(blocks * members, -1, LANES), planes // 2, hi, lo, done)
    back = lax.all_to_all(done.reshape((blocks, members) + done.shape[1:]), MA, 0, 0, tiled=True)
    return back.transpose(1, 2, 0, 3).reshape(members, planes, columns)


def solution(mesh):
    torus = Mesh(mesh.devices.reshape(4, 4, 2, mesh.shape["sa"]), ("ma_0", "ma_1", "ma_2", "sa"))
    in_specs = (
        P(MA, "sa", None),
        P("sa", None),
        P(MA, None),
        P(MA, None),
        P("sa", MA),
        P("sa", MA),
        P("sa", MA),
    )
    out_specs = P(MA, "sa", None)
    return jax.shard_map(
        per_device, mesh=torus, in_specs=in_specs, out_specs=out_specs, check_vma=False
    )
```

```python
import functools

import jax
import jax.numpy as jnp
from jax import lax
from jax.experimental import pallas as pl
from jax.experimental.pallas import tpu as pltpu
from jax.sharding import Mesh
from jax.sharding import PartitionSpec as P

DEPTH = 64
STEPS = 2
LANES = 128
VMEM_BYTES = 60 << 20
MA = ("ma_0", "ma_1", "ma_2")
MA_SA = ("ma_0", "ma_1", "ma_2", "sa")

step_dt = 0.025
alpha_cond = 0.05
laser_power = 12.0
beam_spot_width = 18.0

def _roll(x, shift, axis):
    return pltpu.roll(x, shift, axis)


def _wide_pair(a, b, low_half):
    return jnp.where(low_half, a, _roll(b, DEPTH, 1)), jnp.where(low_half, _roll(a, DEPTH, 1), b)


UNROLL = {2: 8, 3: 8}
FILL_UNROLL = 32


def _stencil_step(src, cond, pitch, base, tiles, apart, exs, ey_at, emit, surface):
    lane = lax.broadcasted_iota(jnp.int32, (8, LANES), 1)
    low_half = lane < DEPTH
    zpos = lane & (DEPTH - 1)
    z_last = zpos == DEPTH - 1
    z_first = zpos == 0
    unroll = UNROLL[tiles]

    def load(y, i):
        at = pl.ds(y * pitch + (base + i), 8, stride=tiles)
        u = src[at, :]
        c = cond[at, :]
        return u, c + c * (alpha_cond * (u * u))

    def face(one, two):
        return (one[1] + two[1]) * (two[0] - one[0])

    here = [load(0, i) for i in range(tiles)]
    fys = []
    for i in range(tiles):
        u, k = load(DEPTH - 1, i)
        before = (
            jnp.where(low_half, 0.0, _roll(u, DEPTH, 1)),
            jnp.where(low_half, 0.0, _roll(k, DEPTH, 1)),
        )
        fys.append(face(before, here[i]))

    def one(y, here, fys):
        after = [load(y + 1, i) for i in range(tiles)]
        line = {i: here[i] for i in range(tiles)}
        for i in range(-apart, tiles + apart):
            if i not in line and (i + apart in range(tiles) or i - apart in range(tiles)):
                line[i] = load(y, i)
        fx = {i: face(line[i], line[i + apart]) for i in range(-apart, tiles) if i in line}
        ey = jnp.broadcast_to(ey_at(y), (8, LANES))
        new_fys, values = [], []
        for i in range(tiles):
            u, k = here[i]
            fy = face(here[i], after[i])
            new_fys.append(fy)
            acc = (fy - fys[i]) + (fx[i] - fx[i - apart])
            up = jnp.where(z_last, 0.0, _roll(u, LANES - 1, 1))
            kp = jnp.where(z_last, 0.0, _roll(k, LANES - 1, 1))
            fz = (k + kp) * (up - u)
            acc = acc + (fz - jnp.where(z_first, k * u, _roll(fz, 1, 1)))
            values.append(u + (0.5 * step_dt) * acc + exs[i] * ey)
        return after, new_fys, values

    def several(a, carry):
        here, fys, tops = carry
        rows = []
        for q in range(unroll):
            here, fys, even = one(2 * (a * unroll + q), here, fys)
            here, fys, odd = one(2 * (a * unroll + q) + 1, here, fys)
            emit(a * unroll + q, even, odd)
            rows += [even, odd]
        if surface:
            kept = []
            for i in range(tiles):
                acc = _roll(tops[i], (LANES - len(rows)) % LANES, 1)
                for q, values in enumerate(rows):
                    shift = (LANES - (len(rows) - 1 - q)) % LANES
                    moved = _roll(values[i], shift, 1) if shift else values[i]
                    acc = jnp.where(zpos == DEPTH - len(rows) + q, moved, acc)
                kept.append(acc)
            tops = kept
        return here, fys, tops

    tops = [jnp.zeros((8, LANES), jnp.float32) for _ in range(tiles)] if surface else []
    return lax.fori_loop(0, DEPTH // 2 // unroll, several, (here, fys, tops))[2]


def _close(ref, pitch):
    lane = lax.broadcasted_iota(jnp.int32, (8, LANES), 1)
    for r in range(0, pitch, 8):
        first = ref[pl.ds(r, 8), :]
        ref[pl.ds(DEPTH * pitch + r, 8), :] = jnp.where(lane < DEPTH, _roll(first, DEPTH, 1), 0.0)


def _fill(ref, pitch, pieces):
    half = DEPTH // 2
    lane = lax.broadcasted_iota(jnp.int32, (8, LANES), 1)
    low_half = lane < DEPTH

    def several(b, carry):
        for q in range(FILL_UNROLL):
            a = b * FILL_UNROLL + q
            ca = pl.ds(pl.multiple_of(a * LANES, LANES), LANES)
            cb = pl.ds(pl.multiple_of((a + half) * LANES, LANES), LANES)
            for read, start, size, row, stride in pieces:
                even, odd = _wide_pair(read(pl.ds(start, size), ca), read(pl.ds(start, size), cb), low_half[:size])
                ref[pl.ds(2 * a * pitch + row, size, stride=stride), :] = even
                ref[pl.ds((2 * a + 1) * pitch + row, size, stride=stride), :] = odd
        return carry

    lax.fori_loop(0, half // FILL_UNROLL, several, 0)
    _close(ref, pitch)


def _two_steps(m, lx_ref, ly_ref, e_ref, ce_ref, u1_ref, ey_ref, pitch, plane_at, step1, step2, edged, put):
    sub = lax.broadcasted_iota(jnp.int32, (8, LANES), 0)
    lane = lax.broadcasted_iota(jnp.int32, (8, LANES), 1)
    last_layer = (lane & (DEPTH - 1)) == DEPTH - 1
    for t in range(STEPS):
        for g in range(0, DEPTH, 8):
            y = sub + g + jnp.where(lane < DEPTH, 0, DEPTH)
            dy = (y - ly_ref[t, m]).astype(jnp.float32)
            ey_ref[t, pl.ds(g, 8), :] = jnp.where(last_layer, jnp.exp(-(dy * dy) / beam_spot_width), 0.0)

    def ey_row(t):
        return lambda y: ey_ref[t, pl.ds(y, 1), :]

    def factors(t, base, tiles):
        found = []
        for i in range(tiles):
            dx = (plane_at(base + i + tiles * sub) - lx_ref[t, m]).astype(jnp.float32)
            found.append((step_dt * laser_power) * jnp.exp(-(dx * dx) / beam_spot_width))
        return found

    base, tiles, apart = step1

    def emit1(a, even, odd):
        for p, values in ((0, even), (1, odd)):
            for i, value in enumerate(values):
                at = pl.ds((2 * a + p) * pitch + base + i, 8, stride=tiles)
                u1_ref[at, :] = jnp.where(ce_ref[at, :] > 0.0, value, 0.0) if edged else value

    _stencil_step(e_ref, ce_ref, pitch, base, tiles, apart, factors(0, base, tiles), ey_row(0), emit1, False)
    _close(u1_ref, pitch)
    base, count, apart = step2
    low_half = lax.broadcasted_iota(jnp.int32, (8, LANES), 1) < DEPTH

    def emit2(a, even, odd):
        for i in range(count):
            one, two = _wide_pair(even[i], odd[i], low_half)
            put(a, i, one)
            put(a + DEPTH // 2, i, two)

    tops = _stencil_step(u1_ref, ce_ref, pitch, base, count, apart, factors(1, base, count), ey_row(1), emit2, True)
    return tops


INNER_PITCH = 32
OUTER_PITCH = 40
OUTER_ROW = 8


def _inner_body(
    lx_ref, ly_ref, u_ref, c_ref, out_ref, bottom_ref, top_ref, e_ref, ce_ref, u1_ref, ey_ref, rows_ref
):
    m = pl.program_id(0)
    planes = u_ref.shape[1]
    half = planes // 2
    pitch = INNER_PITCH

    @pl.when(m == 0)
    def _():
        _fill(ce_ref, pitch, [(lambda r, c: c_ref[r, c], 8 * i, 8, 8 * i, 1) for i in range(planes // 8)])
        bottom_ref[bottom_ref.shape[0] - 1] = c_ref[pl.ds(0, 2), :]
        top_ref[top_ref.shape[0] - 1] = c_ref[pl.ds(planes - 2, 2), :]

    bottom_ref[m] = u_ref[0, pl.ds(0, 2), :]
    top_ref[m] = u_ref[0, pl.ds(planes - 2, 2), :]
    _fill(e_ref, pitch, [(lambda r, c: u_ref[0, r, c], 8 * i, 8, 8 * i, 1) for i in range(planes // 8)])
    blocks, _, rows, _ = out_ref.shape
    halves = DEPTH // blocks
    out = out_ref.reshape(blocks * rows, LANES)

    def put(v, i, value):
        row = v * half + lax.div(v, halves) * (rows - halves * half)
        out[pl.ds(row + i, 8, stride=2), :] = value

    tops = _two_steps(
        m, lx_ref, ly_ref, e_ref, ce_ref, u1_ref, ey_ref, pitch,
        lambda row: lax.axis_index("sa") * planes + row, (4, 3, 1), (8, 2, 1), False, put,
    )
    for i in range(2):
        rows_ref[pl.ds(i, 8, stride=2), :] = tops[i]
    for d in range(blocks):
        out_ref[d, 0, pl.ds(halves * half, 8), :] = rows_ref[pl.ds(8 * (d % 2), 8), :]


def _outer_body(
    lx_ref, ly_ref, u_ref, c_ref, lo_ref, hi_ref, clo_ref, chi_ref, out_ref, surf_ref, e_ref, ce_ref, u1_ref,
    ey_ref,
):
    m = pl.program_id(0)
    planes = u_ref.shape[1]
    half = planes // 2
    pitch = OUTER_PITCH

    def pieces(main, low, high):
        row = OUTER_ROW
        return [
            (low, 0, 2, row, 2),
            (main, 0, 8, row + 4, 2),
            (main, 8, 2, row + 20, 2),
            (main, planes - 10, 2, row + 1, 2),
            (main, planes - 8, 8, row + 5, 2),
            (high, 0, 2, row + 21, 2),
        ]

    @pl.when(m == 0)
    def _():
        _fill(
            ce_ref,
            pitch,
            pieces(lambda r, c: c_ref[r, c], lambda r, c: clo_ref[0, r, c], lambda r, c: chi_ref[0, r, c]),
        )

    _fill(
        e_ref,
        pitch,
        pieces(lambda r, c: u_ref[0, r, c], lambda r, c: lo_ref[0, r, c], lambda r, c: hi_ref[0, r, c]),
    )
    out = out_ref.reshape(DEPTH * half, LANES)

    def put(v, i, value):
        out[pl.ds(pl.multiple_of(v * half + 8 * i, 8), 8), :] = value

    def plane_at(row):
        return lax.axis_index("sa") * planes + ((row - OUTER_ROW) >> 1) - 2 + (row & 1) * (planes - 8)

    tops = _two_steps(
        m, lx_ref, ly_ref, e_ref, ce_ref, u1_ref, ey_ref, pitch, plane_at,
        (OUTER_ROW, 3, 2), (OUTER_ROW + 4, 2, 2), True, put,
    )
    for i in range(2):
        surf_ref[0, pl.ds(8 * i, 8), :] = tops[i]


def _forecast_call(body, name, pitch, lasers, operands, specs, out_specs, out_shape, more_scratch):
    scratch = pltpu.VMEM(((DEPTH + 1) * pitch, LANES), jnp.float32)
    return pl.pallas_call(
        body,
        grid=(operands[0].shape[0],),
        in_specs=[pl.BlockSpec(memory_space=pltpu.SMEM)] * 2 + specs,
        out_specs=out_specs,
        out_shape=[jax.ShapeDtypeStruct(shape, jnp.float32) for shape in out_shape],
        scratch_shapes=[scratch, scratch, scratch, pltpu.VMEM((STEPS, DEPTH, LANES), jnp.float32)] + more_scratch,
        compiler_params=pltpu.CompilerParams(
            dimension_semantics=("arbitrary",), vmem_limit_bytes=VMEM_BYTES
        ),
        cost_estimate=pl.CostEstimate(flops=100_000_000, bytes_accessed=7_000_000, transcendentals=0),
        name=name,
    )(*lasers, *operands)


def forecast_inner(lasers, u, cond, blocks):
    members, planes, columns = u.shape
    rows = columns // blocks // LANES * (planes // 2) + 8
    edge = (members + 1, 2, columns)
    specs = [
        pl.BlockSpec((1, planes, columns), lambda m: (m, 0, 0)),
        pl.BlockSpec((planes, columns), lambda m: (0, 0)),
    ]
    out_specs = [
        pl.BlockSpec((blocks, 1, rows, LANES), lambda m: (0, m, 0, 0)),
        pl.BlockSpec(edge, lambda m: (0, 0, 0)),
        pl.BlockSpec(edge, lambda m: (0, 0, 0)),
    ]
    return _forecast_call(
        _inner_body, "inner", INNER_PITCH, lasers, (u, cond), specs, out_specs,
        [(blocks, members, rows, LANES), edge, edge], [pltpu.VMEM((planes // 2, LANES), jnp.float32)],
    )


def forecast_outer(lasers, u, cond, low, high, blocks):
    members, planes, columns = u.shape
    halves = columns // blocks // LANES
    edge = lambda at: pl.BlockSpec((1, 2, columns), at)
    specs = [
        pl.BlockSpec((1, planes, columns), lambda m: (m, 0, 0)),
        pl.BlockSpec((planes, columns), lambda m: (0, 0)),
        edge(lambda m: (m, 0, 0)),
        edge(lambda m: (m, 0, 0)),
        edge(lambda m: (members, 0, 0)),
        edge(lambda m: (members, 0, 0)),
    ]
    out_specs = [
        pl.BlockSpec((blocks, 1, halves, planes // 2, LANES), lambda m: (0, m, 0, 0, 0)),
        pl.BlockSpec((1, planes // 2, LANES), lambda m: (m, 0, 0)),
    ]
    return _forecast_call(
        _outer_body, "outer", OUTER_PITCH, lasers, (u, cond, low, high, low, high), specs, out_specs,
        [(blocks, members, halves, planes // 2, LANES), (members, planes // 2, LANES)], [],
    )


def _nt(a, b):
    return lax.dot_general(
        a, b, (((1,), (1,)), ((), ())), precision=lax.Precision.HIGHEST, preferred_element_type=jnp.float32
    )


def _cell_sums_body(pc_ref, obs_ref, var_ref, out_ref):
    planes = pc_ref.shape[0]
    cell = lax.broadcasted_iota(jnp.int32, (planes, LANES), 1)
    weight = 1.0 / var_ref[...]
    value = weight * obs_ref[...]
    pc = pc_ref[...]
    wsum = jnp.zeros((planes, LANES), jnp.float32)
    rsum = jnp.zeros((planes, LANES), jnp.float32)
    for j in range(pc.shape[1]):
        hit = pc[:, j : j + 1] == cell
        wsum = wsum + jnp.where(hit, weight[:, j : j + 1], 0.0)
        rsum = rsum + jnp.where(hit, value[:, j : j + 1], 0.0)
    tiles = [8 * i for i in range(planes // 8)]
    for part, (one, two) in enumerate(((tiles[1], tiles[0]), (tiles[-2], tiles[-1]))):
        out_ref[part] = (
            wsum[one : one + 8]
            + _roll(rsum[one : one + 8], 64, 1)
            + _roll(wsum[two : two + 8], 32, 1)
            + _roll(rsum[two : two + 8], 96, 1)
        )


def cell_sums(pixel_cell, observed, obs_var):
    return pl.pallas_call(
        _cell_sums_body,
        out_shape=jax.ShapeDtypeStruct((2, 8, LANES), jnp.float32),
        cost_estimate=pl.CostEstimate(flops=400_000, bytes_accessed=100_000, transcendentals=0),
        compiler_params=pltpu.CompilerParams(vmem_limit_bytes=VMEM_BYTES),
        name="cell_sums",
    )(pixel_cell, observed, obs_var)


def _gram_body(members, inner_ref, seen_ref, out_ref, s_ref):
    sources = seen_ref.shape[0]
    count = sources * members
    outer = members * 8
    group = lax.broadcasted_iota(jnp.int32, (8, LANES), 1) // 4
    sums = [jnp.zeros((8, LANES), jnp.float32) for _ in range(4)]
    for i in range(sources):
        row = seen_ref[i, pl.ds(outer, 8), :]
        for g in range(4):
            sums[g] = jnp.where(group == (i + 8 * g) % sources, row, sums[g])
        s_ref[pl.ds(i * outer, outer), :] = seen_ref[i, pl.ds(0, outer), :]
    w_in, w_out, r_in, r_out = (
        _roll(sums[g], (LANES - 32 * g) % LANES, 1) if g else sums[g] for g in range(4)
    )
    both = jnp.zeros((count + 8, count), jnp.float32)
    for x in range(8):
        left, right = [], []
        for cells, wsums, rsums in ((inner_ref.reshape(count * 8, LANES), w_in, r_in), (s_ref, w_out, r_out)):
            s = cells[pl.ds(x, count, stride=8), :]
            wsum = wsums[x : x + 1]
            rsum = rsums[x : x + 1]
            mean = jnp.sum(s, axis=0, keepdims=True) * (1.0 / count)
            anom = s - mean
            q = jnp.broadcast_to(rsum - wsum * mean, (8, LANES))
            left.append(jnp.concatenate([anom * wsum, q], axis=0))
            right.append(anom)
        both = both + _nt(jnp.concatenate(left, axis=1), jnp.concatenate(right, axis=1))
    out_ref[...] = both


def gram_part(inner, seen, members):
    count, rows, _ = inner.shape
    last = rows // 8 - 1
    return pl.pallas_call(
        functools.partial(_gram_body, members),
        grid=(1,),
        in_specs=[
            pl.BlockSpec((count, 8, LANES), lambda i: (0, last, 0)),
            pl.BlockSpec(seen.shape, lambda i: (0, 0, 0)),
        ],
        out_specs=pl.BlockSpec((count + 8, count), lambda i: (0, 0)),
        out_shape=jax.ShapeDtypeStruct((count + 8, count), jnp.float32),
        scratch_shapes=[pltpu.VMEM((count * 8, LANES), jnp.float32)],
        cost_estimate=pl.CostEstimate(flops=80_000_000, bytes_accessed=1_700_000, transcendentals=0),
        compiler_params=pltpu.CompilerParams(vmem_limit_bytes=VMEM_BYTES),
        name="gram",
    )(inner, seen)


GROUP = 8


def _mix_body(p0_ref, p1_ref, p2_ref, p3_ref, hi_ref, lo_ref, a_ref):
    count = hi_ref.shape[0]

    def total(rows):
        return (p0_ref[rows, :] + p1_ref[rows, :]) + (p2_ref[rows, :] + p3_ref[rows, :])

    proj = total(pl.ds(count, 8))
    ntile = count // 8
    sub = lax.broadcasted_iota(jnp.int32, (8, LANES), 0)
    lane = lax.broadcasted_iota(jnp.int32, (8, LANES), 1)
    a, inv, diag = [], [], []
    for i in range(ntile):
        eye = (lane == sub + 8 * i).astype(jnp.float32)
        a.append(eye + total(pl.ds(8 * i, 8)) * (1.0 / (count - 1)))
        inv.append(eye)
        diag.append(jnp.ones((8, LANES), jnp.float32))

    def row_of(tile, r):
        return jnp.broadcast_to(tile[r : r + 1, :], (8, LANES))

    for j0 in range(0, count, GROUP):
        base = j0 // 8
        cols = [
            {i: jnp.broadcast_to(a[i][:, j0 + t : j0 + t + 1], (8, LANES)) for i in range(base, ntile)}
            for t in range(GROUP)
        ]
        r0 = j0 % 8
        arow = [row_of(a[base], r0 + t) for t in range(GROUP)]
        irow = [row_of(inv[base], r0 + t) for t in range(GROUP)]
        for t in range(GROUP):
            pivot = row_of(cols[t][base], r0 + t)
            recip = 1.0 / pivot
            diag[base] = jnp.where(sub == r0 + t, pivot, diag[base])
            for s in range(t + 1, GROUP):
                factor = row_of(cols[t][base], r0 + s) * recip
                for i in range(base, ntile):
                    cols[s][i] = cols[s][i] - factor * cols[t][i]
                arow[s] = arow[s] - factor * arow[t]
                irow[s] = irow[s] - factor * irow[t]
            arow[t] = arow[t] * recip
            irow[t] = irow[t] * recip
            cols[t][base] = jnp.where(sub > r0 + t, cols[t][base], 0.0)
        for i in range(base, ntile):
            for t in range(GROUP):
                a[i] = a[i] - cols[t][i] * arow[t]
                inv[i] = inv[i] - cols[t][i] * irow[t]
    for i in range(ntile):
        a_ref[pl.ds(8 * i, 8), :] = inv[i] / jnp.sqrt(diag[i])
    linv = a_ref[...]
    middle = _nt(proj, linv)
    wmean = lax.dot_general(
        middle, linv, (((1,), (0,)), ((), ())), precision=lax.Precision.HIGHEST, preferred_element_type=jnp.float32
    ) * (1.0 / (count - 1))
    mix = linv + wmean[0:1]
    mix = mix + (1.0 - jnp.sum(mix, axis=1, keepdims=True)) * (1.0 / count)
    hi = mix.astype(jnp.bfloat16)
    hi_ref[...] = hi
    lo_ref[...] = (mix - hi.astype(jnp.float32)).astype(jnp.bfloat16)


def mix_matrices(parts):
    count = parts[0].shape[1]
    shape = jax.ShapeDtypeStruct((count, count), jnp.bfloat16)
    return pl.pallas_call(
        _mix_body,
        out_shape=[shape, shape],
        scratch_shapes=[pltpu.VMEM((count, LANES), jnp.float32)],
        cost_estimate=pl.CostEstimate(flops=200_000_000, bytes_accessed=600_000, transcendentals=0),
        compiler_params=pltpu.CompilerParams(vmem_limit_bytes=VMEM_BYTES),
        name="mix",
    )(*parts)


def _transform_body(f_ref, hi_ref, lo_ref, out_ref):
    count = hi_ref.shape[0]
    hi = hi_ref[...]
    lo = lo_ref[...]
    src = f_ref.reshape(count * 8, LANES)
    dst = out_ref.reshape(count * 8, LANES)
    wide = jnp.concatenate([hi, hi], axis=1)
    for x in range(0, 8, 2):
        f = jnp.concatenate([src[pl.ds(x + i, count, stride=8), :] for i in range(2)], axis=1)
        fhi = f.astype(jnp.bfloat16)
        flo = (f - fhi.astype(jnp.float32)).astype(jnp.bfloat16)
        out = jnp.dot(wide, jnp.concatenate([fhi, flo], axis=0), preferred_element_type=jnp.float32)
        out = out + jnp.dot(lo, fhi, preferred_element_type=jnp.float32)
        for i in range(2):
            dst[pl.ds(x + i, count, stride=8), :] = out[:, i * LANES : (i + 1) * LANES]


def _transform_more(f_ref, hi_ref, lo_ref, _, out_ref):
    _transform_body(f_ref, hi_ref, lo_ref, out_ref)


def transform(block, planes, hi, lo, onto=None):
    count = block.shape[0]
    tiles = planes // 8
    halves = 2
    mat = pl.BlockSpec((count, count), lambda x, c: (0, 0))
    in_specs = [pl.BlockSpec((count, 8, LANES), lambda x, c: (0, c * tiles + x, 0)), mat, mat]
    operands = (block, hi, lo)
    if onto is None:
        out_map = lambda x, c: (0, x + 1, c)
    else:
        out_map = lambda x, c: (0, x * (tiles + 1), c)
        in_specs.append(pl.BlockSpec(memory_space=pl.ANY))
        operands += (onto,)
    return pl.pallas_call(
        _transform_body if onto is None else _transform_more,
        grid=(tiles, halves),
        in_specs=in_specs,
        out_specs=pl.BlockSpec((count, 8, LANES), out_map),
        out_shape=jax.ShapeDtypeStruct((count, 2 * planes, halves * LANES), jnp.float32),
        input_output_aliases={} if onto is None else {3: 0},
        compiler_params=pltpu.CompilerParams(
            dimension_semantics=("arbitrary", "arbitrary"), vmem_limit_bytes=VMEM_BYTES
        ),
        cost_estimate=pl.CostEstimate(flops=450_000_000, bytes_accessed=4_300_000, transcendentals=0),
        name="transform",
    )(*operands)


def per_device(initial_heat_matrix, conductivity, laser_x, laser_y, pixel_cell, observed, obs_var):
    members, planes, columns = initial_heat_matrix.shape
    blocks = 1
    for axis in MA:
        blocks *= lax.axis_size(axis)
    slabs = lax.axis_size("sa")
    u = initial_heat_matrix
    forward = [(i, i + 1) for i in range(slabs - 1)]
    backward = [(b, a) for a, b in forward]
    lasers = (laser_x.T, laser_y.T)
    sent_in, bottom, top = forecast_inner(lasers, u, conductivity, blocks)
    low = lax.ppermute(top, "sa", forward)
    high = lax.ppermute(bottom, "sa", backward)
    held_in = lax.all_to_all(sent_in, MA, 0, 0, tiled=True)
    sent_out, surf_out = forecast_outer(lasers, u, conductivity, low, high, blocks)

    sums = cell_sums(pixel_cell, observed, obs_var)
    surf = surf_out.reshape(members, 2, planes // 4, LANES).transpose(1, 0, 2, 3)
    rows = jnp.concatenate([surf.reshape(2, members * planes // 4, LANES), sums], axis=1)
    rows = jnp.broadcast_to(rows[None], (blocks // 2,) + rows.shape).reshape((blocks,) + rows.shape[1:])
    rows, held_in = lax.optimization_barrier((rows, held_in))
    seen = lax.all_to_all(rows, MA, 0, 0, tiled=True)
    inner = held_in.reshape((blocks * members,) + held_in.shape[2:])
    part = gram_part(inner, seen, members)
    part = part + lax.ppermute(part, "ma_2", [(0, 1), (1, 0)])
    parts = [part] + [
        lax.ppermute(part, "sa", [(i, (i + s) % slabs) for i in range(slabs)]) for s in range(1, slabs)
    ]
    hi, lo = mix_matrices(parts)

    held_out = lax.all_to_all(sent_out, MA, 0, 0, tiled=True)
    done = transform(inner, planes // 2, hi, lo)
    done = transform(held_out.reshape(blocks * members, -1, LANES), planes // 2, hi, lo, done)
    back = lax.all_to_all(done.reshape((blocks, members) + done.shape[1:]), MA, 0, 0, tiled=True)
    return back.transpose(1, 2, 0, 3).reshape(members, planes, columns)


def solution(mesh):
    torus = Mesh(mesh.devices.reshape(4, 4, 2, mesh.shape["sa"]), ("ma_0", "ma_1", "ma_2", "sa"))
    in_specs = (
        P(MA, "sa", None),
        P("sa", None),
        P(MA, None),
        P(MA, None),
        P("sa", MA),
        P("sa", MA),
        P("sa", MA),
    )
    out_specs = P(MA, "sa", None)
    return jax.shard_map(
        per_device, mesh=torus, in_specs=in_specs, out_specs=out_specs, check_vma=False
    )
```
